128 devices in a mesh: aa: 8 (over y, core), ba: 16 (over x, z).
Axes of the slice: x: 4, y: 4, z: 4, core: 2. Of those that a mesh axis runs over, the one named last changes fastest.
Arguments:
- grid_nodes: bfloat16 [131072, 512], P(('aa', 'ba')), may hold values from -6 to 6
- mesh_nodes: bfloat16 [24576, 512], P(('aa', 'ba')), may hold values from -6 to 6
- owned_nodes: int32 [128], P(('aa', 'ba')), may hold values from 96 to 192, as said below
- grid_rim: int32 [128, 8, 128], P(('aa', 'ba')), may hold values from 0 to 1023
- mesh_rim: int32 [128, 8, 16], P(('aa', 'ba')), may hold values from 0 to 95
- long_send: int32 [128, 128, 8], P(('aa', 'ba')), may hold values from 0 to 15
- g2m_edges: int32 [128, 2, 3072], P(('aa', 'ba')), may hold values from 0 to 2047, as said below
- short_edges: int32 [128, 2, 1536], P(('aa', 'ba')), may hold values from 0 to 319, as said below
- long_edges: int32 [128, 2, 1536], P(('aa', 'ba')), may hold values from 0 to 1215, as said below
- m2g_edges: int32 [128, 3, 1024], P(('aa', 'ba')), may hold values from 0 to 319, as said below
- edge_first: bfloat16 [4, 2, 512, 512], replicated, may hold values from -0.1875 to 0.1875
- edge_second: bfloat16 [4, 512, 512], replicated, may hold values from -0.25 to 0.25
- edge_bias: float32 [4, 512], replicated, may hold values from -3 to 3
- edge_gain: float32 [4, 512], replicated, may hold values from 0.5 to 2
- node_first: bfloat16 [4, 2, 512, 512], replicated, may hold values from -0.1875 to 0.1875
- node_second: bfloat16 [4, 512, 512], replicated, may hold values from -0.25 to 0.25
- node_bias: float32 [4, 512], replicated, may hold values from -3 to 3
- node_gain: float32 [4, 512], replicated, may hold values from 0.5 to 2
Outputs:
- grid_out: bfloat16 [131072, 512], P(('aa', 'ba'))
- mesh_out: bfloat16 [24576, 512], P(('aa', 'ba'))
The draws below stay inside these ranges and needn't reach their ends.
Inputs may be any that keep to these rules, and one draw needn't show every extreme that they name: `owned_nodes`: some device owns 192 nodes in every draw. `g2m_edges`: row 0 holds senders, row 1 receivers. On device d the first 16 * owned_nodes[d] slots are used, with receivers below owned_nodes[d]; the others have receiver 192. Senders at or above 1024 never name a direction with a_k = -1 on band i = 0 or a_k = 1 on band i = 7. `short_edges`: row 0 holds senders, row 1 receivers. On device d the first 8 * owned_nodes[d] slots are used, with receivers below owned_nodes[d]; the others have receiver 192. Senders below 192 are below owned_nodes[d]; senders at or above 192 never name a direction with a_k = -1 on band 0 or a_k = 1 on band 8 - 1. `long_edges`: row 0 holds senders, row 1 receivers. On device d the first 8 * owned_nodes[d] slots are used, with receivers below owned_nodes[d]; the others have receiver 192. Senders below 192 are below owned_nodes[d]. `m2g_edges`: senders below 192 are below owned_nodes[d]; senders at or above 192 never name a direction with a_k = -1 on band 0 or a_k = 1 on band 8 - 1.
All inputs are finite; a program needn't handle non-finite values.
Results may differ from the reference program's by a relative error of at most 0.013.
Values may be sent and summed in bfloat16 or wider, within the bound.
A program may use at most 128 MiB of HBM per device.

```python
import math
import jax
import jax.numpy as jnp
from jax import lax

D = 512
G_DEV = 1024
M_DEV = 192
GB = 128
HB = 16
KL = 8
CS = 16
G2M_PER = 16
SHORT_PER = 8
LONG_PER = 8
GRID = 131072
MESH_SLOTS = 24576
N_AA = 8
N_BA = 16
DEVICES = 128


def owned_counts(key):
    base = jax.random.fold_in(key, 7001)
    devices = N_AA * N_BA
    counts = jax.random.randint(jax.random.fold_in(base, 1), (devices,), M_DEV // 2, M_DEV + 1)
    busiest = jax.random.randint(jax.random.fold_in(base, 2), (), 0, devices)
    counts = jnp.where(jnp.arange(devices) == busiest, M_DEV, counts)
    return counts.astype(jnp.int32)


def rim_senders(key, shape, local_high, local_count, block_depth):
    devices = N_AA * N_BA
    row_first = (jnp.arange(devices, dtype=jnp.int32) // N_BA).reshape((devices,) + (1,) * (len(shape) - 1))
    choose = jax.random.randint(jax.random.fold_in(key, 1), shape, 0, 2) == 0
    local_rows = jax.random.randint(jax.random.fold_in(key, 2), shape, 0, local_high)
    direction = jax.random.randint(jax.random.fold_in(key, 3), shape, 0, 8)
    direction = jnp.where((row_first == 0) & (direction < 3), direction + 3, direction)
    direction = jnp.where((row_first == N_AA - 1) & (direction >= 5), direction - 3, direction)
    position = jax.random.randint(jax.random.fold_in(key, 4), shape, 0, block_depth)
    return jnp.where(choose, local_rows, local_count + direction * block_depth + position).astype(jnp.int32)


def edge_targets(key, salted, per_slot):
    counts = owned_counts(key)
    devices = N_AA * N_BA
    slot_count = per_slot * M_DEV
    alive = jnp.arange(slot_count)[None, :] < counts[:, None] * per_slot
    chosen = jax.random.randint(salted, (devices, slot_count), 0, counts[:, None])
    return jnp.where(alive, chosen, M_DEV).astype(jnp.int32)


def draw_owned_nodes(key, part):
    return owned_counts(key)


def draw_g2m_edges(key, part):
    devices = N_AA * N_BA
    senders = rim_senders(jax.random.fold_in(key, 11), (devices, G2M_PER * M_DEV), G_DEV, G_DEV, GB)
    targets = edge_targets(key, jax.random.fold_in(key, 12), G2M_PER)
    return jnp.stack([senders, targets], 1)


def draw_short_edges(key, part):
    devices = N_AA * N_BA
    counts = owned_counts(key)
    senders = rim_senders(jax.random.fold_in(key, 21), (devices, SHORT_PER * M_DEV), counts[:, None], M_DEV, HB)
    targets = edge_targets(key, jax.random.fold_in(key, 22), SHORT_PER)
    return jnp.stack([senders, targets], 1)


def draw_long_edges(key, part):
    devices = N_AA * N_BA
    counts = owned_counts(key)
    shape = (devices, LONG_PER * M_DEV)
    choose = jax.random.randint(jax.random.fold_in(key, 31), shape, 0, 4) == 0
    local_rows = jax.random.randint(jax.random.fold_in(key, 32), shape, 0, counts[:, None])
    remote = M_DEV + jax.random.randint(jax.random.fold_in(key, 33), shape, 0, devices * KL)
    senders = jnp.where(choose, local_rows, remote).astype(jnp.int32)
    targets = edge_targets(key, jax.random.fold_in(key, 34), LONG_PER)
    return jnp.stack([senders, targets], 1)


def draw_m2g_edges(key, part):
    devices = N_AA * N_BA
    counts = owned_counts(key)
    return rim_senders(jax.random.fold_in(key, 41), (devices, 3, G_DEV), counts[:, None, None], M_DEV, HB)


def draw_grid_nodes(key, part):
    second_key = jax.random.fold_in(key, 52)
    values = jnp.clip(jax.random.normal(second_key, (GRID, D)), -6.0, 6.0)
    return values.astype(jnp.bfloat16)


def set_ends(values, key, low, top_value):
    longest = values.shape.index(max(values.shape))
    spots = []
    for shift in (0, 1):
        where = [jax.random.randint(jax.random.fold_in(key, axis), (), 0, length) for axis, length in enumerate(values.shape)]
        where[longest] = (where[longest] + shift) % values.shape[longest]
        spots.append(tuple(where))
    return values.at[spots[0]].set(low).at[spots[1]].set(top_value)


def block_levels(rng, extent, pieces, smallest, largest):
    factor_of = 1.0
    for dim, shards_of in pieces:
        heights = jax.random.uniform(jax.random.fold_in(jax.random.fold_in(rng, 6), dim), (shards_of,), jnp.float32, smallest / len(pieces), largest / len(pieces))
        factor_of = factor_of * jnp.repeat(jnp.exp(heights), extent[dim] // shards_of).reshape((-1,) + (1,) * (len(extent) - 1 - dim))
    return factor_of


def gaussian(stream_key, extent, scale, most, split=(), kind=jnp.bfloat16):
    values = jax.random.normal(stream_key, extent, jnp.float32) * scale
    if len(split) > 0:
        values = block_levels(stream_key, extent, split, -0.22, 0.18) * values
    return jnp.clip(values, min=-most, max=most).astype(kind)


def setup_inputs(seed: int = 0) -> dict:
    seeds = jax.random.split(jax.random.key(seed), 19)
    grid_nodes = draw_grid_nodes(jax.random.fold_in(seeds[18], 71), 0)
    mesh_nodes = gaussian(seeds[1], (MESH_SLOTS, D), 1.0, 6.0, ((0, 128),))
    owned_nodes = draw_owned_nodes(jax.random.fold_in(seeds[18], 71), 0)
    grid_rim = set_ends(jax.random.randint(seeds[3], (DEVICES, 8, GB), 0, G_DEV), jax.random.fold_in(seeds[3], 1), 0, G_DEV - 1).astype(jnp.int32)
    mesh_rim = set_ends(jax.random.randint(seeds[4], (DEVICES, 8, HB), 0, M_DEV // 2), jax.random.fold_in(seeds[4], 1), 0, (M_DEV // 2) - 1).astype(jnp.int32)
    long_send = set_ends(jax.random.randint(seeds[5], (DEVICES, DEVICES, KL), 0, CS), jax.random.fold_in(seeds[5], 1), 0, CS - 1).astype(jnp.int32)
    g2m_edges = draw_g2m_edges(jax.random.fold_in(seeds[18], 71), 0)
    short_edges = draw_short_edges(jax.random.fold_in(seeds[18], 71), 0)
    long_edges = draw_long_edges(jax.random.fold_in(seeds[18], 71), 0)
    m2g_edges = draw_m2g_edges(jax.random.fold_in(seeds[18], 71), 0)
    edge_first = gaussian(seeds[10], (4, 2, D, D), (2 * D) ** -0.5, 0.1875)
    edge_second = gaussian(seeds[11], (4, D, D), D ** -0.5, 0.25)
    edge_bias = gaussian(seeds[12], (4, D), 0.5, 3.0, (), jnp.float32)
    edge_gain = jnp.clip(jnp.exp(jax.random.uniform(seeds[13], (4, D), jnp.float32, math.log(0.5), math.log(2.0))), 0.5, 2.0)
    node_first = gaussian(seeds[14], (4, 2, D, D), (2 * D) ** -0.5, 0.1875)
    node_second = gaussian(seeds[15], (4, D, D), D ** -0.5, 0.25)
    node_bias = gaussian(seeds[16], (4, D), 0.5, 3.0, (), jnp.float32)
    node_gain = jnp.clip(jnp.exp(jax.random.uniform(seeds[17], (4, D), jnp.float32, math.log(0.5), math.log(2.0))), 0.5, 2.0)
    return {"grid_nodes": grid_nodes, "mesh_nodes": mesh_nodes, "owned_nodes": owned_nodes, "grid_rim": grid_rim, "mesh_rim": mesh_rim, "long_send": long_send, "g2m_edges": g2m_edges, "short_edges": short_edges, "long_edges": long_edges, "m2g_edges": m2g_edges, "edge_first": edge_first, "edge_second": edge_second, "edge_bias": edge_bias, "edge_gain": edge_gain, "node_first": node_first, "node_second": node_second, "node_bias": node_bias, "node_gain": node_gain}


EPSILON = 1e-05
ALONG_FIRST = (-1, -1, -1, 0, 0, 1, 1, 1)
ALONG_SECOND = (-1, 0, 1, -1, 1, -1, 0, 1)

def layer_norm(values, norm_gain):
    average = lax.optimization_barrier(jnp.mean(values, axis=-1, keepdims=True))
    centred = values - average
    spread = lax.optimization_barrier(jnp.mean(centred * centred, axis=-1, keepdims=True))
    return centred * lax.rsqrt(spread + EPSILON) * norm_gain

def messages(source_table, senders, target_proj, biases, second, norm_gain):
    gathered = source_table[senders]
    hidden = jax.nn.silu(gathered.astype(jnp.float32) + target_proj + biases).astype(jnp.bfloat16)
    flat_hidden = hidden.reshape(-1, hidden.shape[-1])
    result = jnp.dot(flat_hidden, second, preferred_element_type=jnp.float32)
    return layer_norm(result, norm_gain).astype(jnp.bfloat16).reshape(hidden.shape)

def node_update(node_rows, totals, first_layer, biases, second, norm_gain):
    summed_input = jnp.dot(node_rows, first_layer[0], preferred_element_type=jnp.float32)
    summed_input = summed_input + jnp.dot(totals.astype(jnp.bfloat16), first_layer[1], preferred_element_type=jnp.float32) + biases
    hidden = jax.nn.silu(summed_input).astype(jnp.bfloat16)
    result = jnp.dot(hidden, second, preferred_element_type=jnp.float32)
    return (node_rows.astype(jnp.float32) + layer_norm(result, norm_gain)).astype(jnp.bfloat16)

def halo_global(senders, rim_rows, local_count):
    devices = N_AA * N_BA
    block_depth = rim_rows.shape[2]
    shape_full = (devices,) + (1,) * (senders.ndim - 1)
    device_ids = jnp.arange(devices, dtype=jnp.int32).reshape(shape_full)
    row_first = device_ids // N_BA
    row_second = device_ids % N_BA
    is_local = senders < local_count
    offset = jnp.maximum(senders - local_count, 0)
    direction = offset // block_depth
    position = offset % block_depth
    step_first = jnp.array(ALONG_FIRST, dtype=jnp.int32)[direction]
    step_second = jnp.array(ALONG_SECOND, dtype=jnp.int32)[direction]
    peer_ids = (row_first + step_first) % N_AA * N_BA + (row_second + step_second) % N_BA
    remote = rim_rows[peer_ids, 7 - direction, position]
    return jnp.where(is_local, device_ids * local_count + senders, peer_ids * local_count + remote).astype(jnp.int32)

def long_global(senders, long_send):
    devices = N_AA * N_BA
    blocks = long_send.shape[2]
    device_ids = jnp.arange(devices, dtype=jnp.int32).reshape(devices, 1)
    offset = jnp.maximum(senders - M_DEV, 0)
    peer_ids = offset // blocks
    position = offset % blocks
    remote = long_send[peer_ids, device_ids, position]
    return jnp.where(senders < M_DEV, device_ids * M_DEV + senders, peer_ids * M_DEV + remote).astype(jnp.int32)

def mesh_section(source_table, node_rows, senders, targets, section_index, weights):
    edge_first, edge_second, edge_bias, edge_gain, node_first, node_second, node_bias, node_gain = weights
    devices = N_AA * N_BA
    target_proj = jnp.dot(node_rows, edge_first[section_index, 1], preferred_element_type=jnp.float32)
    target_proj = target_proj.reshape(devices, M_DEV, D)

    def one_device(inputs):
        sender_ids, target_ids, proj_rows = inputs
        picked = proj_rows[jnp.minimum(target_ids, M_DEV - 1)]
        message_rows = messages(source_table, sender_ids, picked, edge_bias[section_index], edge_second[section_index], edge_gain[section_index])
        summed = jax.ops.segment_sum(message_rows.astype(jnp.float32), target_ids, num_segments=M_DEV + 1)
        return summed[:M_DEV]
    totals = lax.map(one_device, (senders, targets, target_proj)).reshape(-1, D)
    return node_update(node_rows, totals, node_first[section_index], node_bias[section_index], node_second[section_index], node_gain[section_index])

def reference(grid_nodes, mesh_nodes, owned_nodes, grid_rim, mesh_rim, long_send, g2m_edges, short_edges, long_edges, m2g_edges, edge_first, edge_second, edge_bias, edge_gain, node_first, node_second, node_bias, node_gain):
    weights = (edge_first, edge_second, edge_bias, edge_gain, node_first, node_second, node_bias, node_gain)
    devices = N_AA * N_BA
    grid_proj = jnp.dot(grid_nodes, edge_first[0, 0], preferred_element_type=jnp.float32).astype(jnp.bfloat16)
    senders = halo_global(g2m_edges[:, 0], grid_rim, G_DEV)
    mesh_one = mesh_section(grid_proj, mesh_nodes, senders, g2m_edges[:, 1], 0, weights)
    short_proj = jnp.dot(mesh_one, edge_first[1, 0], preferred_element_type=jnp.float32).astype(jnp.bfloat16)
    senders = halo_global(short_edges[:, 0], mesh_rim, M_DEV)
    mesh_two = mesh_section(short_proj, mesh_one, senders, short_edges[:, 1], 1, weights)
    long_proj = jnp.dot(mesh_two, edge_first[2, 0], preferred_element_type=jnp.float32).astype(jnp.bfloat16)
    senders = long_global(long_edges[:, 0], long_send)
    mesh_three = mesh_section(long_proj, mesh_two, senders, long_edges[:, 1], 2, weights)
    decode_proj = jnp.dot(mesh_three, edge_first[3, 0], preferred_element_type=jnp.float32).astype(jnp.bfloat16)
    senders = halo_global(m2g_edges, mesh_rim, M_DEV)
    target_proj = jnp.dot(grid_nodes, edge_first[3, 1], preferred_element_type=jnp.float32).reshape(devices, G_DEV, D)

    def one_tile(inputs):
        sender_ids, proj_rows = inputs
        message_rows = messages(decode_proj, sender_ids, proj_rows[None], edge_bias[3], edge_second[3], edge_gain[3])
        return lax.optimization_barrier(jnp.sum(message_rows.astype(jnp.float32), axis=0))
    totals = lax.map(one_tile, (senders, target_proj)).reshape(-1, D)
    grid_out = node_update(grid_nodes, totals, node_first[3], node_bias[3], node_second[3], node_gain[3])
    alive_rows = (jnp.arange(M_DEV, dtype=jnp.int32)[None, :] < owned_nodes[:, None]).reshape(-1, 1)
    mesh_out = jnp.where(alive_rows, mesh_three, jnp.zeros_like(mesh_three))
    return (grid_out, mesh_out)
```

```python
import functools

import jax
import jax.numpy as jnp
from jax import lax
from jax.experimental import pallas as pl
from jax.experimental.pallas import tpu as pltpu
from jax.sharding import PartitionSpec as P

EPSILON = 1e-05
D = 512
G_DEV = 1024
M_DEV = 192
GB = 128
HB = 16
KL = 8
N_AA = 8
N_BA = 16
DEVICES = 128
E_G2M = 3072
E_MESH = 1536
TILE = 512
ALONG_FIRST = (-1, -1, -1, 0, 0, 1, 1, 1)
ALONG_SECOND = (-1, 0, 1, -1, 1, -1, 0, 1)
F32 = jnp.float32
BF16 = jnp.bfloat16
MESH = pl.DeviceIdType.MESH


def dot(a, b):
    return jnp.dot(a, b, preferred_element_type=F32)


def silu(x):
    half = 0.5 * x
    return half * jnp.tanh(half) + half


def normalised(values):
    centred = values - jnp.mean(values, axis=-1, keepdims=True)
    spread = jnp.mean(centred * centred, axis=-1, keepdims=True)
    return centred * lax.rsqrt(spread + EPSILON)


def columns(row):
    parts = []
    for start in range(0, row.shape[1], 128):
        part = row[:, start : start + 128].astype(F32)
        parts.append(jnp.broadcast_to(part, (128, 128)).T)
    return parts[0] if len(parts) == 1 else jnp.concatenate(parts, 0)


def one_hot(cols, first, width):
    rows = cols.shape[0]
    lane = lax.broadcasted_iota(jnp.int32, (rows, 128), 1).astype(F32)
    parts = []
    for start in range(first, first + width, 128):
        parts.append(jnp.where(cols == lane + float(start), 1.0, 0.0).astype(BF16))
    return parts[0] if len(parts) == 1 else jnp.concatenate(parts, 1)


def scatter_matrix(row):
    slots = lax.broadcasted_iota(jnp.int32, (M_DEV, row.shape[1]), 0)
    return jnp.where(slots == row, 1.0, 0.0).astype(BF16)


def node_update(rows, totals, first_own, first_sum, bias, second, gain):
    pre = dot(rows, first_own) + dot(totals.astype(BF16), first_sum) + bias
    hidden = silu(pre).astype(BF16)
    result = normalised(dot(hidden, second)) * gain
    return (rows.astype(F32) + result).astype(BF16)


def mesh_kernel(
    grid_nodes,
    mesh_nodes,
    grid_rim,
    mesh_rim,
    long_send,
    g2m_edges,
    short_edges,
    long_edges,
    edge_first,
    edge_second,
    edge_bias,
    edge_gain,
    node_first,
    node_second,
    node_bias,
    node_gain,
    dec_out,
    mesh_out,
    gq_out,
    gp_out,
    grid_v,
    mesh_v,
    grim_v,
    mrim_v,
    send_v,
    g2m_v,
    short_v,
    long_v,
    ef_v,
    es_v,
    eb_v,
    eg_v,
    nf_v,
    ns_v,
    nb_v,
    ng_v,
    enc_table,
    enc_halo,
    enc_rim,
    partial,
    cols_v,
    proj_v,
    short_table,
    short_rim,
    long_table,
    long_out,
    long_in,
    long_rows,
    dec_table,
    dec_rim,
    totals,
    gq_v,
    gp_v,
    in_sem,
    out_sem,
    halo_send,
    halo_recv,
    long_ssem,
    long_rsem,
):
    band = lax.axis_index("aa")
    sector = lax.axis_index("ba")
    me = band * N_BA + sector

    loads = {}

    def load(name, src, dst):
        copy = pltpu.make_async_copy(src, dst, in_sem.at[len(loads)])
        copy.start()
        loads[name] = copy

    load("grid", grid_nodes, grid_v)
    load("ef00", edge_first.at[0, 0], ef_v.at[0, 0])
    load("grim", grid_rim, grim_v)
    load("mesh", mesh_nodes, mesh_v)
    load("ef01", edge_first.at[0, 1], ef_v.at[0, 1])
    load("eb", edge_bias, eb_v)
    load("g2m", g2m_edges, g2m_v)
    load("mrim", mesh_rim, mrim_v)
    load("send", long_send, send_v)
    load("short", short_edges, short_v)
    load("long", long_edges, long_v)
    load("ef31", edge_first.at[3, 1], ef_v.at[3, 1])
    load("nf30", node_first.at[3, 0], nf_v.at[3, 0])
    load("nb", node_bias, nb_v)
    load("eg", edge_gain, eg_v)
    load("ng", node_gain, ng_v)
    load("es0", edge_second.at[0], es_v.at[0])
    load("nf0", node_first.at[0], nf_v.at[0])
    load("ns0", node_second.at[0], ns_v.at[0])
    load("ef1", edge_first.at[1], ef_v.at[1])
    load("es1", edge_second.at[1], es_v.at[1])
    load("nf1", node_first.at[1], nf_v.at[1])
    load("ns1", node_second.at[1], ns_v.at[1])
    load("ef2", edge_first.at[2], ef_v.at[2])
    load("es2", edge_second.at[2], es_v.at[2])
    load("nf2", node_first.at[2], nf_v.at[2])
    load("ns2", node_second.at[2], ns_v.at[2])
    load("ef30", edge_first.at[3, 0], ef_v.at[3, 0])

    barrier = pltpu.get_barrier_semaphore()

    def greet(step, carry):
        peer = lax.rem(me + step, DEVICES)
        pl.semaphore_signal(
            barrier, inc=1, device_id=(peer // N_BA, lax.rem(peer, N_BA)), device_id_type=MESH
        )
        return carry

    lax.fori_loop(1, DEVICES, greet, 0)

    def neighbour(k):
        return (
            lax.rem(band + (ALONG_FIRST[k] + N_AA), N_AA),
            lax.rem(sector + (ALONG_SECOND[k] + N_BA), N_BA),
        )

    def halo_copy(k, sem_base, rim, table, first, depth):
        return pltpu.make_async_remote_copy(
            src_ref=rim.at[pl.ds(k * depth, depth)],
            dst_ref=table.at[pl.ds(first + (7 - k) * depth, depth)],
            send_sem=halo_send.at[sem_base + k],
            recv_sem=halo_recv.at[sem_base + 7 - k],
            device_id=neighbour(k),
            device_id_type=MESH,
        )

    loads["grid"].wait()
    loads["ef00"].wait()
    for start in range(0, G_DEV, 512):
        enc_table[start : start + 512, :] = dot(grid_v[start : start + 512, :], ef_v[0, 0]).astype(BF16)
    loads["grim"].wait()
    copies = []
    for half in range(2):
        cols = jnp.concatenate([columns(grim_v[0, k : k + 1, :]) for k in range(4 * half, 4 * half + 4)], 0)
        enc_rim[half * 512 : half * 512 + 512, :] = dot(
            one_hot(cols, 0, G_DEV), enc_table[0:G_DEV, :]
        ).astype(BF16)
        if half == 0:
            pl.semaphore_wait(barrier, DEVICES - 1)
        for k in range(4 * half, 4 * half + 4):
            copy = halo_copy(k, 0, enc_rim, enc_halo, 0, GB)
            copy.start()
            copies.append(copy)

    loads["mesh"].wait()
    loads["ef01"].wait()
    loads["eb"].wait()
    enc_table[G_DEV : G_DEV + M_DEV, :] = (dot(mesh_v[...], ef_v[0, 1]) + eb_v[0:1, :]).astype(BF16)
    enc_table[G_DEV + M_DEV : G_DEV + 256, :] = jnp.zeros((64, D), BF16)
    proj_v[M_DEV:256, :] = jnp.zeros((64, D), BF16)
    loads["g2m"].wait()

    def enc_local(step, carry):
        start = pl.multiple_of(step * TILE, TILE)
        here = pl.ds(start, TILE)
        senders = columns(g2m_v[0, 0:1, here])
        cols_v[here, :] = senders
        targets = columns(g2m_v[0, 1:2, here])
        picks = jnp.concatenate([one_hot(senders, 0, G_DEV), one_hot(targets, 0, 256)], 1)
        partial[here, :] = dot(picks, enc_table[...])
        return carry

    lax.fori_loop(0, E_G2M // TILE, enc_local, 0)

    for name in ("ef31", "nf30", "nb"):
        loads[name].wait()
    for start in range(0, G_DEV, 512):
        rows = grid_v[start : start + 512, :]
        gq_v[start : start + 512, :] = (dot(rows, ef_v[3, 1]) + eb_v[3:4, :]).astype(BF16)
        gp_v[start : start + 512, :] = (dot(rows, nf_v[3, 0]) + nb_v[3:4, :]).astype(BF16)
    gq_copy = pltpu.make_async_copy(gq_v, gq_out, out_sem.at[0])
    gp_copy = pltpu.make_async_copy(gp_v, gp_out, out_sem.at[1])
    gq_copy.start()
    gp_copy.start()

    def add_messages(x, second, target_row):
        hidden = silu(x).astype(BF16)
        message = normalised(dot(hidden, second)).astype(BF16)
        totals[...] += dot(scatter_matrix(target_row), message)

    for name in ("eg", "ng", "es0", "nf0", "ns0"):
        loads[name].wait()
    totals[...] = jnp.zeros((M_DEV, D), F32)
    for copy in copies:
        copy.wait()

    def enc_remote(step, carry):
        start = pl.multiple_of(step * TILE, TILE)
        here = pl.ds(start, TILE)
        x = partial[here, :] + dot(one_hot(cols_v[here, :], G_DEV, 8 * GB), enc_halo[...])
        add_messages(x, es_v[0], g2m_v[0, 1:2, here])
        return carry

    lax.fori_loop(0, E_G2M // TILE, enc_remote, 0)

    def update(section):
        mesh_v[...] = node_update(
            mesh_v[...],
            totals[...] * eg_v[section : section + 1, :],
            nf_v[section, 0],
            nf_v[section, 1],
            nb_v[section : section + 1, :],
            ns_v[section],
            ng_v[section : section + 1, :],
        )

    update(0)

    loads["mrim"].wait()

    def rim_columns():
        parts = []
        sub = lax.broadcasted_iota(jnp.int32, (HB, HB), 0)
        lane = lax.broadcasted_iota(jnp.int32, (HB, HB), 1)
        for k in range(8):
            row = jnp.broadcast_to(mrim_v[0, k : k + 1, :].astype(F32), (HB, HB))
            col = jnp.sum(jnp.where(sub == lane, row, 0.0), axis=1, keepdims=True)
            parts.append(jnp.broadcast_to(col, (HB, 128)))
        return jnp.concatenate(parts, 0)

    def mesh_halo(section, sem_base, rim, table):
        proj = dot(mesh_v[...], ef_v[section, 0]).astype(BF16)
        proj_v[0:M_DEV, :] = proj
        table[0:M_DEV, :] = proj
        rim[...] = dot(one_hot(rim_columns(), 0, 128), proj_v[0:128, :]).astype(BF16)
        started = []
        for k in range(8):
            copy = halo_copy(k, sem_base, rim, table, M_DEV, HB)
            copy.start()
            started.append(copy)
        return started

    loads["ef1"].wait()
    copies = mesh_halo(1, 8, short_rim, short_table)
    short_table[M_DEV + 8 * HB : 512, :] = (dot(mesh_v[...], ef_v[1, 1]) + eb_v[1:2, :]).astype(BF16)
    for name in ("short", "es1", "nf1", "ns1"):
        loads[name].wait()
    totals[...] = jnp.zeros((M_DEV, D), F32)
    for copy in copies:
        copy.wait()

    def short_step(step, carry):
        start = pl.multiple_of(step * TILE, TILE)
        here = pl.ds(start, TILE)
        senders = columns(short_v[0, 0:1, here])
        targets = columns(short_v[0, 1:2, here]) + float(M_DEV + 8 * HB)
        lane = lax.broadcasted_iota(jnp.int32, (TILE, 128), 1).astype(F32)
        parts = []
        for first in range(0, 512, 128):
            place = lane + float(first)
            parts.append(
                jnp.where((senders == place) | (targets == place), 1.0, 0.0).astype(BF16)
            )
        x = dot(jnp.concatenate(parts, 1), short_table[...])
        add_messages(x, es_v[1], short_v[0, 1:2, here])
        return carry

    lax.fori_loop(0, E_MESH // TILE, short_step, 0)
    update(1)

    loads["ef2"].wait()
    loads["send"].wait()
    proj = dot(mesh_v[...], ef_v[2, 0]).astype(BF16)
    proj_v[0:M_DEV, :] = proj
    long_table[0:M_DEV, :] = proj
    lists = send_v[0].astype(F32).astype(BF16)
    for start in range(0, DEVICES * KL, 512):
        sub = lax.broadcasted_iota(jnp.int32, (512, DEVICES), 0) + start
        lane = lax.broadcasted_iota(jnp.int32, (512, DEVICES), 1)
        spread = dot(jnp.where(sub // KL == lane, 1.0, 0.0).astype(BF16), lists)
        sub = lax.broadcasted_iota(jnp.int32, (512, KL), 0)
        lane = lax.broadcasted_iota(jnp.int32, (512, KL), 1)
        col = jnp.sum(jnp.where(lax.rem(sub, KL) == lane, spread, 0.0), axis=1, keepdims=True)
        rows = dot(one_hot(jnp.broadcast_to(col, (512, 128)), 0, 128), proj_v[0:128, :])
        long_out[start // KL : (start + 512) // KL] = rows.reshape(512 // KL, KL, D).astype(BF16)

    def send_long(step, carry):
        peer = lax.rem(me + step, DEVICES)
        pltpu.make_async_remote_copy(
            src_ref=long_out.at[peer],
            dst_ref=long_in.at[me],
            send_sem=long_ssem,
            recv_sem=long_rsem,
            device_id=(peer // N_BA, lax.rem(peer, N_BA)),
            device_id_type=MESH,
        ).start()
        return carry

    lax.fori_loop(1, DEVICES, send_long, 0)
    long_in[me] = long_out[me]
    long_table[M_DEV : 2 * M_DEV, :] = (dot(mesh_v[...], ef_v[2, 1]) + eb_v[2:3, :]).astype(BF16)
    loads["long"].wait()

    def long_local(step, carry):
        start = pl.multiple_of(step * TILE, TILE)
        here = pl.ds(start, TILE)
        senders = columns(long_v[0, 0:1, here])
        cols_v[here, :] = senders
        own = jnp.where(senders < float(M_DEV), senders, -1.0)
        targets = columns(long_v[0, 1:2, here]) + float(M_DEV)
        lane = lax.broadcasted_iota(jnp.int32, (TILE, 128), 1).astype(F32)
        parts = []
        for first in range(0, 2 * M_DEV, 128):
            place = lane + float(first)
            parts.append(jnp.where((own == place) | (targets == place), 1.0, 0.0).astype(BF16))
        partial[here, :] = dot(jnp.concatenate(parts, 1), long_table[...])
        return carry

    lax.fori_loop(0, E_MESH // TILE, long_local, 0)
    for name in ("es2", "nf2", "ns2", "ef30"):
        loads[name].wait()
    totals[...] = jnp.zeros((M_DEV, D), F32)
    others = pl.ds(0, DEVICES - 1)
    pltpu.make_async_copy(long_out.at[others], long_out.at[others], long_ssem).wait()
    pltpu.make_async_copy(long_in.at[others], long_in.at[others], long_rsem).wait()
    for start in range(0, DEVICES, 32):
        block = long_in[start : start + 32].astype(F32).reshape(32 * KL, D)
        long_rows[start * KL : (start + 32) * KL, :] = block.astype(BF16)

    def long_remote(step, carry):
        start = pl.multiple_of(step * TILE, TILE)
        here = pl.ds(start, TILE)
        x = partial[here, :] + dot(one_hot(cols_v[here, :], M_DEV, DEVICES * KL), long_rows[...])
        add_messages(x, es_v[2], long_v[0, 1:2, here])
        return carry

    lax.fori_loop(0, E_MESH // TILE, long_remote, 0)
    update(2)

    copies = mesh_halo(3, 16, dec_rim, dec_table)
    dec_table[M_DEV + 8 * HB : 384, :] = jnp.zeros((64, D), BF16)
    mesh_copy = pltpu.make_async_copy(mesh_v, mesh_out, out_sem.at[2])
    mesh_copy.start()
    gq_copy.wait()
    gp_copy.wait()
    for copy in copies:
        copy.wait()
    dec_copy = pltpu.make_async_copy(dec_table, dec_out, out_sem.at[3])
    dec_copy.start()
    mesh_copy.wait()
    dec_copy.wait()


def mesh_part(
    grid_nodes,
    mesh_nodes,
    grid_rim,
    mesh_rim,
    long_send,
    g2m_edges,
    short_edges,
    long_edges,
    edge_first,
    edge_second,
    edge_bias,
    edge_gain,
    node_first,
    node_second,
    node_bias,
    node_gain,
):
    vmem = pltpu.VMEM
    anywhere = pl.BlockSpec(memory_space=pl.ANY)
    return pl.pallas_call(
        mesh_kernel,
        name="mesh_part",
        in_specs=[anywhere] * 16,
        out_specs=[anywhere] * 4,
        out_shape=[
            jax.ShapeDtypeStruct((384, D), BF16),
            jax.ShapeDtypeStruct((M_DEV, D), BF16),
            jax.ShapeDtypeStruct((G_DEV, D), BF16),
            jax.ShapeDtypeStruct((G_DEV, D), BF16),
        ],
        scratch_shapes=[
            vmem((G_DEV, D), BF16),
            vmem((M_DEV, D), BF16),
            vmem((1, 8, GB), jnp.int32),
            vmem((1, 8, HB), jnp.int32),
            vmem((1, DEVICES, KL), jnp.int32),
            vmem((1, 2, E_G2M), jnp.int32),
            vmem((1, 2, E_MESH), jnp.int32),
            vmem((1, 2, E_MESH), jnp.int32),
            vmem((4, 2, D, D), BF16),
            vmem((3, D, D), BF16),
            vmem((4, D), F32),
            vmem((4, D), F32),
            vmem((4, 2, D, D), BF16),
            vmem((3, D, D), BF16),
            vmem((4, D), F32),
            vmem((4, D), F32),
            vmem((G_DEV + 256, D), BF16),
            vmem((8 * GB, D), BF16),
            vmem((8 * GB, D), BF16),
            vmem((E_G2M, D), F32),
            vmem((E_G2M, 128), F32),
            vmem((256, D), BF16),
            vmem((512, D), BF16),
            vmem((8 * HB, D), BF16),
            vmem((2 * M_DEV, D), BF16),
            vmem((DEVICES, KL, D), BF16),
            vmem((DEVICES, KL, D), BF16),
            vmem((DEVICES * KL, D), BF16),
            vmem((384, D), BF16),
            vmem((8 * HB, D), BF16),
            vmem((M_DEV, D), F32),
            vmem((G_DEV, D), BF16),
            vmem((G_DEV, D), BF16),
            pltpu.SemaphoreType.DMA((28,)),
            pltpu.SemaphoreType.DMA((4,)),
            pltpu.SemaphoreType.DMA((24,)),
            pltpu.SemaphoreType.DMA((24,)),
            pltpu.SemaphoreType.DMA,
            pltpu.SemaphoreType.DMA,
        ],
        compiler_params=pltpu.CompilerParams(
            collective_id=0, has_side_effects=True, vmem_limit_bytes=60 * 1024 * 1024
        ),
    )(
        grid_nodes,
        mesh_nodes,
        grid_rim,
        mesh_rim,
        long_send,
        g2m_edges,
        short_edges,
        long_edges,
        edge_first,
        edge_second,
        edge_bias,
        edge_gain,
        node_first,
        node_second,
        node_bias,
        node_gain,
    )


DEC_TILE = 256


def decode_kernel(
    owned,
    edges,
    table,
    gq,
    gp,
    grid_rows,
    mesh_rows,
    edge_second,
    node_sum,
    node_second,
    edge_gain,
    node_gain,
    grid_out,
    mesh_out,
):
    step = pl.program_id(0)

    @pl.when(step == 0)
    def _():
        slot = lax.broadcasted_iota(jnp.int32, (M_DEV, D), 0)
        mesh_out[...] = jnp.where(slot < owned[0], mesh_rows[...].astype(F32), 0.0).astype(BF16)

    start = pl.multiple_of(step * DEC_TILE, DEC_TILE)
    total = jnp.zeros((DEC_TILE, D), F32)
    target = gq[...].astype(F32)
    for k in range(3):
        cols = columns(edges[0, k : k + 1, pl.ds(start, DEC_TILE)])
        x = dot(one_hot(cols, 0, 384), table[...]) + target
        hidden = silu(x).astype(BF16)
        total = total + normalised(dot(hidden, edge_second[0]))
    total = total * edge_gain[3:4, :]
    pre = gp[...].astype(F32) + dot(total.astype(BF16), node_sum[0, 0])
    hidden = silu(pre).astype(BF16)
    result = normalised(dot(hidden, node_second[0])) * node_gain[3:4, :]
    grid_out[...] = (grid_rows[...].astype(F32) + result).astype(BF16)


def decode_part(owned, edges, table, gq, gp, grid_rows, mesh_rows, es, nf, ns, eg, ng):
    def whole(*shape):
        return pl.BlockSpec(shape, lambda i: (0,) * len(shape))

    def tiled():
        return pl.BlockSpec((DEC_TILE, D), lambda i: (i, 0))

    return pl.pallas_call(
        decode_kernel,
        name="decode_part",
        grid=(G_DEV // DEC_TILE,),
        in_specs=[
            pl.BlockSpec(memory_space=pltpu.SMEM),
            whole(1, 3, G_DEV),
            whole(384, D),
            tiled(),
            tiled(),
            tiled(),
            whole(M_DEV, D),
            pl.BlockSpec((1, D, D), lambda i: (3, 0, 0)),
            pl.BlockSpec((1, 1, D, D), lambda i: (3, 1, 0, 0)),
            pl.BlockSpec((1, D, D), lambda i: (3, 0, 0)),
            whole(4, D),
            whole(4, D),
        ],
        out_specs=[tiled(), whole(M_DEV, D)],
        out_shape=[
            jax.ShapeDtypeStruct((G_DEV, D), BF16),
            jax.ShapeDtypeStruct((M_DEV, D), BF16),
        ],
    )(owned, edges, table, gq, gp, grid_rows, mesh_rows, es, nf, ns, eg, ng)


def per_device(
    grid_nodes,
    mesh_nodes,
    owned_nodes,
    grid_rim,
    mesh_rim,
    long_send,
    g2m_edges,
    short_edges,
    long_edges,
    m2g_edges,
    edge_first,
    edge_second,
    edge_bias,
    edge_gain,
    node_first,
    node_second,
    node_bias,
    node_gain,
):
    table, mesh_three, gq, gp = mesh_part(
        grid_nodes,
        mesh_nodes,
        grid_rim,
        mesh_rim,
        long_send,
        g2m_edges,
        short_edges,
        long_edges,
        edge_first,
        edge_second,
        edge_bias,
        edge_gain,
        node_first,
        node_second,
        node_bias,
        node_gain,
    )
    grid_out, mesh_out = decode_part(
        owned_nodes,
        m2g_edges,
        table,
        gq,
        gp,
        grid_nodes,
        mesh_three,
        edge_second,
        node_first,
        node_second,
        edge_gain,
        node_gain,
    )
    return (grid_out, mesh_out)


def solution(mesh):
    rows = P(("aa", "ba"), None)
    lists = P(("aa", "ba"), None, None)
    in_specs = (rows, rows, P(("aa", "ba"))) + (lists,) * 7 + (P(),) * 8
    return jax.shard_map(
        per_device, mesh=mesh, in_specs=in_specs, out_specs=(rows, rows), check_vma=False
    )
```

```python
import jax
import jax.numpy as jnp
from jax import lax
from jax.experimental import pallas as pl
from jax.experimental.pallas import tpu as pltpu
from jax.sharding import PartitionSpec as P

EPSILON = 1e-05
D = 512
G_DEV = 1024
M_DEV = 192
GB = 128
HB = 16
KL = 8
CS = 16
N_AA = 8
N_BA = 16
DEVICES = 128
E_G2M = 3072
E_MESH = 1536
TILE = 512
ALONG_FIRST = (-1, -1, -1, 0, 0, 1, 1, 1)
ALONG_SECOND = (-1, 0, 1, -1, 1, -1, 0, 1)
F32 = jnp.float32
BF16 = jnp.bfloat16
MESH = pl.DeviceIdType.MESH


def hops(first, second):
    steps = ((first + 1) // 2, second // 4, second % 4)
    return sum(min(step, 4 - step) for step in steps)


PEERS = sorted(
    [(a, b) for a in range(N_AA) for b in range(N_BA) if (a, b) != (0, 0)],
    key=lambda peer: -hops(*peer),
)


def dot(a, b):
    return jnp.dot(a, b, preferred_element_type=F32)


def silu(x):
    half = (0.5 * x).astype(BF16)
    return half * jnp.tanh(half) + half


def centred_weights(weights):
    wide = weights.astype(F32)
    return (wide - jnp.mean(wide, axis=-1, keepdims=True)).astype(BF16)


def normalised(centred):
    spread = jnp.mean(centred * centred, axis=-1, keepdims=True)
    return centred * lax.rsqrt(spread + EPSILON)


def columns(row):
    parts = []
    for start in range(0, row.shape[1], 128):
        part = row[:, start : start + 128].astype(F32)
        parts.append(jnp.broadcast_to(part, (128, 128)).T)
    return parts[0] if len(parts) == 1 else jnp.concatenate(parts, 0)


def split_ids(cols):
    block = jnp.floor(cols * (1.0 / 256.0))
    return block.astype(BF16), (cols - 256.0 * block).astype(BF16)


def one_hot(cols, first, width):
    rows = cols.shape[0]
    block, place = split_ids(cols)
    lane = lax.broadcasted_iota(jnp.int32, (rows, 128), 1).astype(F32)
    lanes = (lane.astype(BF16), (lane + 128.0).astype(BF16))
    one, zero = jnp.ones((), BF16), jnp.zeros((), BF16)
    parts = []
    for start in range(first, first + width, 256):
        here = jnp.where(block == jnp.asarray(start // 256, BF16), place, jnp.asarray(-1, BF16))
        for half in range(2):
            if start + 128 * half < first + width:
                parts.append(jnp.where(here == lanes[half], one, zero))
    return parts[0] if len(parts) == 1 else jnp.concatenate(parts, 1)


def scatter_matrix(row):
    slots = lax.broadcasted_iota(jnp.int32, (M_DEV, row.shape[1]), 0)
    return jnp.where(slots == row, 1.0, 0.0).astype(BF16)


def node_update(rows, totals, first_own, first_sum, bias, second, gain):
    pre = dot(rows, first_own) + dot(totals.astype(BF16), first_sum) + bias
    hidden = silu(pre)
    result = normalised(dot(hidden, second)) * gain
    return (rows.astype(F32) + result).astype(BF16)


def mesh_kernel(
    grid_nodes,
    mesh_nodes,
    grid_rim,
    mesh_rim,
    long_send,
    g2m_edges,
    short_edges,
    long_edges,
    m2g_edges,
    edge_first,
    edge_second,
    edge_bias,
    edge_gain,
    node_first,
    node_second,
    node_bias,
    node_gain,
    dec_out,
    mesh_out,
    gq_out,
    gp_out,
    picks_out,
    second_out,
    grid_v,
    mesh_v,
    grim_v,
    mrim_v,
    send_v,
    g2m_v,
    short_v,
    long_v,
    m2g_v,
    ef_v,
    es_v,
    eb_v,
    eg_v,
    nf_v,
    ns_v,
    nb_v,
    ng_v,
    enc_table,
    enc_halo,
    enc_rim,
    partial,
    picks_v,
    hidden_v,
    proj_v,
    coarse_v,
    rim_picks,
    short_table,
    short_rim,
    long_table,
    long_out,
    long_in,
    long_rows,
    dec_table,
    dec_rim,
    dec_picks,
    totals,
    gq_v,
    gp_v,
    in_sem,
    out_sem,
    halo_send,
    halo_recv,
    long_ssem,
    long_rsem,
    spread_sem,
):
    band = lax.axis_index("aa")
    sector = lax.axis_index("ba")
    me = band * N_BA + sector

    loads = {}

    def load(name, src, dst):
        copy = pltpu.make_async_copy(src, dst, in_sem.at[len(loads)])
        copy.start()
        loads[name] = copy

    def arrived(*names):
        for name in names:
            loads[name].wait()

    def at(first, second):
        return (
            lax.rem(band + (first + N_AA), N_AA),
            lax.rem(sector + (second + N_BA), N_BA),
        )

    def greet(semaphore, stride_first, stride_second, around):
        for k in around:
            pl.semaphore_signal(
                semaphore,
                inc=1,
                device_id=at(stride_first * ALONG_FIRST[k], stride_second * ALONG_SECOND[k]),
                device_id_type=MESH,
            )

    barrier = pltpu.get_barrier_semaphore()
    greet(barrier, 1, 1, range(8))

    load("grim", grid_rim, grim_v)
    load("grid", grid_nodes, grid_v)
    load("ef00", edge_first.at[0, 0], ef_v.at[0, 0])
    load("mesh", mesh_nodes, mesh_v)
    load("ef01", edge_first.at[0, 1], ef_v.at[0, 1])
    load("eb", edge_bias, eb_v)
    load("g2m", g2m_edges, g2m_v)
    load("es0", edge_second.at[0], es_v.at[0])
    load("ns0", node_second.at[0], ns_v.at[0])
    load("nf0", node_first.at[0], nf_v.at[0])
    load("eg", edge_gain, eg_v)
    load("ng", node_gain, ng_v)
    load("nb", node_bias, nb_v)
    load("mrim", mesh_rim, mrim_v)
    load("ef1", edge_first.at[1], ef_v.at[1])
    load("short", short_edges, short_v)
    load("es1", edge_second.at[1], es_v.at[1])
    load("nf1", node_first.at[1], nf_v.at[1])
    load("ns1", node_second.at[1], ns_v.at[1])
    load("send", long_send, send_v)
    load("ef2", edge_first.at[2], ef_v.at[2])
    load("long", long_edges, long_v)
    load("es2", edge_second.at[2], es_v.at[2])
    load("nf2", node_first.at[2], nf_v.at[2])
    load("ns2", node_second.at[2], ns_v.at[2])
    load("ef3", edge_first.at[3], ef_v.at[3])
    load("nf30", node_first.at[3, 0], nf_v.at[3, 0])
    load("es3", edge_second.at[3], es_v.at[3])
    load("ns3", node_second.at[3], ns_v.at[3])
    load("m2g", m2g_edges, m2g_v)

    def halo_copy(k, sem_base, rim, table, first, depth):
        return pltpu.make_async_remote_copy(
            src_ref=rim.at[pl.ds(k * depth, depth)],
            dst_ref=table.at[pl.ds(first + (7 - k) * depth, depth)],
            send_sem=halo_send.at[sem_base + k],
            recv_sem=halo_recv.at[sem_base + 7 - k],
            device_id=at(ALONG_FIRST[k], ALONG_SECOND[k]),
            device_id_type=MESH,
        )

    copies = []
    arrived("grim", "grid")
    for pair in ((3, 4), (0, 7), (2, 5), (1, 6)):
        cols = jnp.concatenate([columns(grim_v[0, k : k + 1, :]) for k in pair], 0)
        rows = dot(one_hot(cols, 0, G_DEV), grid_v[...]).astype(BF16)
        if not copies:
            arrived("ef00")
        rows = dot(rows, ef_v[0, 0]).astype(BF16)
        for place, k in enumerate(pair):
            enc_rim[k * GB : (k + 1) * GB, :] = rows[place * GB : (place + 1) * GB, :]
        if not copies:
            pl.semaphore_wait(barrier, 8)
        for k in pair:
            copy = halo_copy(k, 0, enc_rim, enc_halo, 0, GB)
            copy.start()
            copies.append(copy)
    greet(spread_sem.at[0], 1, 1, range(8))

    for start in range(0, G_DEV, 512):
        enc_table[start : start + 512, :] = dot(grid_v[start : start + 512, :], ef_v[0, 0]).astype(BF16)
    arrived("mesh", "ef01", "eb")
    enc_table[G_DEV : G_DEV + M_DEV, :] = (dot(mesh_v[...], ef_v[0, 1]) + eb_v[0:1, :]).astype(BF16)
    enc_table[G_DEV + M_DEV : G_DEV + 256, :] = jnp.zeros((64, D), BF16)
    proj_v[M_DEV:256, :] = jnp.zeros((64, D), BF16)
    coarse_v[...] = jnp.zeros((128, D), BF16)
    arrived("g2m")

    def enc_local(step, carry):
        start = pl.multiple_of(step * TILE, TILE)
        here = pl.ds(start, TILE)
        senders = columns(g2m_v[0, 0:1, here])
        targets = columns(g2m_v[0, 1:2, here])
        picks = jnp.concatenate([one_hot(senders, 0, G_DEV), one_hot(targets, 0, 256)], 1)
        partial[here, :] = dot(picks, enc_table[...])
        picks_v[here, :] = one_hot(senders, G_DEV, 8 * GB)
        return carry

    lax.fori_loop(0, E_G2M // TILE, enc_local, 0)

    def centre(section):
        es_v[section] = centred_weights(es_v[section])
        ns_v[section] = centred_weights(ns_v[section])

    arrived("es0", "ns0")
    centre(0)
    arrived("mrim")
    sub = lax.broadcasted_iota(jnp.int32, (HB, HB), 0)
    lane = lax.broadcasted_iota(jnp.int32, (HB, HB), 1)
    parts = []
    for k in range(8):
        row = jnp.broadcast_to(mrim_v[0, k : k + 1, :].astype(F32), (HB, HB))
        col = jnp.sum(jnp.where(sub == lane, row, 0.0), axis=1, keepdims=True)
        parts.append(jnp.broadcast_to(col, (HB, 128)))
    rim_picks[...] = one_hot(jnp.concatenate(parts, 0), 0, 128)
    arrived("es1", "ns1")
    centre(1)

    def produce(x):
        hidden_v[...] = silu(x)

    def consume(section, edges, start):
        message = normalised(dot(hidden_v[...], es_v[section])).astype(BF16)
        totals[...] += dot(scatter_matrix(edges[0, 1:2, pl.ds(start, TILE)]), message)

    def rounds(section, edges, count, picked):
        totals[...] = jnp.zeros((M_DEV, D), F32)
        produce(picked(0))

        def step(index, carry):
            start = pl.multiple_of(index * TILE, TILE)
            consume(section, edges, pl.multiple_of(start - TILE, TILE))
            produce(picked(start))
            return carry

        lax.fori_loop(1, count, step, 0)
        consume(section, edges, (count - 1) * TILE)

    def updated(section, rows, sums):
        return node_update(
            rows,
            sums * eg_v[section : section + 1, :],
            nf_v[section, 0],
            nf_v[section, 1],
            nb_v[section : section + 1, :],
            ns_v[section],
            ng_v[section : section + 1, :],
        )

    arrived("nf0", "eg", "ng", "nb")
    pl.semaphore_wait(spread_sem.at[0], 8)
    greet(spread_sem.at[1], 2, 2, range(8))
    for copy in copies:
        copy.wait()

    def enc_picked(start):
        here = pl.ds(start, TILE)
        return partial[here, :] + dot(picks_v[here, :], enc_halo[...])

    rounds(0, g2m_v, E_G2M // TILE, enc_picked)
    mesh_v[...] = updated(0, mesh_v[...], totals[...])

    def mesh_halo(section, sem_base, rim, table):
        proj = dot(mesh_v[...], ef_v[section, 0]).astype(BF16)
        proj_v[0:M_DEV, :] = proj
        rim[...] = dot(rim_picks[...], proj_v[0:128, :]).astype(BF16)
        started = []
        for k in range(8):
            copy = halo_copy(k, sem_base, rim, table, M_DEV, HB)
            copy.start()
            started.append(copy)
        table[0:M_DEV, :] = proj
        return started

    arrived("ef1")
    copies = mesh_halo(1, 8, short_rim, short_table)
    short_table[M_DEV + 8 * HB : 512, :] = (dot(mesh_v[...], ef_v[1, 1]) + eb_v[1:2, :]).astype(BF16)
    arrived("short")

    def double_one_hot(first, second, width):
        rows = first.shape[0]
        one_block, one_place = split_ids(first)
        two_block, two_place = split_ids(second)
        lane = lax.broadcasted_iota(jnp.int32, (rows, 128), 1).astype(F32)
        lanes = (lane.astype(BF16), (lane + 128.0).astype(BF16))
        one, zero, none = jnp.ones((), BF16), jnp.zeros((), BF16), jnp.asarray(-1, BF16)
        parts = []
        for start in range(0, width, 128):
            group = jnp.asarray(start // 256, BF16)
            here = lanes[start // 128 % 2]
            one_here = jnp.where(one_block == group, one_place, none)
            two_here = jnp.where(two_block == group, two_place, none)
            parts.append(jnp.where((one_here == here) | (two_here == here), one, zero))
        return jnp.concatenate(parts, 1)

    def short_picks(step, carry):
        here = pl.ds(pl.multiple_of(step * TILE, TILE), TILE)
        senders = columns(short_v[0, 0:1, here])
        targets = columns(short_v[0, 1:2, here]) + float(M_DEV + 8 * HB)
        picks_v[here, 0:512] = double_one_hot(senders, targets, 512)
        return carry

    lax.fori_loop(0, E_MESH // TILE, short_picks, 0)
    arrived("es2", "ns2", "nf1")
    centre(2)
    pl.semaphore_wait(spread_sem.at[1], 8)
    greet(spread_sem.at[2], 0, 4, (3, 4))
    for copy in copies:
        copy.wait()

    def short_picked(start):
        return dot(picks_v[pl.ds(start, TILE), 0:512], short_table[...])

    rounds(1, short_v, E_MESH // TILE, short_picked)

    arrived("ef2", "send")
    coarse = updated(1, mesh_v[0:CS, :], totals[0:CS, :])
    coarse_v[0:CS, :] = dot(coarse, ef_v[2, 0]).astype(BF16)
    lists = send_v[0].astype(F32).astype(BF16)
    for start in range(0, DEVICES * KL, 512):
        sub = lax.broadcasted_iota(jnp.int32, (512, DEVICES), 0) + start
        lane = lax.broadcasted_iota(jnp.int32, (512, DEVICES), 1)
        owner = jnp.where(sub // KL == lane, 1.0, 0.0).astype(BF16)
        listed = lax.dot_general(owner, lists, (((1,), (1,)), ((), ())), preferred_element_type=F32)
        sub = lax.broadcasted_iota(jnp.int32, (512, KL), 0)
        lane = lax.broadcasted_iota(jnp.int32, (512, KL), 1)
        col = jnp.sum(jnp.where(lax.rem(sub, KL) == lane, listed, 0.0), axis=1, keepdims=True)
        rows = dot(one_hot(jnp.broadcast_to(col, (512, 128)), 0, 128), coarse_v[...])
        long_out[start // KL : (start + 512) // KL] = rows.reshape(512 // KL, KL, D).astype(BF16)
    pl.semaphore_wait(spread_sem.at[2], 2)
    for first, second in PEERS:
        peer_first = lax.rem(band + first, N_AA)
        peer_second = (sector // 4 + second // 4) % 4 * 4 + (sector + second) % 4
        pltpu.make_async_remote_copy(
            src_ref=long_out.at[peer_first * N_BA + peer_second],
            dst_ref=long_in.at[me],
            send_sem=long_ssem,
            recv_sem=long_rsem,
            device_id=(peer_first, peer_second),
            device_id_type=MESH,
        ).start()
    long_in[me] = long_out[me]

    mesh_v[...] = updated(1, mesh_v[...], totals[...])
    long_table[0:M_DEV, :] = dot(mesh_v[...], ef_v[2, 0]).astype(BF16)
    long_table[M_DEV : 2 * M_DEV, :] = (dot(mesh_v[...], ef_v[2, 1]) + eb_v[2:3, :]).astype(BF16)
    arrived("long")

    def long_local(step, carry):
        here = pl.ds(pl.multiple_of(step * TILE, TILE), TILE)
        senders = columns(long_v[0, 0:1, here])
        own = jnp.where(senders < float(M_DEV), senders, -1.0)
        targets = columns(long_v[0, 1:2, here]) + float(M_DEV)
        partial[here, :] = dot(double_one_hot(own, targets, 2 * M_DEV), long_table[...])
        away = jnp.where(senders < float(M_DEV), -1.0, senders - float(M_DEV))
        picks_v[here, :] = one_hot(away, 0, DEVICES * KL)
        return carry

    lax.fori_loop(0, E_MESH // TILE, long_local, 0)
    arrived("ef3", "nf30", "es3", "ns3", "m2g")
    for start in range(0, G_DEV, 512):
        rows = grid_v[start : start + 512, :]
        gq_v[start : start + 512, :] = (dot(rows, ef_v[3, 1]) + eb_v[3:4, :]).astype(BF16)
        gp_v[start : start + 512, :] = (dot(rows, nf_v[3, 0]) + nb_v[3:4, :]).astype(BF16)
    centre(3)
    gq_copy = pltpu.make_async_copy(gq_v, gq_out, out_sem.at[0])
    gp_copy = pltpu.make_async_copy(gp_v, gp_out, out_sem.at[1])
    es_copy = pltpu.make_async_copy(es_v.at[3], second_out.at[0], out_sem.at[2])
    ns_copy = pltpu.make_async_copy(ns_v.at[3], second_out.at[1], out_sem.at[3])
    outs = [gq_copy, gp_copy, es_copy, ns_copy]

    def dec_ids(step, carry):
        here = pl.ds(pl.multiple_of(step * 512, 512), 512)
        for k in range(3):
            dec_picks[k, here, :] = one_hot(columns(m2g_v[k, :, here]), 0, 384)
        return carry

    lax.fori_loop(0, G_DEV // 512, dec_ids, 0)
    outs.append(pltpu.make_async_copy(dec_picks, picks_out, out_sem.at[4]))
    for copy in outs:
        copy.start()
    arrived("nf2")
    others = pl.ds(0, DEVICES - 1)
    pltpu.make_async_copy(long_out.at[others], long_out.at[others], long_ssem).wait()
    pltpu.make_async_copy(long_in.at[others], long_in.at[others], long_rsem).wait()
    for start in range(0, DEVICES, 32):
        block = long_in[start : start + 32].astype(F32).reshape(32 * KL, D)
        long_rows[start * KL : (start + 32) * KL, :] = block.astype(BF16)

    def long_picked(start):
        here = pl.ds(start, TILE)
        return partial[here, :] + dot(picks_v[here, :], long_rows[...])

    rounds(2, long_v, E_MESH // TILE, long_picked)
    mesh_v[...] = updated(2, mesh_v[...], totals[...])

    copies = mesh_halo(3, 16, dec_rim, dec_table)
    dec_table[M_DEV + 8 * HB : 384, :] = jnp.zeros((64, D), BF16)
    outs.append(pltpu.make_async_copy(mesh_v, mesh_out, out_sem.at[5]))
    outs[-1].start()
    for copy in outs:
        copy.wait()
    for copy in copies:
        copy.wait()
    dec_copy = pltpu.make_async_copy(dec_table, dec_out, out_sem.at[6])
    dec_copy.start()
    dec_copy.wait()


def mesh_part(*operands):
    vmem = pltpu.VMEM
    anywhere = pl.BlockSpec(memory_space=pl.ANY)
    return pl.pallas_call(
        mesh_kernel,
        name="mesh_part",
        in_specs=[anywhere] * 17,
        out_specs=[anywhere] * 6,
        out_shape=[
            jax.ShapeDtypeStruct((384, D), BF16),
            jax.ShapeDtypeStruct((M_DEV, D), BF16),
            jax.ShapeDtypeStruct((G_DEV, D), BF16),
            jax.ShapeDtypeStruct((G_DEV, D), BF16),
            jax.ShapeDtypeStruct((3, G_DEV, 384), BF16),
            jax.ShapeDtypeStruct((2, D, D), BF16),
        ],
        scratch_shapes=[
            vmem((G_DEV, D), BF16),
            vmem((M_DEV, D), BF16),
            vmem((1, 8, GB), jnp.int32),
            vmem((1, 8, HB), jnp.int32),
            vmem((1, KL, DEVICES), jnp.int32),
            vmem((1, 2, E_G2M), jnp.int32),
            vmem((1, 2, E_MESH), jnp.int32),
            vmem((1, 2, E_MESH), jnp.int32),
            vmem((3, 1, G_DEV), jnp.int32),
            vmem((4, 2, D, D), BF16),
            vmem((4, D, D), BF16),
            vmem((4, D), F32),
            vmem((4, D), F32),
            vmem((4, 2, D, D), BF16),
            vmem((4, D, D), BF16),
            vmem((4, D), F32),
            vmem((4, D), F32),
            vmem((G_DEV + 256, D), BF16),
            vmem((8 * GB, D), BF16),
            vmem((8 * GB, D), BF16),
            vmem((E_G2M, D), F32),
            vmem((E_G2M, 8 * GB), BF16),
            vmem((TILE, D), BF16),
            vmem((256, D), BF16),
            vmem((128, D), BF16),
            vmem((128, 128), BF16),
            vmem((512, D), BF16),
            vmem((8 * HB, D), BF16),
            vmem((2 * M_DEV, D), BF16),
            vmem((DEVICES, KL, D), BF16),
            vmem((DEVICES, KL, D), BF16),
            vmem((DEVICES * KL, D), BF16),
            vmem((384, D), BF16),
            vmem((8 * HB, D), BF16),
            vmem((3, G_DEV, 384), BF16),
            vmem((M_DEV, D), F32),
            vmem((G_DEV, D), BF16),
            vmem((G_DEV, D), BF16),
            pltpu.SemaphoreType.DMA((30,)),
            pltpu.SemaphoreType.DMA((7,)),
            pltpu.SemaphoreType.DMA((24,)),
            pltpu.SemaphoreType.DMA((24,)),
            pltpu.SemaphoreType.DMA,
            pltpu.SemaphoreType.DMA,
            pltpu.SemaphoreType.REGULAR((3,)),
        ],
        compiler_params=pltpu.CompilerParams(
            collective_id=0, has_side_effects=True, vmem_limit_bytes=60 * 1024 * 1024
        ),
    )(*operands)


DEC_TILE = 256


def decode_kernel(
    owned,
    picks,
    table,
    gq,
    gp,
    grid_rows,
    mesh_rows,
    seconds,
    node_sum,
    edge_gain,
    node_gain,
    grid_out,
    mesh_out,
):
    @pl.when(pl.program_id(0) == 0)
    def _():
        slot = lax.broadcasted_iota(jnp.int32, (M_DEV, D), 0)
        mesh_out[...] = jnp.where(slot < owned[0], mesh_rows[...].astype(F32), 0.0).astype(BF16)

    target = gq[...].astype(F32)
    x = dot(picks[...].reshape(3 * DEC_TILE, 384), table[...])
    hidden = silu(x + jnp.concatenate([target] * 3, 0))
    message = normalised(dot(hidden, seconds[0]))
    total = message[0:DEC_TILE] + message[DEC_TILE : 2 * DEC_TILE] + message[2 * DEC_TILE :]
    total = total * edge_gain[3:4, :]
    pre = gp[...].astype(F32) + dot(total.astype(BF16), node_sum[0, 0])
    result = normalised(dot(silu(pre), seconds[1])) * node_gain[3:4, :]
    grid_out[...] = (grid_rows[...].astype(F32) + result).astype(BF16)


def decode_part(owned, picks, table, gq, gp, grid_rows, mesh_rows, seconds, nf, eg, ng):
    def whole(*shape):
        return pl.BlockSpec(shape, lambda i: (0,) * len(shape))

    def tiled():
        return pl.BlockSpec((DEC_TILE, D), lambda i: (i, 0))

    return pl.pallas_call(
        decode_kernel,
        name="decode_part",
        grid=(G_DEV // DEC_TILE,),
        in_specs=[
            pl.BlockSpec(memory_space=pltpu.SMEM),
            pl.BlockSpec((3, DEC_TILE, 384), lambda i: (0, i, 0)),
            whole(384, D),
            tiled(),
            tiled(),
            tiled(),
            whole(M_DEV, D),
            whole(2, D, D),
            pl.BlockSpec((1, 1, D, D), lambda i: (3, 1, 0, 0)),
            whole(4, D),
            whole(4, D),
        ],
        out_specs=[tiled(), whole(M_DEV, D)],
        out_shape=[
            jax.ShapeDtypeStruct((G_DEV, D), BF16),
            jax.ShapeDtypeStruct((M_DEV, D), BF16),
        ],
    )(owned, picks, table, gq, gp, grid_rows, mesh_rows, seconds, nf, eg, ng)


def per_device(
    grid_nodes,
    mesh_nodes,
    owned_nodes,
    grid_rim,
    mesh_rim,
    long_send,
    g2m_edges,
    short_edges,
    long_edges,
    m2g_edges,
    edge_first,
    edge_second,
    edge_bias,
    edge_gain,
    node_first,
    node_second,
    node_bias,
    node_gain,
):
    table, mesh_three, gq, gp, picks, seconds = mesh_part(
        grid_nodes,
        mesh_nodes,
        grid_rim,
        mesh_rim,
        jnp.transpose(long_send, (0, 2, 1)),
        g2m_edges,
        short_edges,
        long_edges,
        jnp.transpose(m2g_edges, (1, 0, 2)),
        edge_first,
        edge_second,
        edge_bias,
        edge_gain,
        node_first,
        node_second,
        node_bias,
        node_gain,
    )
    grid_out, mesh_out = decode_part(
        owned_nodes,
        picks,
        table,
        gq,
        gp,
        grid_nodes,
        mesh_three,
        seconds,
        node_first,
        edge_gain,
        node_gain,
    )
    return (grid_out, mesh_out)


def solution(mesh):
    rows = P(("aa", "ba"), None)
    lists = P(("aa", "ba"), None, None)
    in_specs = (rows, rows, P(("aa", "ba"))) + (lists,) * 7 + (P(),) * 8
    return jax.shard_map(
        per_device, mesh=mesh, in_specs=in_specs, out_specs=(rows, rows), check_vma=False
    )
```

```python
import jax
import jax.numpy as jnp
from jax import lax
from jax.experimental import pallas as pl
from jax.experimental.pallas import tpu as pltpu
from jax.sharding import PartitionSpec as P

EPSILON = 1e-05
D = 512
G_DEV = 1024
M_DEV = 192
GB = 128
HB = 16
KL = 8
CS = 16
NOWHERE = 4095
EARLY = 4
N_AA = 8
N_BA = 16
DEVICES = 128
E_G2M = 3072
E_MESH = 1536
TILE_LOCAL = 512
TILE_ENC = 768
TILE_MESH = 768
ALONG_FIRST = (-1, -1, -1, 0, 0, 1, 1, 1)
ALONG_SECOND = (-1, 0, 1, -1, 1, -1, 0, 1)
F32 = jnp.float32
BF16 = jnp.bfloat16
MESH = pl.DeviceIdType.MESH


def hops(first, second):
    steps = ((first + 1) // 2, second // 4, second % 4)
    return sum(min(step, 4 - step) for step in steps)


PEERS = sorted(
    [(a, b) for a in range(N_AA) for b in range(N_BA) if (a, b) != (0, 0)],
    key=lambda peer: -hops(*peer),
)


def dot(a, b):
    return jnp.dot(a, b, preferred_element_type=F32)


def silu_of_half(half):
    return half * jnp.tanh(half) + half


def centred_weights(weights):
    wide = weights.astype(F32)
    return (wide - jnp.mean(wide, axis=-1, keepdims=True)).astype(BF16)


def normalised(centred):
    spread = jnp.mean(centred * centred, axis=-1, keepdims=True)
    return centred * lax.rsqrt(spread + EPSILON)


def spread_out(row):
    parts = []
    for start in range(0, row.shape[1], 128):
        parts.append(jnp.broadcast_to(row[:, start : start + 128], (128, 128)).T.astype(BF16))
    return parts[0] if len(parts) == 1 else jnp.concatenate(parts, 0)


def columns(row):
    return spread_out((row >> 8).astype(F32)), spread_out((row & 255).astype(F32))


def lane_ids(rows):
    lane = lax.broadcasted_iota(jnp.int32, (rows, 128), 1).astype(F32)
    return lane.astype(BF16), (lane + 128.0).astype(BF16)


def one_hot(cols, first, width):
    block, place = cols
    lanes = lane_ids(place.shape[0])
    one, zero = jnp.ones((), BF16), jnp.zeros((), BF16)
    parts = []
    for start in range(first, first + width, 256):
        here = place
        if block is not None:
            here = jnp.where(block == jnp.asarray(start // 256, BF16), place, jnp.asarray(-1, BF16))
        for half in range(2):
            if start + 128 * half < first + width:
                parts.append(jnp.where(here == lanes[half], one, zero))
    return parts[0] if len(parts) == 1 else jnp.concatenate(parts, 1)


def double_one_hot(first, second, width):
    lanes = lane_ids(first[1].shape[0])
    one, zero, none = jnp.ones((), BF16), jnp.zeros((), BF16), jnp.asarray(-1, BF16)
    parts = []
    for start in range(0, width, 256):
        group = jnp.asarray(start // 256, BF16)
        one_here = jnp.where(first[0] == group, first[1], none)
        two_here = jnp.where(second[0] == group, second[1], none)
        for half in range(2):
            if start + 128 * half < width:
                found = (one_here == lanes[half]) | (two_here == lanes[half])
                parts.append(jnp.where(found, one, zero))
    return jnp.concatenate(parts, 1)


def scatter_matrix(row):
    slots = lax.broadcasted_iota(jnp.int32, (M_DEV, row.shape[1]), 0).astype(F32).astype(BF16)
    ids = row.astype(F32).astype(BF16)
    return jnp.where(slots == ids, jnp.ones((), BF16), jnp.zeros((), BF16))


def node_update(rows, totals, first_own, first_sum, bias, second, gain):
    pre = dot(rows, first_own) + dot(totals.astype(BF16), first_sum) + bias
    result = dot(silu_of_half((0.5 * pre).astype(BF16)), second)
    result = normalised(result) * gain
    return (rows.astype(F32) + result).astype(BF16)


def mesh_kernel(
    grid_nodes,
    mesh_nodes,
    grid_rim,
    mesh_rim,
    long_send,
    g2m_edges,
    short_edges,
    long_edges,
    m2g_edges,
    edge_first,
    edge_second,
    edge_bias,
    edge_gain,
    node_first,
    node_second,
    node_bias,
    node_gain,
    dec_out,
    mesh_out,
    gq_out,
    gp_out,
    picks_out,
    second_out,
    grid_v,
    mesh_v,
    grim_v,
    mrim_v,
    send_v,
    g2m_v,
    short_v,
    long_v,
    m2g_v,
    ef_v,
    es_v,
    eb_v,
    eg_v,
    nf_v,
    ns_v,
    nb_v,
    ng_v,
    enc_table,
    enc_halo,
    enc_rim,
    partial,
    picks_v,
    proj_v,
    coarse_v,
    rim_picks,
    list_picks,
    short_table,
    short_rim,
    long_table,
    long_out,
    long_in,
    long_rows,
    dec_table,
    dec_rim,
    dec_picks,
    totals,
    gq_v,
    gp_v,
    in_sem,
    out_sem,
    halo_send,
    halo_recv,
    long_ssem,
    long_rsem,
    spread_sem,
):
    band = lax.axis_index("aa")
    sector = lax.axis_index("ba")
    me = band * N_BA + sector

    loads = {}

    def load(name, src, dst):
        copy = pltpu.make_async_copy(src, dst, in_sem.at[len(loads)])
        copy.start()
        loads[name] = copy

    def arrived(*names):
        for name in names:
            loads[name].wait()

    def at(first, second):
        return (
            lax.rem(band + (first + N_AA), N_AA),
            lax.rem(sector + (second + N_BA), N_BA),
        )

    def greet(semaphore, stride_first, stride_second, around):
        for k in around:
            pl.semaphore_signal(
                semaphore,
                inc=1,
                device_id=at(stride_first * ALONG_FIRST[k], stride_second * ALONG_SECOND[k]),
                device_id_type=MESH,
            )

    barrier = pltpu.get_barrier_semaphore()
    greet(barrier, 1, 1, range(8))

    load("grim", grid_rim, grim_v)
    load("grid", grid_nodes, grid_v)
    load("ef00", edge_first.at[0, 0], ef_v.at[0, 0])
    load("mesh", mesh_nodes, mesh_v)
    load("ef01", edge_first.at[0, 1], ef_v.at[0, 1])
    load("eb", edge_bias, eb_v)
    load("g2m", g2m_edges, g2m_v)
    def halo_copy(k, sem_base, rim, table, first, depth):
        return pltpu.make_async_remote_copy(
            src_ref=rim.at[pl.ds(k * depth, depth)],
            dst_ref=table.at[pl.ds(first + (7 - k) * depth, depth)],
            send_sem=halo_send.at[sem_base + k],
            recv_sem=halo_recv.at[sem_base + 7 - k],
            device_id=at(ALONG_FIRST[k], ALONG_SECOND[k]),
            device_id_type=MESH,
        )

    copies = []
    arrived("grim", "grid")
    for pair in ((5, 4), (3, 2), (7, 6), (1, 0)):
        cols = columns(jnp.concatenate([grim_v[0, k : k + 1, :] for k in pair], 1))
        rows = dot(one_hot(cols, 0, G_DEV), grid_v[...]).astype(BF16)
        if not copies:
            arrived("ef00")
        rows = (0.5 * dot(rows, ef_v[0, 0])).astype(BF16)
        for place, k in enumerate(pair):
            enc_rim[k * GB : (k + 1) * GB, :] = rows[place * GB : (place + 1) * GB, :]
        if not copies:
            pl.semaphore_wait(barrier, 8)
        for k in pair:
            copy = halo_copy(k, 0, enc_rim, enc_halo, 0, GB)
            copy.start()
            copies.append((k, copy))
    greet(spread_sem.at[0], 1, 1, range(8))
    load("es0", edge_second.at[0], es_v.at[0])
    load("ns0", node_second.at[0], ns_v.at[0])
    load("nf0", node_first.at[0], nf_v.at[0])
    load("eg", edge_gain, eg_v)
    load("ng", node_gain, ng_v)
    load("nb", node_bias, nb_v)
    load("mrim", mesh_rim, mrim_v)
    load("ef1", edge_first.at[1], ef_v.at[1])
    load("short", short_edges, short_v)
    load("es1", edge_second.at[1], es_v.at[1])
    load("nf1", node_first.at[1], nf_v.at[1])
    load("ns1", node_second.at[1], ns_v.at[1])
    load("send", long_send, send_v)
    load("ef2", edge_first.at[2], ef_v.at[2])
    load("long", long_edges, long_v)
    load("es2", edge_second.at[2], es_v.at[2])
    load("nf2", node_first.at[2], nf_v.at[2])
    load("ns2", node_second.at[2], ns_v.at[2])
    load("ef3", edge_first.at[3], ef_v.at[3])
    load("nf30", node_first.at[3, 0], nf_v.at[3, 0])
    load("es3", edge_second.at[3], es_v.at[3])
    load("ns3", node_second.at[3], ns_v.at[3])
    load("m2g", m2g_edges, m2g_v)

    for start in range(0, G_DEV, 512):
        half = 0.5 * dot(grid_v[start : start + 512, :], ef_v[0, 0])
        enc_table[start : start + 512, :] = half.astype(BF16)
    arrived("mesh", "ef01", "eb")
    enc_table[G_DEV : G_DEV + M_DEV, :] = (0.5 * (dot(mesh_v[...], ef_v[0, 1]) + eb_v[0:1, :])).astype(BF16)
    enc_table[G_DEV + M_DEV : G_DEV + 256, :] = jnp.zeros((64, D), BF16)
    proj_v[M_DEV:256, :] = jnp.zeros((64, D), BF16)
    coarse_v[...] = jnp.zeros((128, D), BF16)
    arrived("g2m")

    def tile_of(index):
        return pl.ds(index * TILE_LOCAL, TILE_LOCAL)

    def near_picks(index):
        here = tile_of(index)
        block, place = columns(g2m_v[0, 0:1, here])
        picks_v[here, :] = one_hot((block, place), G_DEV, 8 * GB)
        targets = columns(g2m_v[0, 1:2, here])
        return jnp.concatenate([one_hot((block, place), 0, G_DEV), one_hot(targets, 0, 256)], 1)

    tiles = E_G2M // TILE_LOCAL
    picks = near_picks(0)
    for index in range(tiles):
        sums = dot(picks, enc_table[...])
        if index + 1 < tiles:
            picks = near_picks(index + 1)
        partial[tile_of(index), :] = sums.astype(BF16)

    def centre(section):
        def block(step, carry):
            here = pl.ds(pl.multiple_of(step * 128, 128), 128)
            es_v[section, here, :] = centred_weights(es_v[section, here, :])
            ns_v[section, here, :] = centred_weights(ns_v[section, here, :])
            return carry

        lax.fori_loop(0, D // 128, block, 0)

    arrived("es0", "ns0")
    centre(0)
    arrived("mrim")
    sub = lax.broadcasted_iota(jnp.int32, (HB, HB), 0)
    lane = lax.broadcasted_iota(jnp.int32, (HB, HB), 1)
    parts = []
    for k in range(8):
        row = jnp.broadcast_to(mrim_v[0, k : k + 1, :].astype(F32), (HB, HB))
        col = jnp.sum(jnp.where(sub == lane, row, 0.0), axis=1, keepdims=True)
        parts.append(jnp.broadcast_to(col, (HB, 128)))
    rim_picks[...] = one_hot((None, jnp.concatenate(parts, 0).astype(BF16)), 0, 128)
    def rounds(section, tile, edges, count, picked):
        totals[...] = jnp.zeros((M_DEV, D), F32)
        tiles = count // tile
        hidden, result = {}, {}
        for step in range(tiles + 2):
            if step < tiles:
                half = picked(step * tile)
            if 0 <= step - 2:
                message = normalised(result.pop(step - 2)).astype(BF16)
            if 0 <= step - 1 < tiles:
                result[step - 1] = dot(hidden.pop(step - 1), es_v[section])
            if step < tiles:
                hidden[step] = silu_of_half(half)
            if 0 <= step - 2:
                targets = edges[0, 1:2, (step - 2) * tile : (step - 1) * tile]
                totals[...] += dot(scatter_matrix(targets), message)

    def updated(section, rows, sums):
        return node_update(
            rows,
            sums * eg_v[section : section + 1, :],
            nf_v[section, 0],
            nf_v[section, 1],
            nb_v[section : section + 1, :],
            ns_v[section],
            ng_v[section : section + 1, :],
        )

    arrived("nf0", "eg", "ng", "nb")
    pl.semaphore_wait(spread_sem.at[0], 8)
    greet(spread_sem.at[1], 2, 2, range(8))

    for k, copy in copies:
        if 7 - k < EARLY:
            copy.wait_recv()

    for index in range(tiles):
        here = tile_of(index)
        partial[here, :] += dot(picks_v[here, 0 : EARLY * GB], enc_halo[0 : EARLY * GB, :]).astype(BF16)
    for k, copy in copies:
        copy.wait_send()
        if 7 - k >= EARLY:
            copy.wait_recv()

    def enc_picked(start):
        here = pl.ds(start, TILE_ENC)
        late = dot(picks_v[here, EARLY * GB :], enc_halo[EARLY * GB :, :])
        return partial[here, :] + late.astype(BF16)

    rounds(0, TILE_ENC, g2m_v, E_G2M, enc_picked)
    mesh_v[...] = updated(0, mesh_v[...], totals[...])

    def mesh_halo(section, sem_base, rim, table):
        proj = (0.5 * dot(mesh_v[...], ef_v[section, 0])).astype(BF16)
        proj_v[0:M_DEV, :] = proj
        rim[...] = dot(rim_picks[...], proj_v[0:128, :]).astype(BF16)
        started = []
        for k in range(8):
            copy = halo_copy(k, sem_base, rim, table, M_DEV, HB)
            copy.start()
            started.append(copy)
        table[0:M_DEV, :] = proj
        return started

    arrived("ef1")
    copies = mesh_halo(1, 8, short_rim, short_table)
    short_table[M_DEV + 8 * HB : 512, :] = (0.5 * (dot(mesh_v[...], ef_v[1, 1]) + eb_v[1:2, :])).astype(
        BF16
    )
    arrived("short")

    def short_picks(step, carry):
        here = pl.ds(pl.multiple_of(step * TILE_LOCAL, TILE_LOCAL), TILE_LOCAL)
        senders = columns(short_v[0, 0:1, here])
        targets = columns(short_v[0, 1:2, here] + (M_DEV + 8 * HB))
        picks_v[here, 0:512] = double_one_hot(senders, targets, 512)
        return carry

    lax.fori_loop(0, E_MESH // TILE_LOCAL, short_picks, 0)
    arrived("es1", "ns1", "nf1", "send")
    centre(1)
    lists = send_v[0].astype(F32).astype(BF16)
    for start in range(0, DEVICES * KL, 512):
        sub = lax.broadcasted_iota(jnp.int32, (512, DEVICES), 0) + start
        lane = lax.broadcasted_iota(jnp.int32, (512, DEVICES), 1)
        owner = jnp.where(sub // KL == lane, 1.0, 0.0).astype(BF16)
        listed = lax.dot_general(owner, lists, (((1,), (1,)), ((), ())), preferred_element_type=F32)
        sub = lax.broadcasted_iota(jnp.int32, (512, KL), 0)
        lane = lax.broadcasted_iota(jnp.int32, (512, KL), 1)
        col = jnp.sum(jnp.where(lax.rem(sub, KL) == lane, listed, 0.0), axis=1, keepdims=True)
        list_picks[start : start + 512, :] = one_hot(
            (None, jnp.broadcast_to(col, (512, 128)).astype(BF16)), 0, 128
        )
    pl.semaphore_wait(spread_sem.at[1], 8)
    greet(spread_sem.at[2], 0, 4, (3, 4))
    for copy in copies:
        copy.wait()

    def short_picked(start):
        return dot(picks_v[pl.ds(start, TILE_MESH), 0:512], short_table[...]).astype(BF16)

    rounds(1, TILE_MESH, short_v, E_MESH, short_picked)

    arrived("ef2")
    coarse = updated(1, mesh_v[0:CS, :], totals[0:CS, :])
    coarse_v[0:CS, :] = (0.5 * dot(coarse, ef_v[2, 0])).astype(BF16)
    for start in range(0, DEVICES * KL, 512):
        rows = dot(list_picks[start : start + 512, :], coarse_v[...])
        long_out[start // KL : (start + 512) // KL] = rows.reshape(512 // KL, KL, D).astype(BF16)
    pl.semaphore_wait(spread_sem.at[2], 2)
    for first, second in PEERS:
        peer_first = lax.rem(band + first, N_AA)
        peer_second = (sector // 4 + second // 4) % 4 * 4 + (sector + second) % 4
        pltpu.make_async_remote_copy(
            src_ref=long_out.at[peer_first * N_BA + peer_second],
            dst_ref=long_in.at[me],
            send_sem=long_ssem,
            recv_sem=long_rsem,
            device_id=(peer_first, peer_second),
            device_id_type=MESH,
        ).start()
    long_in[me] = long_out[me]

    mesh_v[...] = updated(1, mesh_v[...], totals[...])
    long_table[0:M_DEV, :] = (0.5 * dot(mesh_v[...], ef_v[2, 0])).astype(BF16)
    long_table[M_DEV : 2 * M_DEV, :] = (0.5 * (dot(mesh_v[...], ef_v[2, 1]) + eb_v[2:3, :])).astype(BF16)
    arrived("long")

    def long_local(step, carry):
        here = pl.ds(pl.multiple_of(step * TILE_LOCAL, TILE_LOCAL), TILE_LOCAL)
        senders = long_v[0, 0:1, here]
        own = columns(jnp.where(senders < M_DEV, senders, NOWHERE))
        targets = columns(long_v[0, 1:2, here] + M_DEV)
        sums = dot(double_one_hot(own, targets, 2 * M_DEV), long_table[...])
        partial[here, :] = sums.astype(BF16)
        away = columns(jnp.where(senders < M_DEV, NOWHERE, senders - M_DEV))
        picks_v[here, :] = one_hot(away, 0, DEVICES * KL)
        return carry

    lax.fori_loop(0, E_MESH // TILE_LOCAL, long_local, 0)
    arrived("ef3", "nf30", "es2", "ns2", "es3", "ns3", "m2g")
    centre(2)
    for start in range(0, G_DEV, 512):
        rows = grid_v[start : start + 512, :]
        gq_v[start : start + 512, :] = (0.5 * (dot(rows, ef_v[3, 1]) + eb_v[3:4, :])).astype(BF16)
        gp_v[start : start + 512, :] = (0.5 * (dot(rows, nf_v[3, 0]) + nb_v[3:4, :])).astype(BF16)
    centre(3)
    gq_copy = pltpu.make_async_copy(gq_v, gq_out, out_sem.at[0])
    gp_copy = pltpu.make_async_copy(gp_v, gp_out, out_sem.at[1])
    es_copy = pltpu.make_async_copy(es_v.at[3], second_out.at[0], out_sem.at[2])
    ns_copy = pltpu.make_async_copy(ns_v.at[3], second_out.at[1], out_sem.at[3])
    outs = [gq_copy, gp_copy, es_copy, ns_copy]

    def dec_ids(step, carry):
        here = pl.ds(pl.multiple_of(step * 512, 512), 512)
        for k in range(3):
            dec_picks[k, here, :] = one_hot(columns(m2g_v[k, :, here]), 0, 384)
        return carry

    lax.fori_loop(0, G_DEV // 512, dec_ids, 0)
    outs.append(pltpu.make_async_copy(dec_picks, picks_out, out_sem.at[4]))
    for copy in outs:
        copy.start()
    arrived("nf2")
    others = pl.ds(0, DEVICES - 1)
    pltpu.make_async_copy(long_out.at[others], long_out.at[others], long_ssem).wait()
    pltpu.make_async_copy(long_in.at[others], long_in.at[others], long_rsem).wait()
    for start in range(0, DEVICES, 32):
        block = long_in[start : start + 32].astype(F32).reshape(32 * KL, D)
        long_rows[start * KL : (start + 32) * KL, :] = block.astype(BF16)

    def long_picked(start):
        here = pl.ds(start, TILE_MESH)
        return partial[here, :] + dot(picks_v[here, :], long_rows[...]).astype(BF16)

    rounds(2, TILE_MESH, long_v, E_MESH, long_picked)
    mesh_v[...] = updated(2, mesh_v[...], totals[...])

    copies = mesh_halo(3, 16, dec_rim, dec_table)
    dec_table[M_DEV + 8 * HB : 384, :] = jnp.zeros((64, D), BF16)
    outs.append(pltpu.make_async_copy(mesh_v, mesh_out, out_sem.at[5]))
    outs[-1].start()
    for copy in outs:
        copy.wait()
    for copy in copies:
        copy.wait()
    dec_copy = pltpu.make_async_copy(dec_table, dec_out, out_sem.at[6])
    dec_copy.start()
    dec_copy.wait()


def mesh_part(*operands):
    vmem = pltpu.VMEM
    anywhere = pl.BlockSpec(memory_space=pl.ANY)
    return pl.pallas_call(
        mesh_kernel,
        name="mesh_part",
        in_specs=[anywhere] * 17,
        out_specs=[anywhere] * 6,
        out_shape=[
            jax.ShapeDtypeStruct((384, D), BF16),
            jax.ShapeDtypeStruct((M_DEV, D), BF16),
            jax.ShapeDtypeStruct((G_DEV, D), BF16),
            jax.ShapeDtypeStruct((G_DEV, D), BF16),
            jax.ShapeDtypeStruct((3, G_DEV, 384), BF16),
            jax.ShapeDtypeStruct((2, D, D), BF16),
        ],
        scratch_shapes=[
            vmem((G_DEV, D), BF16),
            vmem((M_DEV, D), BF16),
            vmem((1, 8, GB), jnp.int32),
            vmem((1, 8, HB), jnp.int32),
            vmem((1, KL, DEVICES), jnp.int32),
            vmem((1, 2, E_G2M), jnp.int32),
            vmem((1, 2, E_MESH), jnp.int32),
            vmem((1, 2, E_MESH), jnp.int32),
            vmem((3, 1, G_DEV), jnp.int32),
            vmem((4, 2, D, D), BF16),
            vmem((4, D, D), BF16),
            vmem((4, D), F32),
            vmem((4, D), F32),
            vmem((4, 2, D, D), BF16),
            vmem((4, D, D), BF16),
            vmem((4, D), F32),
            vmem((4, D), F32),
            vmem((G_DEV + 256, D), BF16),
            vmem((8 * GB, D), BF16),
            vmem((8 * GB, D), BF16),
            vmem((E_G2M, D), BF16),
            vmem((E_G2M, 8 * GB), BF16),
            vmem((256, D), BF16),
            vmem((128, D), BF16),
            vmem((128, 128), BF16),
            vmem((DEVICES * KL, 128), BF16),
            vmem((512, D), BF16),
            vmem((8 * HB, D), BF16),
            vmem((2 * M_DEV, D), BF16),
            vmem((DEVICES, KL, D), BF16),
            vmem((DEVICES, KL, D), BF16),
            vmem((DEVICES * KL, D), BF16),
            vmem((384, D), BF16),
            vmem((8 * HB, D), BF16),
            vmem((3, G_DEV, 384), BF16),
            vmem((M_DEV, D), F32),
            vmem((G_DEV, D), BF16),
            vmem((G_DEV, D), BF16),
            pltpu.SemaphoreType.DMA((30,)),
            pltpu.SemaphoreType.DMA((7,)),
            pltpu.SemaphoreType.DMA((24,)),
            pltpu.SemaphoreType.DMA((24,)),
            pltpu.SemaphoreType.DMA,
            pltpu.SemaphoreType.DMA,
            pltpu.SemaphoreType.REGULAR((3,)),
        ],
        compiler_params=pltpu.CompilerParams(
            collective_id=0, has_side_effects=True, vmem_limit_bytes=60 * 1024 * 1024
        ),
    )(*operands)


DEC_TILE = 256
DEC_ROWS = 512


def decode_kernel(
    owned,
    picks,
    table,
    gq,
    gp,
    grid_rows,
    mesh_rows,
    seconds,
    node_sum,
    edge_gain,
    node_gain,
    grid_out,
    mesh_out,
    picks_v,
    total_v,
    table_v,
    gq_v,
    gp_v,
    grid_v,
    mesh_v,
    second_v,
    sum_v,
    eg_v,
    ng_v,
    in_sem,
    out_sem,
):
    tiles = G_DEV // DEC_TILE
    loads = {}

    def load(name, src, dst):
        copy = pltpu.make_async_copy(src, dst, in_sem.at[len(loads)])
        copy.start()
        loads[name] = copy

    def part(index):
        return pl.ds(index * DEC_TILE, DEC_TILE)

    load("table", table, table_v)
    for t in range(tiles):
        load(("picks", t), picks.at[:, part(t)], picks_v.at[:, part(t)])
        load(("gq", t), gq.at[part(t)], gq_v.at[part(t)])
        if t == 0:
            load("es", seconds.at[0], second_v.at[0])
            load("eg", edge_gain, eg_v)
    load("nf", node_sum.at[3, 1], sum_v)
    load("ns", seconds.at[1], second_v.at[1])
    load("ng", node_gain, ng_v)
    for t in range(tiles):
        load(("gp", t), gp.at[part(t)], gp_v.at[part(t)])
        load(("grid", t), grid_rows.at[part(t)], grid_v.at[part(t)])
    load("mesh", mesh_rows, mesh_v)
    outs = []
    hidden, result, node, update = {}, {}, {}, {}

    def rows_of(index):
        return pl.ds(index * DEC_ROWS, DEC_ROWS)

    blocks = G_DEV // DEC_ROWS
    first_block = DEC_ROWS // DEC_TILE + 2

    def node_start(t):
        if t == 0:
            for name in ("nf", "ns", "ng"):
                loads[name].wait()
        for index in range(t * DEC_ROWS // DEC_TILE, (t + 1) * DEC_ROWS // DEC_TILE):
            loads["gp", index].wait()
            loads["grid", index].wait()
        return (0.5 * dot(total_v[rows_of(t), :], sum_v[...])).astype(BF16)

    def node_end(t):
        rows = grid_v[rows_of(t), :].astype(F32) + normalised(update.pop(t)) * ng_v[3:4, :]
        grid_v[rows_of(t), :] = rows.astype(BF16)
        outs.append(
            pltpu.make_async_copy(grid_v.at[rows_of(t)], grid_out.at[rows_of(t)], out_sem.at[t])
        )
        outs[-1].start()

    loads["table"].wait()
    gap = DEC_ROWS // DEC_TILE
    for step in range(first_block + gap * (blocks - 1) + 3):
        if step < tiles:
            loads["picks", step].wait()
            loads["gq", step].wait()
            picked = dot(picks_v[:, part(step), :].reshape(3 * DEC_TILE, 384), table_v[...]).astype(BF16)
        t = step - 2
        if 0 <= t < tiles:
            message = normalised(result.pop(t))
            summed = message[0:DEC_TILE] + message[DEC_TILE : 2 * DEC_TILE] + message[2 * DEC_TILE :]
            total_v[part(t), :] = (summed * eg_v[3:4, :]).astype(BF16)
        t = step - 1
        if 0 <= t < tiles:
            if t == 0:
                loads["es"].wait()
                loads["eg"].wait()
            result[t] = dot(hidden.pop(t), second_v[0])
        block, phase = divmod(step - first_block, gap) if gap > 1 else (step - first_block, 0)
        starts = phase == 0 and 0 <= block < blocks
        if starts:
            pre = node_start(block)
        if step < tiles:
            hidden[step] = silu_of_half(picked + jnp.concatenate([gq_v[part(step), :]] * 3, 0))
        for t in list(update):
            node_end(t)
        for t in list(node):
            update[t] = dot(node.pop(t), second_v[1])
        if starts:
            node[block] = silu_of_half(pre + gp_v[rows_of(block), :])
        if step == tiles:
            loads["mesh"].wait()
            slot = lax.broadcasted_iota(jnp.int32, (M_DEV, D), 0)
            mesh_v[...] = jnp.where(slot < owned[0], mesh_v[...].astype(F32), 0.0).astype(BF16)
            outs.append(pltpu.make_async_copy(mesh_v, mesh_out, out_sem.at[tiles]))
            outs[-1].start()
    for copy in outs:
        copy.wait()


def decode_part(*operands):
    vmem = pltpu.VMEM
    anywhere = pl.BlockSpec(memory_space=pl.ANY)
    tiles = G_DEV // DEC_TILE
    return pl.pallas_call(
        decode_kernel,
        name="decode_part",
        in_specs=[pl.BlockSpec(memory_space=pltpu.SMEM)] + [anywhere] * 10,
        out_specs=[anywhere] * 2,
        out_shape=[
            jax.ShapeDtypeStruct((G_DEV, D), BF16),
            jax.ShapeDtypeStruct((M_DEV, D), BF16),
        ],
        scratch_shapes=[
            vmem((3, G_DEV, 384), BF16),
            vmem((G_DEV, D), BF16),
            vmem((384, D), BF16),
            vmem((G_DEV, D), BF16),
            vmem((G_DEV, D), BF16),
            vmem((G_DEV, D), BF16),
            vmem((M_DEV, D), BF16),
            vmem((2, D, D), BF16),
            vmem((D, D), BF16),
            vmem((4, D), F32),
            vmem((4, D), F32),
            pltpu.SemaphoreType.DMA((8 + 4 * tiles,)),
            pltpu.SemaphoreType.DMA((tiles + 1,)),
        ],
        compiler_params=pltpu.CompilerParams(vmem_limit_bytes=60 * 1024 * 1024),
    )(*operands)


def per_device(
    grid_nodes,
    mesh_nodes,
    owned_nodes,
    grid_rim,
    mesh_rim,
    long_send,
    g2m_edges,
    short_edges,
    long_edges,
    m2g_edges,
    edge_first,
    edge_second,
    edge_bias,
    edge_gain,
    node_first,
    node_second,
    node_bias,
    node_gain,
):
    table, mesh_three, gq, gp, picks, seconds = mesh_part(
        grid_nodes,
        mesh_nodes,
        grid_rim,
        mesh_rim,
        jnp.transpose(long_send, (0, 2, 1)),
        g2m_edges,
        short_edges,
        long_edges,
        jnp.transpose(m2g_edges, (1, 0, 2)),
        edge_first,
        edge_second,
        edge_bias,
        edge_gain,
        node_first,
        node_second,
        node_bias,
        node_gain,
    )
    grid_out, mesh_out = decode_part(
        owned_nodes,
        picks,
        table,
        gq,
        gp,
        grid_nodes,
        mesh_three,
        seconds,
        node_first,
        edge_gain,
        node_gain,
    )
    return (grid_out, mesh_out)


def solution(mesh):
    rows = P(("aa", "ba"), None)
    lists = P(("aa", "ba"), None, None)
    in_specs = (rows, rows, P(("aa", "ba"))) + (lists,) * 7 + (P(),) * 8
    return jax.shard_map(
        per_device, mesh=mesh, in_specs=in_specs, out_specs=(rows, rows), check_vma=False
    )
```

```python
import jax
import jax.numpy as jnp
from jax import lax
from jax.experimental import pallas as pl
from jax.experimental.pallas import tpu as pltpu
from jax.sharding import PartitionSpec as P

EPSILON = 1e-05
D = 512
G_DEV = 1024
M_DEV = 192
GB = 128
HB = 16
KL = 8
CS = 16
NOWHERE = 4095
EARLY = 4
N_AA = 8
N_BA = 16
DEVICES = 128
E_G2M = 3072
E_MESH = 1536
TILE_LOCAL = 512
TILE_ENC = 768
TILE_MESH = 768
ALONG_FIRST = (-1, -1, -1, 0, 0, 1, 1, 1)
ALONG_SECOND = (-1, 0, 1, -1, 1, -1, 0, 1)
F32 = jnp.float32
BF16 = jnp.bfloat16
MESH = pl.DeviceIdType.MESH


def hops(first, second):
    steps = ((first + 1) // 2, second // 4, second % 4)
    return sum(min(step, 4 - step) for step in steps)


GROUP_ORDER = (2, 1, 3, 0)
PEERS = sorted(
    [(a, b) for a in range(N_AA) for b in range(N_BA) if (a, b) != (0, 0)],
    key=lambda peer: (GROUP_ORDER.index(peer[1] // 4), -hops(*peer)),
)


def dot(a, b):
    return jnp.dot(a, b, preferred_element_type=F32)


def silu_of_half(half):
    return half * jnp.tanh(half) + half


def centred_weights(weights):
    wide = weights.astype(F32)
    return (wide - jnp.mean(wide, axis=-1, keepdims=True)).astype(BF16)


def normalised(centred):
    spread = jnp.mean(centred * centred, axis=-1, keepdims=True)
    return centred * lax.rsqrt(spread + EPSILON)


def spread_out(row):
    parts = []
    for start in range(0, row.shape[1], 128):
        parts.append(jnp.broadcast_to(row[:, start : start + 128], (128, 128)).T.astype(BF16))
    return parts[0] if len(parts) == 1 else jnp.concatenate(parts, 0)


def columns(row):
    return spread_out((row >> 8).astype(F32)), spread_out((row & 255).astype(F32))


def lane_ids(rows):
    lane = lax.broadcasted_iota(jnp.int32, (rows, 128), 1).astype(F32)
    return lane.astype(BF16), (lane + 128.0).astype(BF16)


def one_hot(cols, first, width):
    block, place = cols
    lanes = lane_ids(place.shape[0])
    one, zero = jnp.ones((), BF16), jnp.zeros((), BF16)
    parts = []
    for start in range(first, first + width, 256):
        here = place
        if block is not None:
            here = jnp.where(block == jnp.asarray(start // 256, BF16), place, jnp.asarray(-1, BF16))
        for half in range(2):
            if start + 128 * half < first + width:
                parts.append(jnp.where(here == lanes[half], one, zero))
    return parts[0] if len(parts) == 1 else jnp.concatenate(parts, 1)


def double_one_hot(first, second, width):
    lanes = lane_ids(first[1].shape[0])
    one, zero, none = jnp.ones((), BF16), jnp.zeros((), BF16), jnp.asarray(-1, BF16)
    parts = []
    for start in range(0, width, 256):
        group = jnp.asarray(start // 256, BF16)
        one_here = jnp.where(first[0] == group, first[1], none)
        two_here = jnp.where(second[0] == group, second[1], none)
        for half in range(2):
            if start + 128 * half < width:
                found = (one_here == lanes[half]) | (two_here == lanes[half])
                parts.append(jnp.where(found, one, zero))
    return jnp.concatenate(parts, 1)


def scatter_matrix(row):
    slots = lax.broadcasted_iota(jnp.int32, (M_DEV, row.shape[1]), 0).astype(F32).astype(BF16)
    ids = row.astype(F32).astype(BF16)
    return jnp.where(slots == ids, jnp.ones((), BF16), jnp.zeros((), BF16))


def node_update(rows, totals, first_own, first_sum, bias, second, gain):
    pre = dot(rows, first_own) + dot(totals.astype(BF16), first_sum) + bias
    result = dot(silu_of_half((0.5 * pre).astype(BF16)), second)
    result = normalised(result) * gain
    return (rows.astype(F32) + result).astype(BF16)


def mesh_kernel(
    grid_nodes,
    mesh_nodes,
    grid_rim,
    mesh_rim,
    long_send,
    g2m_edges,
    short_edges,
    long_edges,
    m2g_edges,
    edge_first,
    edge_second,
    edge_bias,
    edge_gain,
    node_first,
    node_second,
    node_bias,
    node_gain,
    dec_out,
    mesh_out,
    gq_out,
    gp_out,
    picks_out,
    second_out,
    grid_v,
    mesh_v,
    grim_v,
    mrim_v,
    send_v,
    g2m_v,
    short_v,
    long_v,
    m2g_v,
    ef_v,
    es_v,
    eb_v,
    eg_v,
    nf_v,
    ns_v,
    nb_v,
    ng_v,
    enc_table,
    enc_halo,
    enc_rim,
    partial,
    picks_v,
    proj_v,
    coarse_v,
    rim_picks,
    list_picks,
    short_table,
    short_rim,
    long_table,
    long_out,
    long_in,
    long_rows,
    dec_halo,
    dec_rim,
    dec_picks,
    dec_near,
    dec_sums,
    totals,
    gq_v,
    gp_v,
    in_sem,
    out_sem,
    halo_send,
    halo_recv,
    long_ssem,
    long_rsem,
    spread_sem,
):
    band = lax.axis_index("aa")
    sector = lax.axis_index("ba")
    me = band * N_BA + sector

    loads = {}

    def load(name, src, dst):
        copy = pltpu.make_async_copy(src, dst, in_sem.at[len(loads)])
        copy.start()
        loads[name] = copy

    def arrived(*names):
        for name in names:
            loads[name].wait()

    def at(first, second):
        return (
            lax.rem(band + (first + N_AA), N_AA),
            lax.rem(sector + (second + N_BA), N_BA),
        )

    def greet(semaphore, stride_first, stride_second, around):
        for k in around:
            pl.semaphore_signal(
                semaphore,
                inc=1,
                device_id=at(stride_first * ALONG_FIRST[k], stride_second * ALONG_SECOND[k]),
                device_id_type=MESH,
            )

    barrier = pltpu.get_barrier_semaphore()
    greet(barrier, 1, 1, range(8))

    load("grim", grid_rim, grim_v)
    load("grid", grid_nodes, grid_v)
    load("ef00", edge_first.at[0, 0], ef_v.at[0, 0])
    load("mesh", mesh_nodes, mesh_v)
    load("ef01", edge_first.at[0, 1], ef_v.at[0, 1])
    load("eb", edge_bias, eb_v)
    load("g2m", g2m_edges, g2m_v)
    def halo_copy(k, sem_base, rim, table, first, depth):
        return pltpu.make_async_remote_copy(
            src_ref=rim.at[pl.ds(k * depth, depth)],
            dst_ref=table.at[pl.ds(first + (7 - k) * depth, depth)],
            send_sem=halo_send.at[sem_base + k],
            recv_sem=halo_recv.at[sem_base + 7 - k],
            device_id=at(ALONG_FIRST[k], ALONG_SECOND[k]),
            device_id_type=MESH,
        )

    copies = []
    arrived("grim", "grid")
    for pair in ((5, 4), (3, 2), (7, 6), (1, 0)):
        cols = columns(jnp.concatenate([grim_v[0, k : k + 1, :] for k in pair], 1))
        rows = dot(one_hot(cols, 0, G_DEV), grid_v[...]).astype(BF16)
        if not copies:
            arrived("ef00")
        rows = (0.5 * dot(rows, ef_v[0, 0])).astype(BF16)
        for place, k in enumerate(pair):
            enc_rim[k * GB : (k + 1) * GB, :] = rows[place * GB : (place + 1) * GB, :]
        if not copies:
            pl.semaphore_wait(barrier, 8)
        for k in pair:
            copy = halo_copy(k, 0, enc_rim, enc_halo, 0, GB)
            copy.start()
            copies.append((k, copy))
    greet(spread_sem.at[0], 1, 1, range(8))
    load("es0", edge_second.at[0], es_v.at[0])
    load("ns0", node_second.at[0], ns_v.at[0])
    load("nf0", node_first.at[0], nf_v.at[0])
    load("eg", edge_gain, eg_v)
    load("ng", node_gain, ng_v)
    load("nb", node_bias, nb_v)
    load("mrim", mesh_rim, mrim_v)
    load("ef1", edge_first.at[1], ef_v.at[1])
    load("short", short_edges, short_v)
    load("es1", edge_second.at[1], es_v.at[1])
    load("nf1", node_first.at[1], nf_v.at[1])
    load("ns1", node_second.at[1], ns_v.at[1])
    load("send", long_send, send_v)
    load("ef2", edge_first.at[2], ef_v.at[2])
    load("long", long_edges, long_v)
    load("es2", edge_second.at[2], es_v.at[2])
    load("nf2", node_first.at[2], nf_v.at[2])
    load("ns2", node_second.at[2], ns_v.at[2])
    load("ef3", edge_first.at[3], ef_v.at[3])
    load("nf30", node_first.at[3, 0], nf_v.at[3, 0])
    load("es3", edge_second.at[3], es_v.at[3])
    load("ns3", node_second.at[3], ns_v.at[3])
    load("m2g", m2g_edges, m2g_v)

    for start in range(0, G_DEV, 512):
        half = 0.5 * dot(grid_v[start : start + 512, :], ef_v[0, 0])
        enc_table[start : start + 512, :] = half.astype(BF16)
    arrived("mesh", "ef01", "eb")
    enc_table[G_DEV : G_DEV + M_DEV, :] = (0.5 * (dot(mesh_v[...], ef_v[0, 1]) + eb_v[0:1, :])).astype(BF16)
    enc_table[G_DEV + M_DEV : G_DEV + 256, :] = jnp.zeros((64, D), BF16)
    proj_v[M_DEV:256, :] = jnp.zeros((64, D), BF16)
    coarse_v[...] = jnp.zeros((128, D), BF16)
    arrived("g2m")

    def tile_of(index):
        return pl.ds(index * TILE_LOCAL, TILE_LOCAL)

    def near_picks(index):
        here = tile_of(index)
        block, place = columns(g2m_v[0, 0:1, here])
        picks_v[here, :] = one_hot((block, place), G_DEV, 8 * GB)
        targets = columns(g2m_v[0, 1:2, here])
        return jnp.concatenate([one_hot((block, place), 0, G_DEV), one_hot(targets, 0, 256)], 1)

    tiles = E_G2M // TILE_LOCAL
    picks = near_picks(0)
    for index in range(tiles):
        sums = dot(picks, enc_table[...])
        if index + 1 < tiles:
            picks = near_picks(index + 1)
        partial[tile_of(index), :] = sums.astype(BF16)

    def centre(section):
        def block(step, carry):
            here = pl.ds(pl.multiple_of(step * 128, 128), 128)
            es_v[section, here, :] = centred_weights(es_v[section, here, :])
            ns_v[section, here, :] = centred_weights(ns_v[section, here, :])
            return carry

        lax.fori_loop(0, D // 128, block, 0)

    arrived("es0", "ns0")
    centre(0)
    arrived("mrim")
    sub = lax.broadcasted_iota(jnp.int32, (HB, HB), 0)
    lane = lax.broadcasted_iota(jnp.int32, (HB, HB), 1)
    parts = []
    for k in range(8):
        row = jnp.broadcast_to(mrim_v[0, k : k + 1, :].astype(F32), (HB, HB))
        col = jnp.sum(jnp.where(sub == lane, row, 0.0), axis=1, keepdims=True)
        parts.append(jnp.broadcast_to(col, (HB, 128)))
    rim_picks[...] = one_hot((None, jnp.concatenate(parts, 0).astype(BF16)), 0, 128)
    def rounds(section, tile, edges, count, picked):
        totals[...] = jnp.zeros((M_DEV, D), F32)
        tiles = count // tile
        hidden, result = {}, {}
        for step in range(tiles + 2):
            if step < tiles:
                half = picked(step * tile)
            if 0 <= step - 2:
                message = normalised(result.pop(step - 2)).astype(BF16)
            if 0 <= step - 1 < tiles:
                result[step - 1] = dot(hidden.pop(step - 1), es_v[section])
            if step < tiles:
                hidden[step] = silu_of_half(half)
            if 0 <= step - 2:
                targets = edges[0, 1:2, (step - 2) * tile : (step - 1) * tile]
                totals[...] += dot(scatter_matrix(targets), message)

    def updated(section, rows, sums):
        return node_update(
            rows,
            sums * eg_v[section : section + 1, :],
            nf_v[section, 0],
            nf_v[section, 1],
            nb_v[section : section + 1, :],
            ns_v[section],
            ng_v[section : section + 1, :],
        )

    arrived("nf0", "eg", "ng", "nb")
    pl.semaphore_wait(spread_sem.at[0], 8)
    greet(spread_sem.at[1], 2, 2, range(8))

    for k, copy in copies:
        if 7 - k < EARLY:
            copy.wait_recv()

    for index in range(tiles):
        here = tile_of(index)
        partial[here, :] += dot(picks_v[here, 0 : EARLY * GB], enc_halo[0 : EARLY * GB, :]).astype(BF16)
    for k, copy in copies:
        copy.wait_send()
        if 7 - k >= EARLY:
            copy.wait_recv()

    def enc_picked(start):
        here = pl.ds(start, TILE_ENC)
        late = dot(picks_v[here, EARLY * GB :], enc_halo[EARLY * GB :, :])
        return partial[here, :] + late.astype(BF16)

    rounds(0, TILE_ENC, g2m_v, E_G2M, enc_picked)
    mesh_v[...] = updated(0, mesh_v[...], totals[...])

    def mesh_halo(section, sem_base, rim, table, first):
        proj = (0.5 * dot(mesh_v[...], ef_v[section, 0])).astype(BF16)
        proj_v[0:M_DEV, :] = proj
        rim[...] = dot(rim_picks[...], proj_v[0:128, :]).astype(BF16)
        started = []
        for k in range(8):
            copy = halo_copy(k, sem_base, rim, table, first, HB)
            copy.start()
            started.append(copy)
        if first:
            table[0:first, :] = proj
        return started

    arrived("ef1")
    copies = mesh_halo(1, 8, short_rim, short_table, M_DEV)
    short_table[M_DEV + 8 * HB : 512, :] = (0.5 * (dot(mesh_v[...], ef_v[1, 1]) + eb_v[1:2, :])).astype(
        BF16
    )
    arrived("short")

    def short_picks(step, carry):
        here = pl.ds(pl.multiple_of(step * TILE_LOCAL, TILE_LOCAL), TILE_LOCAL)
        senders = columns(short_v[0, 0:1, here])
        targets = columns(short_v[0, 1:2, here] + (M_DEV + 8 * HB))
        picks_v[here, 0:512] = double_one_hot(senders, targets, 512)
        return carry

    lax.fori_loop(0, E_MESH // TILE_LOCAL, short_picks, 0)
    arrived("es1", "ns1", "nf1", "send")
    centre(1)
    lists = send_v[0].astype(F32).astype(BF16)
    for start in range(0, DEVICES * KL, 512):
        sub = lax.broadcasted_iota(jnp.int32, (512, DEVICES), 0) + start
        lane = lax.broadcasted_iota(jnp.int32, (512, DEVICES), 1)
        owner = jnp.where(sub // KL == lane, 1.0, 0.0).astype(BF16)
        listed = lax.dot_general(owner, lists, (((1,), (1,)), ((), ())), preferred_element_type=F32)
        sub = lax.broadcasted_iota(jnp.int32, (512, KL), 0)
        lane = lax.broadcasted_iota(jnp.int32, (512, KL), 1)
        col = jnp.sum(jnp.where(lax.rem(sub, KL) == lane, listed, 0.0), axis=1, keepdims=True)
        list_picks[start : start + 512, :] = one_hot(
            (None, jnp.broadcast_to(col, (512, 128)).astype(BF16)), 0, 128
        )
    pl.semaphore_wait(spread_sem.at[1], 8)
    greet(spread_sem.at[2], 0, 4, (3, 4))
    for copy in copies:
        copy.wait()

    def short_picked(start):
        return dot(picks_v[pl.ds(start, TILE_MESH), 0:512], short_table[...]).astype(BF16)

    rounds(1, TILE_MESH, short_v, E_MESH, short_picked)

    arrived("ef2")
    coarse = updated(1, mesh_v[0:CS, :], totals[0:CS, :])
    coarse_v[0:CS, :] = (0.5 * dot(coarse, ef_v[2, 0])).astype(BF16)
    for start in range(0, DEVICES * KL, 512):
        rows = dot(list_picks[start : start + 512, :], coarse_v[...])
        long_out[start // KL : (start + 512) // KL] = rows.reshape(512 // KL, KL, D).astype(BF16)
    pl.semaphore_wait(spread_sem.at[2], 2)
    for first, second in PEERS:
        peer_first = lax.rem(band + first, N_AA)
        peer_second = (sector // 4 + second // 4) % 4 * 4 + (sector + second) % 4
        group = -(second // 4) % 4
        slot = group * 32 + -first % N_AA * 4 + -second % 4
        pltpu.make_async_remote_copy(
            src_ref=long_out.at[peer_first * N_BA + peer_second],
            dst_ref=long_in.at[slot],
            send_sem=long_ssem,
            recv_sem=long_rsem.at[group],
            device_id=(peer_first, peer_second),
            device_id_type=MESH,
        ).start()
    long_in[0] = long_out[me]

    mesh_v[...] = updated(1, mesh_v[...], totals[...])
    long_table[0:M_DEV, :] = (0.5 * dot(mesh_v[...], ef_v[2, 0])).astype(BF16)
    long_table[M_DEV : 2 * M_DEV, :] = (0.5 * (dot(mesh_v[...], ef_v[2, 1]) + eb_v[2:3, :])).astype(BF16)
    arrived("long")

    def long_local(step, carry):
        here = pl.ds(pl.multiple_of(step * TILE_LOCAL, TILE_LOCAL), TILE_LOCAL)
        senders = long_v[0, 0:1, here]
        own = columns(jnp.where(senders < M_DEV, senders, NOWHERE))
        targets = columns(long_v[0, 1:2, here] + M_DEV)
        sums = dot(double_one_hot(own, targets, 2 * M_DEV), long_table[...])
        partial[here, :] = sums.astype(BF16)
        far = jnp.maximum(senders - M_DEV, 0)
        peer = far >> 3
        slot = (((peer >> 2) - (sector >> 2)) & 3) * 32
        slot = slot + (((peer >> 4) - band) & 7) * 4 + ((peer - sector) & 3)
        away = columns(jnp.where(senders < M_DEV, NOWHERE, slot * KL + (far & 7)))
        picks_v[here, :] = one_hot(away, 0, DEVICES * KL)
        return carry

    lax.fori_loop(0, E_MESH // TILE_LOCAL, long_local, 0)
    arrived("ef3", "nf30", "es2", "ns2", "es3", "ns3", "m2g")
    centre(2)
    for start in range(0, G_DEV, 512):
        rows = grid_v[start : start + 512, :]
        gq_v[start : start + 512, :] = (0.5 * (dot(rows, ef_v[3, 1]) + eb_v[3:4, :])).astype(BF16)
        gp_v[start : start + 512, :] = (0.5 * (dot(rows, nf_v[3, 0]) + nb_v[3:4, :])).astype(BF16)
    centre(3)
    gp_copy = pltpu.make_async_copy(gp_v, gp_out, out_sem.at[1])
    es_copy = pltpu.make_async_copy(es_v.at[3], second_out.at[0], out_sem.at[2])
    ns_copy = pltpu.make_async_copy(ns_v.at[3], second_out.at[1], out_sem.at[3])
    outs = [gp_copy, es_copy, ns_copy]

    def dec_ids(step, carry):
        here = pl.ds(pl.multiple_of(step * 512, 512), 512)
        for k in range(3):
            senders = m2g_v[k, :, here]
            dec_near[k, here, :] = one_hot(columns(senders), 0, 256)
            rims = jnp.where(senders < M_DEV, NOWHERE, senders - M_DEV)
            dec_picks[k, here, :] = one_hot(columns(rims), 0, 128)
        return carry

    lax.fori_loop(0, G_DEV // 512, dec_ids, 0)
    outs.append(pltpu.make_async_copy(dec_picks, picks_out, out_sem.at[4]))
    for copy in outs:
        copy.start()
    arrived("nf2")
    def long_arrived(group):
        first = 1 if group == 0 else group * 32
        blocks = long_in.at[pl.ds(first, (group + 1) * 32 - first)]
        pltpu.make_async_copy(blocks, blocks, long_rsem.at[group]).wait()
        rows = long_in[group * 32 : (group + 1) * 32].astype(F32).reshape(32 * KL, D)
        long_rows[group * 256 : (group + 1) * 256, :] = rows.astype(BF16)

    for group in (2, 3, 1):
        long_arrived(group)
        some = pl.ds(group * 256, 256)
        for index in range(E_MESH // TILE_LOCAL):
            here = tile_of(index)
            partial[here, :] += dot(picks_v[here, some], long_rows[some, :]).astype(BF16)
    others = pl.ds(0, DEVICES - 1)
    pltpu.make_async_copy(long_out.at[others], long_out.at[others], long_ssem).wait()
    long_arrived(0)

    def long_picked(start):
        here = pl.ds(start, TILE_MESH)
        return partial[here, :] + dot(picks_v[here, 0:256], long_rows[0:256, :]).astype(BF16)

    rounds(2, TILE_MESH, long_v, E_MESH, long_picked)
    mesh_v[...] = updated(2, mesh_v[...], totals[...])

    copies = mesh_halo(3, 16, dec_rim, dec_halo, 0)
    outs.append(pltpu.make_async_copy(mesh_v, mesh_out, out_sem.at[5]))
    outs[-1].start()
    for half in range(2):
        for k in range(3):
            here = pl.ds(half * 512, 512)
            sums = dot(dec_near[k, here, :], proj_v[...]).astype(BF16)
            dec_sums[k, here, :] = sums + gq_v[here, :]
            outs.append(
                pltpu.make_async_copy(
                    dec_sums.at[k, here], gq_out.at[k, here], out_sem.at[7 + 3 * half + k]
                )
            )
            outs[-1].start()
    for copy in copies:
        copy.wait()
    outs.append(pltpu.make_async_copy(dec_halo, dec_out, out_sem.at[6]))
    outs[-1].start()
    for copy in outs:
        copy.wait()


def mesh_part(*operands):
    vmem = pltpu.VMEM
    anywhere = pl.BlockSpec(memory_space=pl.ANY)
    return pl.pallas_call(
        mesh_kernel,
        name="mesh_part",
        in_specs=[anywhere] * 17,
        out_specs=[anywhere] * 6,
        out_shape=[
            jax.ShapeDtypeStruct((8 * HB, D), BF16),
            jax.ShapeDtypeStruct((M_DEV, D), BF16),
            jax.ShapeDtypeStruct((3, G_DEV, D), BF16),
            jax.ShapeDtypeStruct((G_DEV, D), BF16),
            jax.ShapeDtypeStruct((3, G_DEV, 128), BF16),
            jax.ShapeDtypeStruct((2, D, D), BF16),
        ],
        scratch_shapes=[
            vmem((G_DEV, D), BF16),
            vmem((M_DEV, D), BF16),
            vmem((1, 8, GB), jnp.int32),
            vmem((1, 8, HB), jnp.int32),
            vmem((1, KL, DEVICES), jnp.int32),
            vmem((1, 2, E_G2M), jnp.int32),
            vmem((1, 2, E_MESH), jnp.int32),
            vmem((1, 2, E_MESH), jnp.int32),
            vmem((3, 1, G_DEV), jnp.int32),
            vmem((4, 2, D, D), BF16),
            vmem((4, D, D), BF16),
            vmem((4, D), F32),
            vmem((4, D), F32),
            vmem((4, 2, D, D), BF16),
            vmem((4, D, D), BF16),
            vmem((4, D), F32),
            vmem((4, D), F32),
            vmem((G_DEV + 256, D), BF16),
            vmem((8 * GB, D), BF16),
            vmem((8 * GB, D), BF16),
            vmem((E_G2M, D), BF16),
            vmem((E_G2M, 8 * GB), BF16),
            vmem((256, D), BF16),
            vmem((128, D), BF16),
            vmem((128, 128), BF16),
            vmem((DEVICES * KL, 128), BF16),
            vmem((512, D), BF16),
            vmem((8 * HB, D), BF16),
            vmem((2 * M_DEV, D), BF16),
            vmem((DEVICES, KL, D), BF16),
            vmem((DEVICES, KL, D), BF16),
            vmem((DEVICES * KL, D), BF16),
            vmem((8 * HB, D), BF16),
            vmem((8 * HB, D), BF16),
            vmem((3, G_DEV, 128), BF16),
            vmem((3, G_DEV, 256), BF16),
            vmem((3, G_DEV, D), BF16),
            vmem((M_DEV, D), F32),
            vmem((G_DEV, D), BF16),
            vmem((G_DEV, D), BF16),
            pltpu.SemaphoreType.DMA((30,)),
            pltpu.SemaphoreType.DMA((13,)),
            pltpu.SemaphoreType.DMA((24,)),
            pltpu.SemaphoreType.DMA((24,)),
            pltpu.SemaphoreType.DMA,
            pltpu.SemaphoreType.DMA((4,)),
            pltpu.SemaphoreType.REGULAR((3,)),
        ],
        compiler_params=pltpu.CompilerParams(
            collective_id=0, has_side_effects=True, vmem_limit_bytes=60 * 1024 * 1024
        ),
    )(*operands)


DEC_TILE = 512


def decode_kernel(
    owned,
    picks,
    halo,
    sums,
    gp,
    grid_rows,
    mesh_rows,
    seconds,
    node_sum,
    edge_gain,
    node_gain,
    grid_out,
    mesh_out,
    picks_v,
    halo_v,
    sums_v,
    added_v,
    total_v,
    gp_v,
    grid_v,
    mesh_v,
    second_v,
    sum_v,
    eg_v,
    ng_v,
    in_sem,
    out_sem,
):
    loads = {}

    def load(name, src, dst):
        copy = pltpu.make_async_copy(src, dst, in_sem.at[len(loads)])
        copy.start()
        loads[name] = copy

    order = [(half, k) for half in range(2) for k in range(3)]

    def rows_of(half):
        return pl.ds(half * DEC_TILE, DEC_TILE)

    load("halo", halo, halo_v)
    for half, k in order:
        here = rows_of(half)
        load(("picks", half, k), picks.at[k, here], picks_v.at[k, here])
        load(("sums", half, k), sums.at[k, here], sums_v.at[k, here])
        if half == 0 and k == 0:
            load("es", seconds.at[0], second_v.at[0])
            load("eg", edge_gain, eg_v)
    load("nf", node_sum.at[3, 1], sum_v)
    load("ns", seconds.at[1], second_v.at[1])
    load("ng", node_gain, ng_v)
    load("gp", gp, gp_v)
    load("grid", grid_rows, grid_v)
    load("mesh", mesh_rows, mesh_v)
    outs = []
    hidden, result, node, update = {}, {}, {}, {}
    starts = {5: [(0, 512)], 8: [(512, 256), (768, 256)]}

    def finish(first, count):
        here = pl.ds(first, count)
        rows = grid_v[here, :].astype(F32) + normalised(update.pop((first, count))) * ng_v[3:4, :]
        grid_v[here, :] = rows.astype(BF16)
        outs.append(
            pltpu.make_async_copy(grid_v.at[here], grid_out.at[here], out_sem.at[len(outs)])
        )
        outs[-1].start()

    loads["halo"].wait()
    for step in range(11):
        if step < 6:
            half, k = order[step]
            loads["picks", half, k].wait()
            loads["sums", half, k].wait()
            picked = dot(picks_v[k, rows_of(half), :], halo_v[...]).astype(BF16)
        if 0 <= step - 2 < 6:
            before, part = order[step - 2]
            message = normalised(result.pop(step - 2))
            if part == 0:
                added_v[...] = message
            elif part == 1:
                added_v[...] += message
            else:
                total_v[rows_of(before), :] = ((added_v[...] + message) * eg_v[3:4, :]).astype(BF16)
        if 0 <= step - 1 < 6:
            if step == 1:
                loads["es"].wait()
                loads["eg"].wait()
            result[step - 1] = dot(hidden.pop(step - 1), second_v[0])
        if step == 5:
            for name in ("nf", "ns", "ng", "gp", "grid"):
                loads[name].wait()
        pres = {}
        for block in starts.get(step, ()):
            pres[block] = (0.5 * dot(total_v[pl.ds(*block), :], sum_v[...])).astype(BF16)
        if step < 6:
            hidden[step] = silu_of_half(picked + sums_v[k, rows_of(half), :])
        for block in list(update):
            finish(*block)
        for block in list(node):
            update[block] = dot(node.pop(block), second_v[1])
        for block, pre in pres.items():
            node[block] = silu_of_half(pre + gp_v[pl.ds(*block), :])
        if step == 6:
            loads["mesh"].wait()
            slot = lax.broadcasted_iota(jnp.int32, (M_DEV, D), 0)
            mesh_v[...] = jnp.where(slot < owned[0], mesh_v[...].astype(F32), 0.0).astype(BF16)
            outs.append(pltpu.make_async_copy(mesh_v, mesh_out, out_sem.at[len(outs)]))
            outs[-1].start()
    for copy in outs:
        copy.wait()


def decode_part(*operands):
    vmem = pltpu.VMEM
    anywhere = pl.BlockSpec(memory_space=pl.ANY)
    return pl.pallas_call(
        decode_kernel,
        name="decode_part",
        in_specs=[pl.BlockSpec(memory_space=pltpu.SMEM)] + [anywhere] * 10,
        out_specs=[anywhere] * 2,
        out_shape=[
            jax.ShapeDtypeStruct((G_DEV, D), BF16),
            jax.ShapeDtypeStruct((M_DEV, D), BF16),
        ],
        scratch_shapes=[
            vmem((3, G_DEV, 128), BF16),
            vmem((8 * HB, D), BF16),
            vmem((3, G_DEV, D), BF16),
            vmem((DEC_TILE, D), F32),
            vmem((G_DEV, D), BF16),
            vmem((G_DEV, D), BF16),
            vmem((G_DEV, D), BF16),
            vmem((M_DEV, D), BF16),
            vmem((2, D, D), BF16),
            vmem((D, D), BF16),
            vmem((4, D), F32),
            vmem((4, D), F32),
            pltpu.SemaphoreType.DMA((21,)),
            pltpu.SemaphoreType.DMA((4,)),
        ],
        compiler_params=pltpu.CompilerParams(vmem_limit_bytes=60 * 1024 * 1024),
    )(*operands)


def per_device(
    grid_nodes,
    mesh_nodes,
    owned_nodes,
    grid_rim,
    mesh_rim,
    long_send,
    g2m_edges,
    short_edges,
    long_edges,
    m2g_edges,
    edge_first,
    edge_second,
    edge_bias,
    edge_gain,
    node_first,
    node_second,
    node_bias,
    node_gain,
):
    halo, mesh_three, sums, gp, picks, seconds = mesh_part(
        grid_nodes,
        mesh_nodes,
        grid_rim,
        mesh_rim,
        jnp.transpose(long_send, (0, 2, 1)),
        g2m_edges,
        short_edges,
        long_edges,
        jnp.transpose(m2g_edges, (1, 0, 2)),
        edge_first,
        edge_second,
        edge_bias,
        edge_gain,
        node_first,
        node_second,
        node_bias,
        node_gain,
    )
    grid_out, mesh_out = decode_part(
        owned_nodes,
        picks,
        halo,
        sums,
        gp,
        grid_nodes,
        mesh_three,
        seconds,
        node_first,
        edge_gain,
        node_gain,
    )
    return (grid_out, mesh_out)


def solution(mesh):
    rows = P(("aa", "ba"), None)
    lists = P(("aa", "ba"), None, None)
    in_specs = (rows, rows, P(("aa", "ba"))) + (lists,) * 7 + (P(),) * 8
    return jax.shard_map(
        per_device, mesh=mesh, in_specs=in_specs, out_specs=(rows, rows), check_vma=False
    )
```

```python
import jax
import jax.numpy as jnp
from jax import lax
from jax.experimental import pallas as pl
from jax.experimental.pallas import tpu as pltpu
from jax.sharding import PartitionSpec as P

EPSILON = 1e-05
D = 512
G_DEV = 1024
M_DEV = 192
GB = 128
HB = 16
KL = 8
CS = 16
NOWHERE = 4095
EARLY = 4
N_AA = 8
N_BA = 16
DEVICES = 128
E_G2M = 3072
E_MESH = 1536
TILE_LOCAL = 512
TILE_ENC = 768
TILE_MESH = 768
ALONG_FIRST = (-1, -1, -1, 0, 0, 1, 1, 1)
ALONG_SECOND = (-1, 0, 1, -1, 1, -1, 0, 1)
F32 = jnp.float32
BF16 = jnp.bfloat16
MESH = pl.DeviceIdType.MESH


def hops(first, second):
    steps = ((first + 1) // 2, second // 4, second % 4)
    return sum(min(step, 4 - step) for step in steps)


GROUP_ORDER = (2, 1, 3, 0)
PEERS = sorted(
    [(a, b) for a in range(N_AA) for b in range(N_BA) if (a, b) != (0, 0)],
    key=lambda peer: (GROUP_ORDER.index(peer[1] // 4), -hops(*peer)),
)


def dot(a, b):
    return jnp.dot(a, b, preferred_element_type=F32)


def silu_of_half(half):
    return half * jnp.tanh(half) + half


def centred_weights(weights):
    wide = weights.astype(F32)
    return (wide - jnp.mean(wide, axis=-1, keepdims=True)).astype(BF16)


def normalised(centred):
    spread = jnp.mean(centred * centred, axis=-1, keepdims=True)
    return centred * lax.rsqrt(spread + EPSILON)


def spread_out(row):
    parts = []
    for start in range(0, row.shape[1], 128):
        parts.append(jnp.broadcast_to(row[:, start : start + 128], (128, 128)).T.astype(BF16))
    return parts[0] if len(parts) == 1 else jnp.concatenate(parts, 0)


def columns(row):
    return spread_out((row >> 8).astype(F32)), spread_out((row & 255).astype(F32))


def lane_ids(rows):
    lane = lax.broadcasted_iota(jnp.int32, (rows, 128), 1).astype(F32)
    return lane.astype(BF16), (lane + 128.0).astype(BF16)


def one_hot(cols, first, width):
    block, place = cols
    lanes = lane_ids(place.shape[0])
    one, zero = jnp.ones((), BF16), jnp.zeros((), BF16)
    parts = []
    for start in range(first, first + width, 256):
        here = place
        if block is not None:
            here = jnp.where(block == jnp.asarray(start // 256, BF16), place, jnp.asarray(-1, BF16))
        for half in range(2):
            if start + 128 * half < first + width:
                parts.append(jnp.where(here == lanes[half], one, zero))
    return parts[0] if len(parts) == 1 else jnp.concatenate(parts, 1)


def double_one_hot(first, second, width):
    lanes = lane_ids(first[1].shape[0])
    one, zero, none = jnp.ones((), BF16), jnp.zeros((), BF16), jnp.asarray(-1, BF16)
    parts = []
    for start in range(0, width, 256):
        group = jnp.asarray(start // 256, BF16)
        one_here = jnp.where(first[0] == group, first[1], none)
        two_here = jnp.where(second[0] == group, second[1], none)
        for half in range(2):
            if start + 128 * half < width:
                found = (one_here == lanes[half]) | (two_here == lanes[half])
                parts.append(jnp.where(found, one, zero))
    return jnp.concatenate(parts, 1)


def receivers(row):
    slots = lax.broadcasted_iota(jnp.int32, (M_DEV, row.shape[1]), 0).astype(F32).astype(BF16)
    return slots == row.astype(F32).astype(BF16)


def scatter_matrix(row, values):
    spread = jnp.mean(values * values, axis=-1, keepdims=True)
    scale = lax.rsqrt(spread + EPSILON)
    parts = []
    for start in range(0, values.shape[0], 128):
        parts.append(jnp.broadcast_to(scale[start : start + 128], (128, 128)).T[0:1, :])
    scales = jnp.concatenate(parts, 1).astype(BF16)
    return jnp.where(receivers(row), scales, jnp.zeros((), BF16))


def node_update(rows, totals, first_own, first_sum, bias, second, gain):
    pre = dot(rows, first_own) + dot(totals.astype(BF16), first_sum) + bias
    result = dot(silu_of_half((0.5 * pre).astype(BF16)), second)
    result = normalised(result) * gain
    return (rows.astype(F32) + result).astype(BF16)


def mesh_kernel(
    grid_nodes,
    mesh_nodes,
    grid_rim,
    mesh_rim,
    long_send,
    g2m_edges,
    short_edges,
    long_edges,
    m2g_edges,
    edge_first,
    edge_second,
    edge_bias,
    edge_gain,
    node_first,
    node_second,
    node_bias,
    node_gain,
    dec_out,
    mesh_out,
    gq_out,
    gp_out,
    picks_out,
    second_out,
    grid_v,
    mesh_v,
    grim_v,
    mrim_v,
    send_v,
    g2m_v,
    short_v,
    long_v,
    m2g_v,
    ef_v,
    es_v,
    eb_v,
    eg_v,
    nf_v,
    ns_v,
    nb_v,
    ng_v,
    enc_table,
    enc_halo,
    enc_rim,
    partial,
    picks_v,
    proj_v,
    coarse_v,
    rim_picks,
    list_picks,
    short_table,
    short_rim,
    long_table,
    long_out,
    long_in,
    long_rows,
    dec_halo,
    dec_rim,
    dec_picks,
    dec_near,
    dec_sums,
    totals,
    gq_v,
    gp_v,
    in_sem,
    out_sem,
    halo_send,
    halo_recv,
    long_ssem,
    long_rsem,
    spread_sem,
):
    band = lax.axis_index("aa")
    sector = lax.axis_index("ba")
    me = band * N_BA + sector

    loads = {}

    def load(name, src, dst):
        copy = pltpu.make_async_copy(src, dst, in_sem.at[len(loads)])
        copy.start()
        loads[name] = copy

    def arrived(*names):
        for name in names:
            loads[name].wait()

    def at(first, second):
        return (
            lax.rem(band + (first + N_AA), N_AA),
            lax.rem(sector + (second + N_BA), N_BA),
        )

    def greet(semaphore, stride_first, stride_second, around):
        for k in around:
            pl.semaphore_signal(
                semaphore,
                inc=1,
                device_id=at(stride_first * ALONG_FIRST[k], stride_second * ALONG_SECOND[k]),
                device_id_type=MESH,
            )

    barrier = pltpu.get_barrier_semaphore()
    greet(barrier, 1, 1, range(8))

    load("grim", grid_rim, grim_v)
    load("grid", grid_nodes, grid_v)
    load("ef00", edge_first.at[0, 0], ef_v.at[0, 0])
    load("mesh", mesh_nodes, mesh_v)
    load("ef01", edge_first.at[0, 1], ef_v.at[0, 1])
    load("eb", edge_bias, eb_v)
    load("g2m", g2m_edges, g2m_v)
    def halo_copy(k, sem_base, rim, table, first, depth):
        return pltpu.make_async_remote_copy(
            src_ref=rim.at[pl.ds(k * depth, depth)],
            dst_ref=table.at[pl.ds(first + (7 - k) * depth, depth)],
            send_sem=halo_send.at[sem_base + k],
            recv_sem=halo_recv.at[sem_base + 7 - k],
            device_id=at(ALONG_FIRST[k], ALONG_SECOND[k]),
            device_id_type=MESH,
        )

    copies = []
    arrived("grim", "grid")
    for pair in ((5, 4), (7, 6, 3), (2, 1, 0)):
        cols = columns(jnp.concatenate([grim_v[0, k : k + 1, :] for k in pair], 1))
        rows = dot(one_hot(cols, 0, G_DEV), grid_v[...]).astype(BF16)
        if not copies:
            arrived("ef00")
        rows = (0.5 * dot(rows, ef_v[0, 0])).astype(BF16)
        for place, k in enumerate(pair):
            enc_rim[k * GB : (k + 1) * GB, :] = rows[place * GB : (place + 1) * GB, :]
        if not copies:
            pl.semaphore_wait(barrier, 8)
        for k in pair:
            copy = halo_copy(k, 0, enc_rim, enc_halo, 0, GB)
            copy.start()
            copies.append((k, copy))
    greet(spread_sem.at[0], 1, 1, range(8))
    load("es0", edge_second.at[0], es_v.at[0])
    load("ns0", node_second.at[0], ns_v.at[0])
    load("nf0", node_first.at[0], nf_v.at[0])
    load("eg", edge_gain, eg_v)
    load("ng", node_gain, ng_v)
    load("nb", node_bias, nb_v)
    load("mrim", mesh_rim, mrim_v)
    load("ef1", edge_first.at[1], ef_v.at[1])
    load("short", short_edges, short_v)
    load("es1", edge_second.at[1], es_v.at[1])
    load("nf1", node_first.at[1], nf_v.at[1])
    load("ns1", node_second.at[1], ns_v.at[1])
    load("send", long_send, send_v)
    load("ef2", edge_first.at[2], ef_v.at[2])
    load("long", long_edges, long_v)
    load("es2", edge_second.at[2], es_v.at[2])
    load("nf2", node_first.at[2], nf_v.at[2])
    load("ns2", node_second.at[2], ns_v.at[2])
    load("ef3", edge_first.at[3], ef_v.at[3])
    load("nf30", node_first.at[3, 0], nf_v.at[3, 0])
    load("es3", edge_second.at[3], es_v.at[3])
    load("ns3", node_second.at[3], ns_v.at[3])
    load("m2g", m2g_edges, m2g_v)

    for start in range(0, G_DEV, 512):
        half = 0.5 * dot(grid_v[start : start + 512, :], ef_v[0, 0])
        enc_table[start : start + 512, :] = half.astype(BF16)
    arrived("mesh", "ef01", "eb")
    enc_table[G_DEV : G_DEV + M_DEV, :] = (0.5 * (dot(mesh_v[...], ef_v[0, 1]) + eb_v[0:1, :])).astype(BF16)
    enc_table[G_DEV + M_DEV : G_DEV + 256, :] = jnp.zeros((64, D), BF16)
    proj_v[M_DEV:256, :] = jnp.zeros((64, D), BF16)
    coarse_v[...] = jnp.zeros((128, D), BF16)
    arrived("g2m")

    def tile_of(index):
        return pl.ds(index * TILE_LOCAL, TILE_LOCAL)

    def near_picks(index):
        here = tile_of(index)
        block, place = columns(g2m_v[0, 0:1, here])
        picks_v[here, :] = one_hot((block, place), G_DEV, 8 * GB)
        targets = columns(g2m_v[0, 1:2, here])
        return jnp.concatenate([one_hot((block, place), 0, G_DEV), one_hot(targets, 0, 256)], 1)

    tiles = E_G2M // TILE_LOCAL
    picks = near_picks(0)
    for index in range(tiles):
        sums = dot(picks, enc_table[...])
        if index + 1 < tiles:
            picks = near_picks(index + 1)
        partial[tile_of(index), :] = sums.astype(BF16)

    def centre(section):
        def block(step, carry):
            here = pl.ds(pl.multiple_of(step * 128, 128), 128)
            es_v[section, here, :] = centred_weights(es_v[section, here, :])
            ns_v[section, here, :] = centred_weights(ns_v[section, here, :])
            return carry

        lax.fori_loop(0, D // 128, block, 0)

    arrived("es0", "ns0")
    centre(0)
    arrived("mrim")
    sub = lax.broadcasted_iota(jnp.int32, (HB, HB), 0)
    lane = lax.broadcasted_iota(jnp.int32, (HB, HB), 1)
    parts = []
    for k in range(8):
        row = jnp.broadcast_to(mrim_v[0, k : k + 1, :].astype(F32), (HB, HB))
        col = jnp.sum(jnp.where(sub == lane, row, 0.0), axis=1, keepdims=True)
        parts.append(jnp.broadcast_to(col, (HB, 128)))
    rim_picks[...] = one_hot((None, jnp.concatenate(parts, 0).astype(BF16)), 0, 128)
    def rounds(section, tile, edges, count, picked):
        totals[...] = jnp.zeros((M_DEV, D), F32)
        tiles = count // tile
        hidden, result = {}, {}
        for step in range(tiles + 2):
            if step < tiles:
                half = picked(step * tile)
            if 0 <= step - 2:
                values = result.pop(step - 2)
                targets = edges[0, 1:2, (step - 2) * tile : (step - 1) * tile]
                if section == 0:
                    scatter = jnp.where(receivers(targets), jnp.ones((), BF16), jnp.zeros((), BF16))
                    message = normalised(values).astype(BF16)
                else:
                    scatter = scatter_matrix(targets, values)
                    message = values.astype(BF16)
            if 0 <= step - 1 < tiles:
                result[step - 1] = dot(hidden.pop(step - 1), es_v[section])
            if step < tiles:
                hidden[step] = silu_of_half(half)
            if 0 <= step - 2:
                totals[...] += dot(scatter, message)

    def updated(section, rows, sums):
        return node_update(
            rows,
            sums * eg_v[section : section + 1, :],
            nf_v[section, 0],
            nf_v[section, 1],
            nb_v[section : section + 1, :],
            ns_v[section],
            ng_v[section : section + 1, :],
        )

    arrived("nf0", "eg", "ng", "nb")
    pl.semaphore_wait(spread_sem.at[0], 8)
    greet(spread_sem.at[1], 2, 2, range(8))

    for k, copy in copies:
        if 7 - k < EARLY:
            copy.wait_recv()

    for index in range(tiles):
        here = tile_of(index)
        partial[here, :] += dot(picks_v[here, 0 : EARLY * GB], enc_halo[0 : EARLY * GB, :]).astype(BF16)
    for k, copy in copies:
        copy.wait_send()
        if 7 - k >= EARLY:
            copy.wait_recv()

    def enc_picked(start):
        here = pl.ds(start, TILE_ENC)
        late = dot(picks_v[here, EARLY * GB :], enc_halo[EARLY * GB :, :])
        return partial[here, :] + late.astype(BF16)

    rounds(0, TILE_ENC, g2m_v, E_G2M, enc_picked)
    mesh_v[...] = updated(0, mesh_v[...], totals[...])

    def mesh_halo(section, sem_base, rim, table, first):
        proj = (0.5 * dot(mesh_v[...], ef_v[section, 0])).astype(BF16)
        proj_v[0:M_DEV, :] = proj
        rim[...] = dot(rim_picks[...], proj_v[0:128, :]).astype(BF16)
        started = []
        for k in range(8):
            copy = halo_copy(k, sem_base, rim, table, first, HB)
            copy.start()
            started.append(copy)
        if first:
            table[0:M_DEV, :] = proj
        return started

    arrived("ef1")
    copies = mesh_halo(1, 8, short_rim, short_table, 2 * M_DEV)
    short_table[M_DEV : 2 * M_DEV, :] = (0.5 * (dot(mesh_v[...], ef_v[1, 1]) + eb_v[1:2, :])).astype(
        BF16
    )
    arrived("short")

    def short_picks(step, carry):
        here = pl.ds(pl.multiple_of(step * TILE_LOCAL, TILE_LOCAL), TILE_LOCAL)
        senders = short_v[0, 0:1, here]
        senders = columns(jnp.where(senders < M_DEV, senders, senders + M_DEV))
        targets = columns(short_v[0, 1:2, here] + M_DEV)
        picks_v[here, 0:512] = double_one_hot(senders, targets, 512)
        return carry

    lax.fori_loop(0, E_MESH // TILE_LOCAL, short_picks, 0)
    arrived("es1", "ns1", "nf1", "send")
    centre(1)
    lists = send_v[0].astype(F32).astype(BF16)
    for start in range(0, DEVICES * KL, 512):
        sub = lax.broadcasted_iota(jnp.int32, (512, DEVICES), 0) + start
        lane = lax.broadcasted_iota(jnp.int32, (512, DEVICES), 1)
        owner = jnp.where(sub // KL == lane, 1.0, 0.0).astype(BF16)
        listed = lax.dot_general(owner, lists, (((1,), (1,)), ((), ())), preferred_element_type=F32)
        sub = lax.broadcasted_iota(jnp.int32, (512, KL), 0)
        lane = lax.broadcasted_iota(jnp.int32, (512, KL), 1)
        col = jnp.sum(jnp.where(lax.rem(sub, KL) == lane, listed, 0.0), axis=1, keepdims=True)
        list_picks[start : start + 512, :] = one_hot(
            (None, jnp.broadcast_to(col, (512, 128)).astype(BF16)), 0, 128
        )
    for index in range(E_MESH // TILE_LOCAL):
        here = tile_of(index)
        partial[here, :] = dot(picks_v[here, 0:256], short_table[0:256, :]).astype(BF16)
    pl.semaphore_wait(spread_sem.at[1], 8)
    greet(spread_sem.at[2], 0, 4, (3, 4))
    for copy in copies:
        copy.wait()

    def short_picked(start):
        here = pl.ds(start, TILE_MESH)
        late = dot(picks_v[here, 256:512], short_table[256:512, :])
        return partial[here, :] + late.astype(BF16)

    rounds(1, TILE_MESH, short_v, E_MESH, short_picked)

    arrived("ef2")
    coarse = updated(1, mesh_v[0:CS, :], totals[0:CS, :])
    coarse_v[0:CS, :] = (0.5 * dot(coarse, ef_v[2, 0])).astype(BF16)
    for start in range(0, DEVICES * KL, 512):
        rows = dot(list_picks[start : start + 512, :], coarse_v[...])
        long_out[start // KL : (start + 512) // KL] = rows.reshape(512 // KL, KL, D).astype(BF16)
    pl.semaphore_wait(spread_sem.at[2], 2)
    for first, second in PEERS:
        peer_first = lax.rem(band + first, N_AA)
        peer_second = (sector // 4 + second // 4) % 4 * 4 + (sector + second) % 4
        group = -(second // 4) % 4
        slot = group * 32 + -first % N_AA * 4 + -second % 4
        pltpu.make_async_remote_copy(
            src_ref=long_out.at[peer_first * N_BA + peer_second],
            dst_ref=long_in.at[slot],
            send_sem=long_ssem,
            recv_sem=long_rsem.at[group],
            device_id=(peer_first, peer_second),
            device_id_type=MESH,
        ).start()
    long_in[0] = long_out[me]

    mesh_v[...] = updated(1, mesh_v[...], totals[...])
    long_table[0:M_DEV, :] = (0.5 * dot(mesh_v[...], ef_v[2, 0])).astype(BF16)
    long_table[M_DEV : 2 * M_DEV, :] = (0.5 * (dot(mesh_v[...], ef_v[2, 1]) + eb_v[2:3, :])).astype(BF16)
    arrived("long")

    def long_local(step, carry):
        here = pl.ds(pl.multiple_of(step * TILE_LOCAL, TILE_LOCAL), TILE_LOCAL)
        senders = long_v[0, 0:1, here]
        own = columns(jnp.where(senders < M_DEV, senders, NOWHERE))
        targets = columns(long_v[0, 1:2, here] + M_DEV)
        sums = dot(double_one_hot(own, targets, 2 * M_DEV), long_table[...])
        partial[here, :] = sums.astype(BF16)
        far = jnp.maximum(senders - M_DEV, 0)
        peer = far >> 3
        slot = (((peer >> 2) - (sector >> 2)) & 3) * 32
        slot = slot + (((peer >> 4) - band) & 7) * 4 + ((peer - sector) & 3)
        away = columns(jnp.where(senders < M_DEV, NOWHERE, slot * KL + (far & 7)))
        picks_v[here, :] = one_hot(away, 0, DEVICES * KL)
        return carry

    lax.fori_loop(0, E_MESH // TILE_LOCAL, long_local, 0)
    arrived("ef3", "nf30", "es2", "ns2", "es3", "ns3", "m2g")
    centre(2)
    for start in range(0, G_DEV, 512):
        rows = grid_v[start : start + 512, :]
        gq_v[start : start + 512, :] = (0.5 * (dot(rows, ef_v[3, 1]) + eb_v[3:4, :])).astype(BF16)
        gp_v[start : start + 512, :] = (0.5 * (dot(rows, nf_v[3, 0]) + nb_v[3:4, :])).astype(BF16)
    centre(3)
    gp_copy = pltpu.make_async_copy(gp_v, gp_out, out_sem.at[1])
    es_copy = pltpu.make_async_copy(es_v.at[3], second_out.at[0], out_sem.at[2])
    ns_copy = pltpu.make_async_copy(ns_v.at[3], second_out.at[1], out_sem.at[3])
    outs = [gp_copy, es_copy, ns_copy]

    def dec_ids(step, carry):
        here = pl.ds(pl.multiple_of(step * 512, 512), 512)
        for k in range(3):
            senders = m2g_v[k, :, here]
            dec_near[k, here, :] = one_hot(columns(senders), 0, 256)
            rims = jnp.where(senders < M_DEV, NOWHERE, senders - M_DEV)
            dec_picks[k, here, :] = one_hot(columns(rims), 0, 128)
        return carry

    lax.fori_loop(0, G_DEV // 512, dec_ids, 0)
    outs.append(pltpu.make_async_copy(dec_picks, picks_out, out_sem.at[4]))
    for copy in outs:
        copy.start()
    arrived("nf2")
    def long_arrived(group):
        first = 1 if group == 0 else group * 32
        blocks = long_in.at[pl.ds(first, (group + 1) * 32 - first)]
        pltpu.make_async_copy(blocks, blocks, long_rsem.at[group]).wait()
        rows = long_in[group * 32 : (group + 1) * 32].astype(F32).reshape(32 * KL, D)
        long_rows[group * 256 : (group + 1) * 256, :] = rows.astype(BF16)

    for group in (2, 3, 1):
        long_arrived(group)
        some = pl.ds(group * 256, 256)
        for index in range(E_MESH // TILE_LOCAL):
            here = tile_of(index)
            partial[here, :] += dot(picks_v[here, some], long_rows[some, :]).astype(BF16)
    others = pl.ds(0, DEVICES - 1)
    pltpu.make_async_copy(long_out.at[others], long_out.at[others], long_ssem).wait()
    long_arrived(0)

    def long_picked(start):
        here = pl.ds(start, TILE_MESH)
        return partial[here, :] + dot(picks_v[here, 0:256], long_rows[0:256, :]).astype(BF16)

    rounds(2, TILE_MESH, long_v, E_MESH, long_picked)
    mesh_v[...] = updated(2, mesh_v[...], totals[...])

    copies = mesh_halo(3, 16, dec_rim, dec_halo, 0)
    outs.append(pltpu.make_async_copy(mesh_v, mesh_out, out_sem.at[5]))
    outs[-1].start()
    for half in range(2):
        for k in range(3):
            here = pl.ds(half * 512, 512)
            sums = dot(dec_near[k, here, :], proj_v[...]).astype(BF16)
            dec_sums[k, here, :] = sums + gq_v[here, :]
            outs.append(
                pltpu.make_async_copy(
                    dec_sums.at[k, here], gq_out.at[k, here], out_sem.at[7 + 3 * half + k]
                )
            )
            outs[-1].start()
    for copy in copies:
        copy.wait()
    outs.append(pltpu.make_async_copy(dec_halo, dec_out, out_sem.at[6]))
    outs[-1].start()
    for copy in outs:
        copy.wait()


def mesh_part(*operands):
    vmem = pltpu.VMEM
    anywhere = pl.BlockSpec(memory_space=pl.ANY)
    return pl.pallas_call(
        mesh_kernel,
        name="mesh_part",
        in_specs=[anywhere] * 17,
        out_specs=[anywhere] * 6,
        out_shape=[
            jax.ShapeDtypeStruct((8 * HB, D), BF16),
            jax.ShapeDtypeStruct((M_DEV, D), BF16),
            jax.ShapeDtypeStruct((3, G_DEV, D), BF16),
            jax.ShapeDtypeStruct((G_DEV, D), BF16),
            jax.ShapeDtypeStruct((3, G_DEV, 128), BF16),
            jax.ShapeDtypeStruct((2, D, D), BF16),
        ],
        scratch_shapes=[
            vmem((G_DEV, D), BF16),
            vmem((M_DEV, D), BF16),
            vmem((1, 8, GB), jnp.int32),
            vmem((1, 8, HB), jnp.int32),
            vmem((1, KL, DEVICES), jnp.int32),
            vmem((1, 2, E_G2M), jnp.int32),
            vmem((1, 2, E_MESH), jnp.int32),
            vmem((1, 2, E_MESH), jnp.int32),
            vmem((3, 1, G_DEV), jnp.int32),
            vmem((4, 2, D, D), BF16),
            vmem((4, D, D), BF16),
            vmem((4, D), F32),
            vmem((4, D), F32),
            vmem((4, 2, D, D), BF16),
            vmem((4, D, D), BF16),
            vmem((4, D), F32),
            vmem((4, D), F32),
            vmem((G_DEV + 256, D), BF16),
            vmem((8 * GB, D), BF16),
            vmem((8 * GB, D), BF16),
            vmem((E_G2M, D), BF16),
            vmem((E_G2M, 8 * GB), BF16),
            vmem((256, D), BF16),
            vmem((128, D), BF16),
            vmem((128, 128), BF16),
            vmem((DEVICES * KL, 128), BF16),
            vmem((512, D), BF16),
            vmem((8 * HB, D), BF16),
            vmem((2 * M_DEV, D), BF16),
            vmem((DEVICES, KL, D), BF16),
            vmem((DEVICES, KL, D), BF16),
            vmem((DEVICES * KL, D), BF16),
            vmem((8 * HB, D), BF16),
            vmem((8 * HB, D), BF16),
            vmem((3, G_DEV, 128), BF16),
            vmem((3, G_DEV, 256), BF16),
            vmem((3, G_DEV, D), BF16),
            vmem((M_DEV, D), F32),
            vmem((G_DEV, D), BF16),
            vmem((G_DEV, D), BF16),
            pltpu.SemaphoreType.DMA((30,)),
            pltpu.SemaphoreType.DMA((13,)),
            pltpu.SemaphoreType.DMA((24,)),
            pltpu.SemaphoreType.DMA((24,)),
            pltpu.SemaphoreType.DMA,
            pltpu.SemaphoreType.DMA((4,)),
            pltpu.SemaphoreType.REGULAR((3,)),
        ],
        compiler_params=pltpu.CompilerParams(
            collective_id=0, has_side_effects=True, vmem_limit_bytes=60 * 1024 * 1024
        ),
    )(*operands)


DEC_TILE = 512


def decode_kernel(
    owned,
    picks,
    halo,
    sums,
    gp,
    grid_rows,
    mesh_rows,
    seconds,
    node_sum,
    edge_gain,
    node_gain,
    grid_out,
    mesh_out,
    picks_v,
    halo_v,
    sums_v,
    added_v,
    total_v,
    gp_v,
    grid_v,
    mesh_v,
    second_v,
    sum_v,
    eg_v,
    ng_v,
    in_sem,
    out_sem,
):
    loads = {}

    def load(name, src, dst):
        copy = pltpu.make_async_copy(src, dst, in_sem.at[len(loads)])
        copy.start()
        loads[name] = copy

    order = [(half, k) for half in range(2) for k in range(3)]

    def rows_of(half):
        return pl.ds(half * DEC_TILE, DEC_TILE)

    load("halo", halo, halo_v)
    for half, k in order:
        here = rows_of(half)
        load(("picks", half, k), picks.at[k, here], picks_v.at[k, here])
        load(("sums", half, k), sums.at[k, here], sums_v.at[k, here])
        if half == 0 and k == 0:
            load("es", seconds.at[0], second_v.at[0])
            load("eg", edge_gain, eg_v)
    load("nf", node_sum.at[3, 1], sum_v)
    load("ns", seconds.at[1], second_v.at[1])
    load("ng", node_gain, ng_v)
    load("gp", gp, gp_v)
    load("grid", grid_rows, grid_v)
    load("mesh", mesh_rows, mesh_v)
    outs = []
    hidden, result, node, update = {}, {}, {}, {}
    starts = {5: [(0, 512)], 8: [(512, 256), (768, 256)]}

    def finish(first, count):
        here = pl.ds(first, count)
        rows = grid_v[here, :].astype(F32) + normalised(update.pop((first, count))) * ng_v[3:4, :]
        grid_v[here, :] = rows.astype(BF16)
        outs.append(
            pltpu.make_async_copy(grid_v.at[here], grid_out.at[here], out_sem.at[len(outs)])
        )
        outs[-1].start()

    def half_sums(step):
        half, k = order[step]
        loads["picks", half, k].wait()
        loads["sums", half, k].wait()
        picked = dot(picks_v[k, rows_of(half), :], halo_v[...]).astype(BF16)
        return silu_of_half(picked + sums_v[k, rows_of(half), :])

    loads["halo"].wait()
    count = len(order)
    for step in range(count + 5):
        if step < count:
            hidden[step] = half_sums(step)
        if step == 1:
            loads["es"].wait()
            loads["eg"].wait()
        if 0 <= step - 1 < count:
            result[step - 1] = dot(hidden.pop(step - 1), second_v[0])
        if 0 <= step - 2 < count:
            before, part = order[step - 2]
            message = normalised(result.pop(step - 2))
            if part == 0:
                added_v[...] = message
            elif part == 1:
                added_v[...] += message
            else:
                total_v[rows_of(before), :] = ((added_v[...] + message) * eg_v[3:4, :]).astype(BF16)
        if step == 5:
            for name in ("nf", "ns", "ng", "gp", "grid"):
                loads[name].wait()
        pres = {}
        for block in starts.get(step, ()):
            pres[block] = (0.5 * dot(total_v[pl.ds(*block), :], sum_v[...])).astype(BF16)
        for block in list(update):
            finish(*block)
        for block in list(node):
            update[block] = dot(node.pop(block), second_v[1])
        for block, pre in pres.items():
            node[block] = silu_of_half(pre + gp_v[pl.ds(*block), :])
        if step == 6:
            loads["mesh"].wait()
            slot = lax.broadcasted_iota(jnp.int32, (M_DEV, D), 0)
            mesh_v[...] = jnp.where(slot < owned[0], mesh_v[...].astype(F32), 0.0).astype(BF16)
            outs.append(pltpu.make_async_copy(mesh_v, mesh_out, out_sem.at[len(outs)]))
            outs[-1].start()
    for copy in outs:
        copy.wait()


def decode_part(*operands):
    vmem = pltpu.VMEM
    anywhere = pl.BlockSpec(memory_space=pl.ANY)
    return pl.pallas_call(
        decode_kernel,
        name="decode_part",
        in_specs=[pl.BlockSpec(memory_space=pltpu.SMEM)] + [anywhere] * 10,
        out_specs=[anywhere] * 2,
        out_shape=[
            jax.ShapeDtypeStruct((G_DEV, D), BF16),
            jax.ShapeDtypeStruct((M_DEV, D), BF16),
        ],
        scratch_shapes=[
            vmem((3, G_DEV, 128), BF16),
            vmem((8 * HB, D), BF16),
            vmem((3, G_DEV, D), BF16),
            vmem((DEC_TILE, D), F32),
            vmem((G_DEV, D), BF16),
            vmem((G_DEV, D), BF16),
            vmem((G_DEV, D), BF16),
            vmem((M_DEV, D), BF16),
            vmem((2, D, D), BF16),
            vmem((D, D), BF16),
            vmem((4, D), F32),
            vmem((4, D), F32),
            pltpu.SemaphoreType.DMA((21,)),
            pltpu.SemaphoreType.DMA((4,)),
        ],
        compiler_params=pltpu.CompilerParams(vmem_limit_bytes=60 * 1024 * 1024),
    )(*operands)


def per_device(
    grid_nodes,
    mesh_nodes,
    owned_nodes,
    grid_rim,
    mesh_rim,
    long_send,
    g2m_edges,
    short_edges,
    long_edges,
    m2g_edges,
    edge_first,
    edge_second,
    edge_bias,
    edge_gain,
    node_first,
    node_second,
    node_bias,
    node_gain,
):
    halo, mesh_three, sums, gp, picks, seconds = mesh_part(
        grid_nodes,
        mesh_nodes,
        grid_rim,
        mesh_rim,
        jnp.transpose(long_send, (0, 2, 1)),
        g2m_edges,
        short_edges,
        long_edges,
        jnp.transpose(m2g_edges, (1, 0, 2)),
        edge_first,
        edge_second,
        edge_bias,
        edge_gain,
        node_first,
        node_second,
        node_bias,
        node_gain,
    )
    grid_out, mesh_out = decode_part(
        owned_nodes,
        picks,
        halo,
        sums,
        gp,
        grid_nodes,
        mesh_three,
        seconds,
        node_first,
        edge_gain,
        node_gain,
    )
    return (grid_out, mesh_out)


def solution(mesh):
    rows = P(("aa", "ba"), None)
    lists = P(("aa", "ba"), None, None)
    in_specs = (rows, rows, P(("aa", "ba"))) + (lists,) * 7 + (P(),) * 8
    return jax.shard_map(
        per_device, mesh=mesh, in_specs=in_specs, out_specs=(rows, rows), check_vma=False
    )
```

```python
import jax
import jax.numpy as jnp
from jax import lax
from jax.experimental import pallas as pl
from jax.experimental.pallas import tpu as pltpu
from jax.sharding import PartitionSpec as P

EPSILON = 1e-05
D = 512
G_DEV = 1024
M_DEV = 192
GB = 128
HB = 16
KL = 8
CS = 16
NOWHERE = 4095
EARLY = 4
N_AA = 8
N_BA = 16
DEVICES = 128
E_G2M = 3072
E_MESH = 1536
TILE_LOCAL = 512
TILE_ENC = 768
TILE_MESH = 768
ALONG_FIRST = (-1, -1, -1, 0, 0, 1, 1, 1)
ALONG_SECOND = (-1, 0, 1, -1, 1, -1, 0, 1)
F32 = jnp.float32
BF16 = jnp.bfloat16
MESH = pl.DeviceIdType.MESH


def hops(first, second):
    steps = ((first + 1) // 2, second // 4, second % 4)
    return sum(min(step, 4 - step) for step in steps)


GROUP_ORDER = (2, 1, 3, 0)
PEERS = sorted(
    [(a, b) for a in range(N_AA) for b in range(N_BA) if (a, b) != (0, 0)],
    key=lambda peer: (GROUP_ORDER.index(peer[1] // 4), -hops(*peer)),
)


def dot(a, b):
    return jnp.dot(a, b, preferred_element_type=F32)


def silu_of_half(half):
    return half * jnp.tanh(half) + half


def centred_weights(weights):
    wide = weights.astype(F32)
    return (wide - jnp.mean(wide, axis=-1, keepdims=True)).astype(BF16)


def normalised(centred):
    spread = jnp.mean(centred * centred, axis=-1, keepdims=True)
    return centred * lax.rsqrt(spread + EPSILON)


def normalised_bf16(centred):
    spread = jnp.mean(centred * centred, axis=-1, keepdims=True)
    return centred.astype(BF16) * lax.rsqrt(spread + EPSILON).astype(BF16)


def spread_out(row):
    parts = []
    for start in range(0, row.shape[1], 128):
        parts.append(jnp.broadcast_to(row[:, start : start + 128], (128, 128)).T.astype(BF16))
    return parts[0] if len(parts) == 1 else jnp.concatenate(parts, 0)


def columns(row):
    return spread_out((row >> 8).astype(F32)), spread_out((row & 255).astype(F32))


def lane_ids(rows):
    lane = lax.broadcasted_iota(jnp.int32, (rows, 128), 1).astype(F32)
    return lane.astype(BF16), (lane + 128.0).astype(BF16)


def one_hot(cols, first, width):
    block, place = cols
    lanes = lane_ids(place.shape[0])
    one, zero = jnp.ones((), BF16), jnp.zeros((), BF16)
    parts = []
    for start in range(first, first + width, 256):
        here = place
        if block is not None:
            here = jnp.where(block == jnp.asarray(start // 256, BF16), place, jnp.asarray(-1, BF16))
        for half in range(2):
            if start + 128 * half < first + width:
                parts.append(jnp.where(here == lanes[half], one, zero))
    return parts[0] if len(parts) == 1 else jnp.concatenate(parts, 1)


def double_one_hot(first, second, width):
    lanes = lane_ids(first[1].shape[0])
    one, zero, none = jnp.ones((), BF16), jnp.zeros((), BF16), jnp.asarray(-1, BF16)
    parts = []
    for start in range(0, width, 256):
        group = jnp.asarray(start // 256, BF16)
        one_here = jnp.where(first[0] == group, first[1], none)
        two_here = jnp.where(second[0] == group, second[1], none)
        for half in range(2):
            if start + 128 * half < width:
                found = (one_here == lanes[half]) | (two_here == lanes[half])
                parts.append(jnp.where(found, one, zero))
    return jnp.concatenate(parts, 1)


def receivers(row):
    slots = lax.broadcasted_iota(jnp.int32, (M_DEV, row.shape[1]), 0).astype(F32).astype(BF16)
    return slots == row.astype(F32).astype(BF16)


def node_update(rows, totals, first_own, first_sum, bias, second, gain):
    pre = dot(rows, first_own) + dot(totals.astype(BF16), first_sum) + bias
    result = dot(silu_of_half((0.5 * pre).astype(BF16)), second)
    result = normalised(result) * gain
    return (rows.astype(F32) + result).astype(BF16)


def mesh_kernel(
    grid_nodes,
    mesh_nodes,
    grid_rim,
    mesh_rim,
    long_send,
    g2m_edges,
    short_edges,
    long_edges,
    m2g_edges,
    edge_first,
    edge_second,
    edge_bias,
    edge_gain,
    node_first,
    node_second,
    node_bias,
    node_gain,
    dec_out,
    mesh_out,
    gq_out,
    gp_out,
    picks_out,
    second_out,
    grid_v,
    mesh_v,
    grim_v,
    mrim_v,
    send_v,
    g2m_v,
    short_v,
    long_v,
    m2g_v,
    ef_v,
    es_v,
    eb_v,
    eg_v,
    nf_v,
    ns_v,
    nb_v,
    ng_v,
    enc_table,
    enc_halo,
    enc_rim,
    partial,
    picks_v,
    proj_v,
    coarse_v,
    rim_picks,
    list_picks,
    short_table,
    short_rim,
    long_table,
    long_out,
    long_in,
    long_rows,
    dec_halo,
    dec_rim,
    dec_picks,
    dec_near,
    dec_sums,
    totals,
    gq_v,
    gp_v,
    in_sem,
    out_sem,
    halo_send,
    halo_recv,
    long_ssem,
    long_rsem,
    spread_sem,
):
    band = lax.axis_index("aa")
    sector = lax.axis_index("ba")
    me = band * N_BA + sector

    loads = {}

    def load(name, src, dst):
        copy = pltpu.make_async_copy(src, dst, in_sem.at[len(loads)])
        copy.start()
        loads[name] = copy

    def arrived(*names):
        for name in names:
            loads[name].wait()

    def at(first, second):
        return (
            lax.rem(band + (first + N_AA), N_AA),
            lax.rem(sector + (second + N_BA), N_BA),
        )

    def greet(semaphore, stride_first, stride_second, around):
        for k in around:
            pl.semaphore_signal(
                semaphore,
                inc=1,
                device_id=at(stride_first * ALONG_FIRST[k], stride_second * ALONG_SECOND[k]),
                device_id_type=MESH,
            )

    barrier = pltpu.get_barrier_semaphore()
    greet(barrier, 1, 1, range(8))

    load("grim", grid_rim, grim_v)
    load("grid", grid_nodes, grid_v)
    load("ef00", edge_first.at[0, 0], ef_v.at[0, 0])
    load("mesh", mesh_nodes, mesh_v)
    load("ef01", edge_first.at[0, 1], ef_v.at[0, 1])
    load("eb", edge_bias, eb_v)
    load("g2m", g2m_edges, g2m_v)
    def halo_copy(k, sem_base, rim, table, first, depth):
        return pltpu.make_async_remote_copy(
            src_ref=rim.at[pl.ds(k * depth, depth)],
            dst_ref=table.at[pl.ds(first + (7 - k) * depth, depth)],
            send_sem=halo_send.at[sem_base + k],
            recv_sem=halo_recv.at[sem_base + 7 - k],
            device_id=at(ALONG_FIRST[k], ALONG_SECOND[k]),
            device_id_type=MESH,
        )

    copies = []
    arrived("grim", "grid")
    for pair in ((5, 4), (7, 6, 3), (2, 1, 0)):
        cols = columns(jnp.concatenate([grim_v[0, k : k + 1, :] for k in pair], 1))
        rows = dot(one_hot(cols, 0, G_DEV), grid_v[...]).astype(BF16)
        if not copies:
            arrived("ef00")
        rows = (0.5 * dot(rows, ef_v[0, 0])).astype(BF16)
        for place, k in enumerate(pair):
            enc_rim[k * GB : (k + 1) * GB, :] = rows[place * GB : (place + 1) * GB, :]
        if not copies:
            pl.semaphore_wait(barrier, 8)
        for k in pair:
            copy = halo_copy(k, 0, enc_rim, enc_halo, 0, GB)
            copy.start()
            copies.append((k, copy))
    greet(spread_sem.at[0], 1, 1, range(8))
    load("es0", edge_second.at[0], es_v.at[0])
    load("ns0", node_second.at[0], ns_v.at[0])
    load("nf0", node_first.at[0], nf_v.at[0])
    load("eg", edge_gain, eg_v)
    load("ng", node_gain, ng_v)
    load("nb", node_bias, nb_v)
    load("mrim", mesh_rim, mrim_v)
    load("ef1", edge_first.at[1], ef_v.at[1])
    load("short", short_edges, short_v)
    load("es1", edge_second.at[1], es_v.at[1])
    load("nf1", node_first.at[1], nf_v.at[1])
    load("ns1", node_second.at[1], ns_v.at[1])
    load("send", long_send, send_v)
    load("ef2", edge_first.at[2], ef_v.at[2])
    load("long", long_edges, long_v)
    load("es2", edge_second.at[2], es_v.at[2])
    load("nf2", node_first.at[2], nf_v.at[2])
    load("ns2", node_second.at[2], ns_v.at[2])
    load("ef3", edge_first.at[3], ef_v.at[3])
    load("nf30", node_first.at[3, 0], nf_v.at[3, 0])
    load("es3", edge_second.at[3], es_v.at[3])
    load("ns3", node_second.at[3], ns_v.at[3])
    load("m2g", m2g_edges, m2g_v)

    for start in range(0, G_DEV, 512):
        half = 0.5 * dot(grid_v[start : start + 512, :], ef_v[0, 0])
        enc_table[start : start + 512, :] = half.astype(BF16)
    arrived("mesh", "ef01", "eb")
    enc_table[G_DEV : G_DEV + M_DEV, :] = (0.5 * (dot(mesh_v[...], ef_v[0, 1]) + eb_v[0:1, :])).astype(BF16)
    enc_table[G_DEV + M_DEV : G_DEV + 256, :] = jnp.zeros((64, D), BF16)
    proj_v[M_DEV:256, :] = jnp.zeros((64, D), BF16)
    coarse_v[...] = jnp.zeros((128, D), BF16)
    arrived("g2m")

    def tile_of(index):
        return pl.ds(index * TILE_LOCAL, TILE_LOCAL)

    def near_picks(index):
        here = tile_of(index)
        block, place = columns(g2m_v[0, 0:1, here])
        picks_v[here, :] = one_hot((block, place), G_DEV, 8 * GB)
        targets = columns(g2m_v[0, 1:2, here])
        return jnp.concatenate([one_hot((block, place), 0, G_DEV), one_hot(targets, 0, 256)], 1)

    tiles = E_G2M // TILE_LOCAL
    picks = near_picks(0)
    for index in range(tiles):
        sums = dot(picks, enc_table[...])
        if index + 1 < tiles:
            picks = near_picks(index + 1)
        partial[tile_of(index), :] = sums.astype(BF16)

    def centre(section):
        def block(step, carry):
            here = pl.ds(pl.multiple_of(step * 128, 128), 128)
            es_v[section, here, :] = centred_weights(es_v[section, here, :])
            ns_v[section, here, :] = centred_weights(ns_v[section, here, :])
            return carry

        lax.fori_loop(0, D // 128, block, 0)

    arrived("es0", "ns0")
    centre(0)
    arrived("mrim")
    sub = lax.broadcasted_iota(jnp.int32, (HB, HB), 0)
    lane = lax.broadcasted_iota(jnp.int32, (HB, HB), 1)
    parts = []
    for k in range(8):
        row = jnp.broadcast_to(mrim_v[0, k : k + 1, :].astype(F32), (HB, HB))
        col = jnp.sum(jnp.where(sub == lane, row, 0.0), axis=1, keepdims=True)
        parts.append(jnp.broadcast_to(col, (HB, 128)))
    rim_picks[...] = one_hot((None, jnp.concatenate(parts, 0).astype(BF16)), 0, 128)
    def rounds(section, tile, edges, count, picked):
        totals[...] = jnp.zeros((M_DEV, D), F32)
        tiles = count // tile
        hidden, result = {}, {}
        for step in range(tiles + 2):
            if step < tiles:
                half = picked(step * tile)
            if 0 <= step - 2:
                values = result.pop(step - 2)
                targets = edges[0, 1:2, (step - 2) * tile : (step - 1) * tile]
                scatter = jnp.where(receivers(targets), jnp.ones((), BF16), jnp.zeros((), BF16))
                if section == 0:
                    message = normalised(values).astype(BF16)
                else:
                    message = normalised_bf16(values)
            if 0 <= step - 1 < tiles:
                result[step - 1] = dot(hidden.pop(step - 1), es_v[section])
            if step < tiles:
                hidden[step] = silu_of_half(half)
            if 0 <= step - 2:
                totals[...] += dot(scatter, message)

    def updated(section, rows, sums):
        return node_update(
            rows,
            sums * eg_v[section : section + 1, :],
            nf_v[section, 0],
            nf_v[section, 1],
            nb_v[section : section + 1, :],
            ns_v[section],
            ng_v[section : section + 1, :],
        )

    arrived("nf0", "eg", "ng", "nb")
    pl.semaphore_wait(spread_sem.at[0], 8)
    greet(spread_sem.at[1], 2, 2, range(8))

    for k, copy in copies:
        if 7 - k < EARLY:
            copy.wait_recv()

    for index in range(tiles):
        here = tile_of(index)
        partial[here, :] += dot(picks_v[here, 0 : EARLY * GB], enc_halo[0 : EARLY * GB, :]).astype(BF16)
    for k, copy in copies:
        copy.wait_send()
        if 7 - k >= EARLY:
            copy.wait_recv()

    def enc_picked(start):
        here = pl.ds(start, TILE_ENC)
        late = dot(picks_v[here, EARLY * GB :], enc_halo[EARLY * GB :, :])
        return partial[here, :] + late.astype(BF16)

    rounds(0, TILE_ENC, g2m_v, E_G2M, enc_picked)
    mesh_v[...] = updated(0, mesh_v[...], totals[...])

    def mesh_halo(section, sem_base, rim, table, first):
        proj = (0.5 * dot(mesh_v[...], ef_v[section, 0])).astype(BF16)
        proj_v[0:M_DEV, :] = proj
        rim[...] = dot(rim_picks[...], proj_v[0:128, :]).astype(BF16)
        started = []
        for k in range(8):
            copy = halo_copy(k, sem_base, rim, table, first, HB)
            copy.start()
            started.append(copy)
        if first:
            table[0:M_DEV, :] = proj
        return started

    arrived("ef1")
    copies = mesh_halo(1, 8, short_rim, short_table, 2 * M_DEV)
    short_table[M_DEV : 2 * M_DEV, :] = (0.5 * (dot(mesh_v[...], ef_v[1, 1]) + eb_v[1:2, :])).astype(
        BF16
    )
    arrived("short")

    def short_picks(step, carry):
        here = pl.ds(pl.multiple_of(step * TILE_LOCAL, TILE_LOCAL), TILE_LOCAL)
        senders = short_v[0, 0:1, here]
        senders = columns(jnp.where(senders < M_DEV, senders, senders + M_DEV))
        targets = columns(short_v[0, 1:2, here] + M_DEV)
        picks_v[here, 0:512] = double_one_hot(senders, targets, 512)
        return carry

    lax.fori_loop(0, E_MESH // TILE_LOCAL, short_picks, 0)
    arrived("es1", "ns1", "nf1", "send")
    centre(1)
    lists = send_v[0].astype(F32).astype(BF16)
    for start in range(0, DEVICES * KL, 512):
        sub = lax.broadcasted_iota(jnp.int32, (512, DEVICES), 0) + start
        lane = lax.broadcasted_iota(jnp.int32, (512, DEVICES), 1)
        owner = jnp.where(sub // KL == lane, 1.0, 0.0).astype(BF16)
        listed = lax.dot_general(owner, lists, (((1,), (1,)), ((), ())), preferred_element_type=F32)
        sub = lax.broadcasted_iota(jnp.int32, (512, KL), 0)
        lane = lax.broadcasted_iota(jnp.int32, (512, KL), 1)
        col = jnp.sum(jnp.where(lax.rem(sub, KL) == lane, listed, 0.0), axis=1, keepdims=True)
        list_picks[start : start + 512, :] = one_hot(
            (None, jnp.broadcast_to(col, (512, 128)).astype(BF16)), 0, 128
        )
    for index in range(E_MESH // TILE_LOCAL):
        here = tile_of(index)
        partial[here, :] = dot(picks_v[here, 0:256], short_table[0:256, :]).astype(BF16)
    pl.semaphore_wait(spread_sem.at[1], 8)
    greet(spread_sem.at[2], 0, 4, (3, 4))
    for copy in copies:
        copy.wait()

    def short_picked(start):
        here = pl.ds(start, TILE_MESH)
        late = dot(picks_v[here, 256:512], short_table[256:512, :])
        return partial[here, :] + late.astype(BF16)

    rounds(1, TILE_MESH, short_v, E_MESH, short_picked)

    arrived("ef2")
    coarse = updated(1, mesh_v[0:CS, :], totals[0:CS, :])
    coarse_v[0:CS, :] = (0.5 * dot(coarse, ef_v[2, 0])).astype(BF16)
    for start in range(0, DEVICES * KL, 512):
        rows = dot(list_picks[start : start + 512, :], coarse_v[...])
        long_out[start // KL : (start + 512) // KL] = rows.reshape(512 // KL, KL, D).astype(BF16)
    pl.semaphore_wait(spread_sem.at[2], 2)
    for first, second in PEERS:
        peer_first = lax.rem(band + first, N_AA)
        peer_second = (sector // 4 + second // 4) % 4 * 4 + (sector + second) % 4
        group = -(second // 4) % 4
        slot = group * 32 + -first % N_AA * 4 + -second % 4
        pltpu.make_async_remote_copy(
            src_ref=long_out.at[peer_first * N_BA + peer_second],
            dst_ref=long_in.at[slot],
            send_sem=long_ssem,
            recv_sem=long_rsem.at[group],
            device_id=(peer_first, peer_second),
            device_id_type=MESH,
        ).start()
    long_in[0] = long_out[me]

    mesh_v[...] = updated(1, mesh_v[...], totals[...])
    long_table[0:M_DEV, :] = (0.5 * dot(mesh_v[...], ef_v[2, 0])).astype(BF16)
    long_table[M_DEV : 2 * M_DEV, :] = (0.5 * (dot(mesh_v[...], ef_v[2, 1]) + eb_v[2:3, :])).astype(BF16)
    arrived("long")

    def long_local(step, carry):
        here = pl.ds(pl.multiple_of(step * TILE_LOCAL, TILE_LOCAL), TILE_LOCAL)
        senders = long_v[0, 0:1, here]
        own = columns(jnp.where(senders < M_DEV, senders, NOWHERE))
        targets = columns(long_v[0, 1:2, here] + M_DEV)
        sums = dot(double_one_hot(own, targets, 2 * M_DEV), long_table[...])
        partial[here, :] = sums.astype(BF16)
        far = jnp.maximum(senders - M_DEV, 0)
        peer = far >> 3
        slot = (((peer >> 2) - (sector >> 2)) & 3) * 32
        slot = slot + (((peer >> 4) - band) & 7) * 4 + ((peer - sector) & 3)
        away = columns(jnp.where(senders < M_DEV, NOWHERE, slot * KL + (far & 7)))
        picks_v[here, :] = one_hot(away, 0, DEVICES * KL)
        return carry

    lax.fori_loop(0, E_MESH // TILE_LOCAL, long_local, 0)
    arrived("ef3", "nf30", "es2", "ns2", "es3", "ns3", "m2g")
    centre(2)
    for start in range(0, G_DEV, 512):
        rows = grid_v[start : start + 512, :]
        gq_v[start : start + 512, :] = (0.5 * (dot(rows, ef_v[3, 1]) + eb_v[3:4, :])).astype(BF16)
        gp_v[start : start + 512, :] = (0.5 * (dot(rows, nf_v[3, 0]) + nb_v[3:4, :])).astype(BF16)
    centre(3)
    gp_copy = pltpu.make_async_copy(gp_v, gp_out, out_sem.at[1])
    es_copy = pltpu.make_async_copy(es_v.at[3], second_out.at[0], out_sem.at[2])
    ns_copy = pltpu.make_async_copy(ns_v.at[3], second_out.at[1], out_sem.at[3])
    outs = [gp_copy, es_copy, ns_copy]

    def dec_ids(step, carry):
        here = pl.ds(pl.multiple_of(step * 512, 512), 512)
        for k in range(3):
            senders = m2g_v[k, :, here]
            dec_near[k, here, :] = one_hot(columns(senders), 0, 256)
            rims = jnp.where(senders < M_DEV, NOWHERE, senders - M_DEV)
            dec_picks[k, here, :] = one_hot(columns(rims), 0, 128)
        return carry

    lax.fori_loop(0, G_DEV // 512, dec_ids, 0)
    outs.append(pltpu.make_async_copy(dec_picks, picks_out, out_sem.at[4]))
    for copy in outs:
        copy.start()
    arrived("nf2")
    def long_arrived(group):
        first = 1 if group == 0 else group * 32
        blocks = long_in.at[pl.ds(first, (group + 1) * 32 - first)]
        pltpu.make_async_copy(blocks, blocks, long_rsem.at[group]).wait()
        rows = long_in[group * 32 : (group + 1) * 32].astype(F32).reshape(32 * KL, D)
        long_rows[group * 256 : (group + 1) * 256, :] = rows.astype(BF16)

    for group in (2, 3, 1):
        long_arrived(group)
        some = pl.ds(group * 256, 256)
        for index in range(E_MESH // TILE_LOCAL):
            here = tile_of(index)
            partial[here, :] += dot(picks_v[here, some], long_rows[some, :]).astype(BF16)
    others = pl.ds(0, DEVICES - 1)
    pltpu.make_async_copy(long_out.at[others], long_out.at[others], long_ssem).wait()
    long_arrived(0)

    def long_picked(start):
        here = pl.ds(start, TILE_MESH)
        return partial[here, :] + dot(picks_v[here, 0:256], long_rows[0:256, :]).astype(BF16)

    rounds(2, TILE_MESH, long_v, E_MESH, long_picked)
    mesh_v[...] = updated(2, mesh_v[...], totals[...])

    copies = mesh_halo(3, 16, dec_rim, dec_halo, 0)
    outs.append(pltpu.make_async_copy(mesh_v, mesh_out, out_sem.at[5]))
    outs[-1].start()
    for half in range(2):
        for k in range(3):
            here = pl.ds(half * 512, 512)
            sums = dot(dec_near[k, here, :], proj_v[...]).astype(BF16)
            dec_sums[k, here, :] = sums + gq_v[here, :]
            outs.append(
                pltpu.make_async_copy(
                    dec_sums.at[k, here], gq_out.at[k, here], out_sem.at[7 + 3 * half + k]
                )
            )
            outs[-1].start()
    for copy in copies:
        copy.wait()
    outs.append(pltpu.make_async_copy(dec_halo, dec_out, out_sem.at[6]))
    outs[-1].start()
    for copy in outs:
        copy.wait()


def mesh_part(*operands):
    vmem = pltpu.VMEM
    anywhere = pl.BlockSpec(memory_space=pl.ANY)
    return pl.pallas_call(
        mesh_kernel,
        name="mesh_part",
        in_specs=[anywhere] * 17,
        out_specs=[anywhere] * 6,
        out_shape=[
            jax.ShapeDtypeStruct((8 * HB, D), BF16),
            jax.ShapeDtypeStruct((M_DEV, D), BF16),
            jax.ShapeDtypeStruct((3, G_DEV, D), BF16),
            jax.ShapeDtypeStruct((G_DEV, D), BF16),
            jax.ShapeDtypeStruct((3, G_DEV, 128), BF16),
            jax.ShapeDtypeStruct((2, D, D), BF16),
        ],
        scratch_shapes=[
            vmem((G_DEV, D), BF16),
            vmem((M_DEV, D), BF16),
            vmem((1, 8, GB), jnp.int32),
            vmem((1, 8, HB), jnp.int32),
            vmem((1, KL, DEVICES), jnp.int32),
            vmem((1, 2, E_G2M), jnp.int32),
            vmem((1, 2, E_MESH), jnp.int32),
            vmem((1, 2, E_MESH), jnp.int32),
            vmem((3, 1, G_DEV), jnp.int32),
            vmem((4, 2, D, D), BF16),
            vmem((4, D, D), BF16),
            vmem((4, D), F32),
            vmem((4, D), F32),
            vmem((4, 2, D, D), BF16),
            vmem((4, D, D), BF16),
            vmem((4, D), F32),
            vmem((4, D), F32),
            vmem((G_DEV + 256, D), BF16),
            vmem((8 * GB, D), BF16),
            vmem((8 * GB, D), BF16),
            vmem((E_G2M, D), BF16),
            vmem((E_G2M, 8 * GB), BF16),
            vmem((256, D), BF16),
            vmem((128, D), BF16),
            vmem((128, 128), BF16),
            vmem((DEVICES * KL, 128), BF16),
            vmem((512, D), BF16),
            vmem((8 * HB, D), BF16),
            vmem((2 * M_DEV, D), BF16),
            vmem((DEVICES, KL, D), BF16),
            vmem((DEVICES, KL, D), BF16),
            vmem((DEVICES * KL, D), BF16),
            vmem((8 * HB, D), BF16),
            vmem((8 * HB, D), BF16),
            vmem((3, G_DEV, 128), BF16),
            vmem((3, G_DEV, 256), BF16),
            vmem((3, G_DEV, D), BF16),
            vmem((M_DEV, D), F32),
            vmem((G_DEV, D), BF16),
            vmem((G_DEV, D), BF16),
            pltpu.SemaphoreType.DMA((30,)),
            pltpu.SemaphoreType.DMA((13,)),
            pltpu.SemaphoreType.DMA((24,)),
            pltpu.SemaphoreType.DMA((24,)),
            pltpu.SemaphoreType.DMA,
            pltpu.SemaphoreType.DMA((4,)),
            pltpu.SemaphoreType.REGULAR((3,)),
        ],
        compiler_params=pltpu.CompilerParams(
            collective_id=0, has_side_effects=True, vmem_limit_bytes=60 * 1024 * 1024
        ),
    )(*operands)


DEC_TILE = 512


def decode_kernel(
    owned,
    picks,
    halo,
    sums,
    gp,
    grid_rows,
    mesh_rows,
    seconds,
    node_sum,
    edge_gain,
    node_gain,
    grid_out,
    mesh_out,
    picks_v,
    halo_v,
    sums_v,
    added_v,
    total_v,
    gp_v,
    grid_v,
    mesh_v,
    second_v,
    sum_v,
    eg_v,
    ng_v,
    in_sem,
    out_sem,
):
    loads = {}

    def load(name, src, dst):
        copy = pltpu.make_async_copy(src, dst, in_sem.at[len(loads)])
        copy.start()
        loads[name] = copy

    order = [(half, k) for half in range(2) for k in range(3)]

    def rows_of(half):
        return pl.ds(half * DEC_TILE, DEC_TILE)

    load("halo", halo, halo_v)
    for half, k in order:
        here = rows_of(half)
        load(("picks", half, k), picks.at[k, here], picks_v.at[k, here])
        load(("sums", half, k), sums.at[k, here], sums_v.at[k, here])
        if half == 0 and k == 0:
            load("es", seconds.at[0], second_v.at[0])
            load("eg", edge_gain, eg_v)
    load("nf", node_sum.at[3, 1], sum_v)
    load("ns", seconds.at[1], second_v.at[1])
    load("ng", node_gain, ng_v)
    load("gp", gp, gp_v)
    load("grid", grid_rows, grid_v)
    load("mesh", mesh_rows, mesh_v)
    outs = []
    hidden, result, node, update = {}, {}, {}, {}
    starts = {5: [(0, 512)], 8: [(512, 256), (768, 256)]}

    def finish(first, count):
        here = pl.ds(first, count)
        change = normalised_bf16(update.pop((first, count))) * ng_v[3:4, :].astype(BF16)
        grid_v[here, :] = grid_v[here, :] + change
        outs.append(
            pltpu.make_async_copy(grid_v.at[here], grid_out.at[here], out_sem.at[len(outs)])
        )
        outs[-1].start()

    def half_sums(step):
        half, k = order[step]
        loads["picks", half, k].wait()
        loads["sums", half, k].wait()
        picked = dot(picks_v[k, rows_of(half), :], halo_v[...]).astype(BF16)
        return silu_of_half(picked + sums_v[k, rows_of(half), :])

    loads["halo"].wait()
    count = len(order)
    for step in range(count + 5):
        if step < count:
            hidden[step] = half_sums(step)
        if step == 1:
            loads["es"].wait()
            loads["eg"].wait()
        if 0 <= step - 1 < count:
            result[step - 1] = dot(hidden.pop(step - 1), second_v[0])
        if 0 <= step - 2 < count:
            before, part = order[step - 2]
            message = normalised_bf16(result.pop(step - 2))
            if part == 0:
                added_v[...] = message
            elif part == 1:
                added_v[...] += message
            else:
                total_v[rows_of(before), :] = (added_v[...] + message) * eg_v[3:4, :].astype(BF16)
        if step == 5:
            for name in ("nf", "ns", "ng", "gp", "grid"):
                loads[name].wait()
        pres = {}
        for block in starts.get(step, ()):
            pres[block] = (0.5 * dot(total_v[pl.ds(*block), :], sum_v[...])).astype(BF16)
        for block in list(update):
            finish(*block)
        for block in list(node):
            update[block] = dot(node.pop(block), second_v[1])
        for block, pre in pres.items():
            node[block] = silu_of_half(pre + gp_v[pl.ds(*block), :])
        if step == 6:
            loads["mesh"].wait()
            slot = lax.broadcasted_iota(jnp.int32, (M_DEV, D), 0)
            mesh_v[...] = jnp.where(slot < owned[0], mesh_v[...].astype(F32), 0.0).astype(BF16)
            outs.append(pltpu.make_async_copy(mesh_v, mesh_out, out_sem.at[len(outs)]))
            outs[-1].start()
    for copy in outs:
        copy.wait()


def decode_part(*operands):
    vmem = pltpu.VMEM
    anywhere = pl.BlockSpec(memory_space=pl.ANY)
    return pl.pallas_call(
        decode_kernel,
        name="decode_part",
        in_specs=[pl.BlockSpec(memory_space=pltpu.SMEM)] + [anywhere] * 10,
        out_specs=[anywhere] * 2,
        out_shape=[
            jax.ShapeDtypeStruct((G_DEV, D), BF16),
            jax.ShapeDtypeStruct((M_DEV, D), BF16),
        ],
        scratch_shapes=[
            vmem((3, G_DEV, 128), BF16),
            vmem((8 * HB, D), BF16),
            vmem((3, G_DEV, D), BF16),
            vmem((DEC_TILE, D), BF16),
            vmem((G_DEV, D), BF16),
            vmem((G_DEV, D), BF16),
            vmem((G_DEV, D), BF16),
            vmem((M_DEV, D), BF16),
            vmem((2, D, D), BF16),
            vmem((D, D), BF16),
            vmem((4, D), F32),
            vmem((4, D), F32),
            pltpu.SemaphoreType.DMA((21,)),
            pltpu.SemaphoreType.DMA((4,)),
        ],
        compiler_params=pltpu.CompilerParams(vmem_limit_bytes=60 * 1024 * 1024),
    )(*operands)


def per_device(
    grid_nodes,
    mesh_nodes,
    owned_nodes,
    grid_rim,
    mesh_rim,
    long_send,
    g2m_edges,
    short_edges,
    long_edges,
    m2g_edges,
    edge_first,
    edge_second,
    edge_bias,
    edge_gain,
    node_first,
    node_second,
    node_bias,
    node_gain,
):
    halo, mesh_three, sums, gp, picks, seconds = mesh_part(
        grid_nodes,
        mesh_nodes,
        grid_rim,
        mesh_rim,
        jnp.transpose(long_send, (0, 2, 1)),
        g2m_edges,
        short_edges,
        long_edges,
        jnp.transpose(m2g_edges, (1, 0, 2)),
        edge_first,
        edge_second,
        edge_bias,
        edge_gain,
        node_first,
        node_second,
        node_bias,
        node_gain,
    )
    grid_out, mesh_out = decode_part(
        owned_nodes,
        picks,
        halo,
        sums,
        gp,
        grid_nodes,
        mesh_three,
        seconds,
        node_first,
        edge_gain,
        node_gain,
    )
    return (grid_out, mesh_out)


def solution(mesh):
    rows = P(("aa", "ba"), None)
    lists = P(("aa", "ba"), None, None)
    in_specs = (rows, rows, P(("aa", "ba"))) + (lists,) * 7 + (P(),) * 8
    return jax.shard_map(
        per_device, mesh=mesh, in_specs=in_specs, out_specs=(rows, rows), check_vma=False
    )
```

```python
import jax
import jax.numpy as jnp
from jax import lax
from jax.experimental import pallas as pl
from jax.experimental.pallas import tpu as pltpu
from jax.sharding import PartitionSpec as P

EPSILON = 1e-05
D = 512
G_DEV = 1024
M_DEV = 192
GB = 128
HB = 16
KL = 8
CS = 16
NOWHERE = 4095
EARLY = 6
N_AA = 8
N_BA = 16
DEVICES = 128
E_G2M = 3072
E_MESH = 1536
TILE_LOCAL = 512
TILE_ENC = 768
TILE_MESH = 768
ALONG_FIRST = (-1, -1, -1, 0, 0, 1, 1, 1)
ALONG_SECOND = (-1, 0, 1, -1, 1, -1, 0, 1)
F32 = jnp.float32
BF16 = jnp.bfloat16
MESH = pl.DeviceIdType.MESH


def hops(first, second):
    steps = ((first + 1) // 2, second // 4, second % 4)
    return sum(min(step, 4 - step) for step in steps)


GROUP_ORDER = (2, 1, 3, 0)
PEERS = sorted(
    [(a, b) for a in range(N_AA) for b in range(N_BA) if (a, b) != (0, 0)],
    key=lambda peer: (GROUP_ORDER.index(peer[1] // 4), -hops(*peer)),
)


def dot(a, b):
    return jnp.dot(a, b, preferred_element_type=F32)


def silu_of_half(half):
    return half * jnp.tanh(half) + half


def centred_weights(weights):
    wide = weights.astype(F32)
    return (wide - jnp.mean(wide, axis=-1, keepdims=True)).astype(BF16)


def normalised(centred):
    spread = jnp.mean(centred * centred, axis=-1, keepdims=True)
    return centred * lax.rsqrt(spread + EPSILON)


def normalised_bf16(centred):
    spread = jnp.mean(centred * centred, axis=-1, keepdims=True)
    return centred.astype(BF16) * lax.rsqrt(spread + EPSILON).astype(BF16)


def spread_out(row):
    parts = []
    for start in range(0, row.shape[1], 128):
        parts.append(jnp.broadcast_to(row[:, start : start + 128], (128, 128)).T.astype(BF16))
    return parts[0] if len(parts) == 1 else jnp.concatenate(parts, 0)


def columns(row):
    return spread_out((row >> 8).astype(F32)), spread_out((row & 255).astype(F32))


def lane_ids(rows):
    lane = lax.broadcasted_iota(jnp.int32, (rows, 128), 1).astype(F32)
    return lane.astype(BF16), (lane + 128.0).astype(BF16)


def one_hot(cols, first, width):
    block, place = cols
    lanes = lane_ids(place.shape[0])
    one, zero = jnp.ones((), BF16), jnp.zeros((), BF16)
    parts = []
    for start in range(first, first + width, 256):
        here = place
        if block is not None:
            here = jnp.where(block == jnp.asarray(start // 256, BF16), place, jnp.asarray(-1, BF16))
        for half in range(2):
            if start + 128 * half < first + width:
                parts.append(jnp.where(here == lanes[half], one, zero))
    return parts[0] if len(parts) == 1 else jnp.concatenate(parts, 1)


def double_one_hot(first, second, width):
    lanes = lane_ids(first[1].shape[0])
    one, zero, none = jnp.ones((), BF16), jnp.zeros((), BF16), jnp.asarray(-1, BF16)
    parts = []
    for start in range(0, width, 256):
        group = jnp.asarray(start // 256, BF16)
        one_here = jnp.where(first[0] == group, first[1], none)
        two_here = jnp.where(second[0] == group, second[1], none)
        for half in range(2):
            if start + 128 * half < width:
                found = (one_here == lanes[half]) | (two_here == lanes[half])
                parts.append(jnp.where(found, one, zero))
    return jnp.concatenate(parts, 1)


def receivers(row):
    slots = lax.broadcasted_iota(jnp.int32, (M_DEV, row.shape[1]), 0).astype(F32).astype(BF16)
    return slots == row.astype(F32).astype(BF16)


def node_update(rows, totals, first_own, first_sum, bias, second, gain):
    pre = dot(rows, first_own) + dot(totals.astype(BF16), first_sum) + bias
    result = dot(silu_of_half((0.5 * pre).astype(BF16)), second)
    result = normalised(result) * gain
    return (rows.astype(F32) + result).astype(BF16)


def mesh_kernel(
    grid_nodes,
    mesh_nodes,
    grid_rim,
    mesh_rim,
    long_send,
    g2m_edges,
    short_edges,
    long_edges,
    m2g_edges,
    edge_first,
    edge_second,
    edge_bias,
    edge_gain,
    node_first,
    node_second,
    node_bias,
    node_gain,
    dec_out,
    mesh_out,
    gq_out,
    gp_out,
    picks_out,
    second_out,
    grid_v,
    mesh_v,
    grim_v,
    mrim_v,
    send_v,
    g2m_v,
    short_v,
    long_v,
    m2g_v,
    ef_v,
    es_v,
    eb_v,
    eg_v,
    nf_v,
    ns_v,
    nb_v,
    ng_v,
    enc_table,
    enc_halo,
    enc_rim,
    partial,
    picks_v,
    proj_v,
    coarse_v,
    rim_picks,
    list_picks,
    short_table,
    short_rim,
    long_table,
    long_out,
    long_in,
    long_rows,
    dec_halo,
    dec_rim,
    dec_picks,
    dec_near,
    dec_sums,
    totals,
    gq_v,
    gp_v,
    in_sem,
    out_sem,
    halo_send,
    halo_recv,
    long_ssem,
    long_rsem,
    spread_sem,
):
    band = lax.axis_index("aa")
    sector = lax.axis_index("ba")
    me = band * N_BA + sector

    loads = {}

    def load(name, src, dst):
        copy = pltpu.make_async_copy(src, dst, in_sem.at[len(loads)])
        copy.start()
        loads[name] = copy

    def arrived(*names):
        for name in names:
            loads[name].wait()

    def at(first, second):
        return (
            lax.rem(band + (first + N_AA), N_AA),
            lax.rem(sector + (second + N_BA), N_BA),
        )

    def greet(semaphore, stride_first, stride_second, around):
        for k in around:
            pl.semaphore_signal(
                semaphore,
                inc=1,
                device_id=at(stride_first * ALONG_FIRST[k], stride_second * ALONG_SECOND[k]),
                device_id_type=MESH,
            )

    barrier = pltpu.get_barrier_semaphore()
    greet(barrier, 1, 1, range(8))

    load("grim", grid_rim, grim_v)
    load("grid", grid_nodes, grid_v)
    load("ef00", edge_first.at[0, 0], ef_v.at[0, 0])
    load("mesh", mesh_nodes, mesh_v)
    load("ef01", edge_first.at[0, 1], ef_v.at[0, 1])
    load("eb", edge_bias, eb_v)
    load("g2m", g2m_edges, g2m_v)
    def halo_copy(k, sem_base, rim, table, first, depth):
        return pltpu.make_async_remote_copy(
            src_ref=rim.at[pl.ds(k * depth, depth)],
            dst_ref=table.at[pl.ds(first + (7 - k) * depth, depth)],
            send_sem=halo_send.at[sem_base + k],
            recv_sem=halo_recv.at[sem_base + 7 - k],
            device_id=at(ALONG_FIRST[k], ALONG_SECOND[k]),
            device_id_type=MESH,
        )

    copies = []
    arrived("grim", "grid")
    for pair in ((5, 4), (7, 3, 2), (6, 1, 0)):
        cols = columns(jnp.concatenate([grim_v[0, k : k + 1, :] for k in pair], 1))
        rows = dot(one_hot(cols, 0, G_DEV), grid_v[...]).astype(BF16)
        if not copies:
            arrived("ef00")
        rows = (0.5 * dot(rows, ef_v[0, 0])).astype(BF16)
        for place, k in enumerate(pair):
            enc_rim[k * GB : (k + 1) * GB, :] = rows[place * GB : (place + 1) * GB, :]
        if not copies:
            pl.semaphore_wait(barrier, 8)
        for k in pair:
            copy = halo_copy(k, 0, enc_rim, enc_halo, 0, GB)
            copy.start()
            copies.append((k, copy))
    greet(spread_sem.at[0], 1, 1, range(8))
    load("es0", edge_second.at[0], es_v.at[0])
    load("ns0", node_second.at[0], ns_v.at[0])
    load("nf0", node_first.at[0], nf_v.at[0])
    load("eg", edge_gain, eg_v)
    load("ng", node_gain, ng_v)
    load("nb", node_bias, nb_v)
    load("mrim", mesh_rim, mrim_v)
    load("ef1", edge_first.at[1], ef_v.at[1])
    load("short", short_edges, short_v)
    load("es1", edge_second.at[1], es_v.at[1])
    load("nf1", node_first.at[1], nf_v.at[1])
    load("ns1", node_second.at[1], ns_v.at[1])
    load("send", long_send, send_v)
    load("ef2", edge_first.at[2], ef_v.at[2])
    load("long", long_edges, long_v)
    load("es2", edge_second.at[2], es_v.at[2])
    load("nf2", node_first.at[2], nf_v.at[2])
    load("ns2", node_second.at[2], ns_v.at[2])
    load("ef3", edge_first.at[3], ef_v.at[3])
    load("nf30", node_first.at[3, 0], nf_v.at[3, 0])
    load("es3", edge_second.at[3], es_v.at[3])
    load("ns3", node_second.at[3], ns_v.at[3])
    load("m2g", m2g_edges, m2g_v)

    for start in range(0, G_DEV, 512):
        half = 0.5 * dot(grid_v[start : start + 512, :], ef_v[0, 0])
        enc_table[start : start + 512, :] = half.astype(BF16)
    arrived("mesh", "ef01", "eb")
    enc_table[G_DEV : G_DEV + M_DEV, :] = (0.5 * (dot(mesh_v[...], ef_v[0, 1]) + eb_v[0:1, :])).astype(BF16)
    enc_table[G_DEV + M_DEV : G_DEV + 256, :] = jnp.zeros((64, D), BF16)
    proj_v[M_DEV:256, :] = jnp.zeros((64, D), BF16)
    coarse_v[...] = jnp.zeros((128, D), BF16)
    arrived("g2m")

    def tile_of(index):
        return pl.ds(index * TILE_LOCAL, TILE_LOCAL)

    def near_picks(index):
        here = tile_of(index)
        block, place = columns(g2m_v[0, 0:1, here])
        picks_v[here, :] = one_hot((block, place), G_DEV, 8 * GB)
        targets = columns(g2m_v[0, 1:2, here])
        return jnp.concatenate([one_hot((block, place), 0, G_DEV), one_hot(targets, 0, 256)], 1)

    tiles = E_G2M // TILE_LOCAL
    picks = near_picks(0)
    for index in range(tiles):
        sums = dot(picks, enc_table[...])
        if index + 1 < tiles:
            picks = near_picks(index + 1)
        partial[tile_of(index), :] = sums.astype(BF16)

    def centre(section):
        def block(step, carry):
            here = pl.ds(pl.multiple_of(step * 128, 128), 128)
            es_v[section, here, :] = centred_weights(es_v[section, here, :])
            ns_v[section, here, :] = centred_weights(ns_v[section, here, :])
            return carry

        lax.fori_loop(0, D // 128, block, 0)

    arrived("es0", "ns0")
    centre(0)
    arrived("mrim")
    sub = lax.broadcasted_iota(jnp.int32, (HB, HB), 0)
    lane = lax.broadcasted_iota(jnp.int32, (HB, HB), 1)
    parts = []
    for k in range(8):
        row = jnp.broadcast_to(mrim_v[0, k : k + 1, :].astype(F32), (HB, HB))
        col = jnp.sum(jnp.where(sub == lane, row, 0.0), axis=1, keepdims=True)
        parts.append(jnp.broadcast_to(col, (HB, 128)))
    rim_picks[...] = one_hot((None, jnp.concatenate(parts, 0).astype(BF16)), 0, 128)
    def rounds(section, tile, edges, count, picked):
        totals[...] = jnp.zeros((M_DEV, D), F32)
        tiles = count // tile
        hidden, result = {}, {}
        for step in range(tiles + 2):
            if step < tiles:
                half = picked(step * tile)
            if 0 <= step - 2:
                values = result.pop(step - 2)
                targets = edges[0, 1:2, (step - 2) * tile : (step - 1) * tile]
                scatter = jnp.where(receivers(targets), jnp.ones((), BF16), jnp.zeros((), BF16))
                if section == 0:
                    message = normalised(values).astype(BF16)
                else:
                    message = normalised_bf16(values)
            if 0 <= step - 1 < tiles:
                result[step - 1] = dot(hidden.pop(step - 1), es_v[section])
            if step < tiles:
                hidden[step] = silu_of_half(half)
            if 0 <= step - 2:
                totals[...] += dot(scatter, message)

    def updated(section, rows, sums):
        return node_update(
            rows,
            sums * eg_v[section : section + 1, :],
            nf_v[section, 0],
            nf_v[section, 1],
            nb_v[section : section + 1, :],
            ns_v[section],
            ng_v[section : section + 1, :],
        )

    arrived("nf0", "eg", "ng", "nb")
    pl.semaphore_wait(spread_sem.at[0], 8)
    greet(spread_sem.at[1], 2, 2, range(8))

    for k, copy in copies:
        if 7 - k < EARLY:
            copy.wait_recv()

    for index in range(tiles):
        here = tile_of(index)
        partial[here, :] += dot(picks_v[here, 0 : EARLY * GB], enc_halo[0 : EARLY * GB, :]).astype(BF16)
    for k, copy in copies:
        copy.wait_send()
        if 7 - k >= EARLY:
            copy.wait_recv()

    def enc_picked(start):
        here = pl.ds(start, TILE_ENC)
        late = dot(picks_v[here, EARLY * GB :], enc_halo[EARLY * GB :, :])
        return partial[here, :] + late.astype(BF16)

    rounds(0, TILE_ENC, g2m_v, E_G2M, enc_picked)
    mesh_v[...] = updated(0, mesh_v[...], totals[...])

    def mesh_halo(section, sem_base, rim, table, first):
        proj = (0.5 * dot(mesh_v[...], ef_v[section, 0])).astype(BF16)
        proj_v[0:M_DEV, :] = proj
        rim[...] = dot(rim_picks[...], proj_v[0:128, :]).astype(BF16)
        started = []
        for k in range(8):
            copy = halo_copy(k, sem_base, rim, table, first, HB)
            copy.start()
            started.append(copy)
        if first:
            table[0:M_DEV, :] = proj
        return started

    arrived("ef1")
    copies = mesh_halo(1, 8, short_rim, short_table, 2 * M_DEV)
    short_table[M_DEV : 2 * M_DEV, :] = (0.5 * (dot(mesh_v[...], ef_v[1, 1]) + eb_v[1:2, :])).astype(
        BF16
    )
    arrived("short")

    def short_picks(step, carry):
        here = pl.ds(pl.multiple_of(step * TILE_LOCAL, TILE_LOCAL), TILE_LOCAL)
        senders = short_v[0, 0:1, here]
        senders = columns(jnp.where(senders < M_DEV, senders, senders + M_DEV))
        targets = columns(short_v[0, 1:2, here] + M_DEV)
        picks_v[here, 0:512] = double_one_hot(senders, targets, 512)
        return carry

    lax.fori_loop(0, E_MESH // TILE_LOCAL, short_picks, 0)
    arrived("es1", "ns1", "nf1", "send")
    centre(1)
    lists = send_v[0].astype(F32).astype(BF16)
    for start in range(0, DEVICES * KL, 512):
        sub = lax.broadcasted_iota(jnp.int32, (512, DEVICES), 0) + start
        lane = lax.broadcasted_iota(jnp.int32, (512, DEVICES), 1)
        owner = jnp.where(sub // KL == lane, 1.0, 0.0).astype(BF16)
        listed = lax.dot_general(owner, lists, (((1,), (1,)), ((), ())), preferred_element_type=F32)
        sub = lax.broadcasted_iota(jnp.int32, (512, KL), 0)
        lane = lax.broadcasted_iota(jnp.int32, (512, KL), 1)
        col = jnp.sum(jnp.where(lax.rem(sub, KL) == lane, listed, 0.0), axis=1, keepdims=True)
        list_picks[start : start + 512, :] = one_hot(
            (None, jnp.broadcast_to(col, (512, 128)).astype(BF16)), 0, 128
        )
    for index in range(E_MESH // TILE_LOCAL):
        here = tile_of(index)
        partial[here, :] = dot(picks_v[here, 0:256], short_table[0:256, :]).astype(BF16)
    pl.semaphore_wait(spread_sem.at[1], 8)
    greet(spread_sem.at[2], 0, 4, (3, 4))
    for copy in copies:
        copy.wait()

    def short_picked(start):
        here = pl.ds(start, TILE_MESH)
        late = dot(picks_v[here, 256:512], short_table[256:512, :])
        return partial[here, :] + late.astype(BF16)

    rounds(1, TILE_MESH, short_v, E_MESH, short_picked)

    arrived("ef2")
    coarse = updated(1, mesh_v[0:CS, :], totals[0:CS, :])
    coarse_v[0:CS, :] = (0.5 * dot(coarse, ef_v[2, 0])).astype(BF16)
    for start in range(0, DEVICES * KL, 512):
        rows = dot(list_picks[start : start + 512, :], coarse_v[...])
        long_out[start // KL : (start + 512) // KL] = rows.reshape(512 // KL, KL, D).astype(BF16)
    pl.semaphore_wait(spread_sem.at[2], 2)
    for first, second in PEERS:
        peer_first = lax.rem(band + first, N_AA)
        peer_second = (sector // 4 + second // 4) % 4 * 4 + (sector + second) % 4
        group = -(second // 4) % 4
        slot = group * 32 + -first % N_AA * 4 + -second % 4
        pltpu.make_async_remote_copy(
            src_ref=long_out.at[peer_first * N_BA + peer_second],
            dst_ref=long_in.at[slot],
            send_sem=long_ssem,
            recv_sem=long_rsem.at[group],
            device_id=(peer_first, peer_second),
            device_id_type=MESH,
        ).start()
    long_in[0] = long_out[me]

    mesh_v[...] = updated(1, mesh_v[...], totals[...])
    long_table[0:M_DEV, :] = (0.5 * dot(mesh_v[...], ef_v[2, 0])).astype(BF16)
    long_table[M_DEV : 2 * M_DEV, :] = (0.5 * (dot(mesh_v[...], ef_v[2, 1]) + eb_v[2:3, :])).astype(BF16)
    arrived("long")

    def long_local(step, carry):
        here = pl.ds(pl.multiple_of(step * TILE_LOCAL, TILE_LOCAL), TILE_LOCAL)
        senders = long_v[0, 0:1, here]
        own = columns(jnp.where(senders < M_DEV, senders, NOWHERE))
        targets = columns(long_v[0, 1:2, here] + M_DEV)
        sums = dot(double_one_hot(own, targets, 2 * M_DEV), long_table[...])
        partial[here, :] = sums.astype(BF16)
        far = jnp.maximum(senders - M_DEV, 0)
        peer = far >> 3
        slot = (((peer >> 2) - (sector >> 2)) & 3) * 32
        slot = slot + (((peer >> 4) - band) & 7) * 4 + ((peer - sector) & 3)
        away = columns(jnp.where(senders < M_DEV, NOWHERE, slot * KL + (far & 7)))
        picks_v[here, :] = one_hot(away, 0, DEVICES * KL)
        return carry

    lax.fori_loop(0, E_MESH // TILE_LOCAL, long_local, 0)
    arrived("ef3", "nf30", "es2", "ns2", "es3", "ns3", "m2g")
    centre(2)
    for start in range(0, G_DEV, 512):
        rows = grid_v[start : start + 512, :]
        gq_v[start : start + 512, :] = (0.5 * (dot(rows, ef_v[3, 1]) + eb_v[3:4, :])).astype(BF16)
        gp_v[start : start + 512, :] = (0.5 * (dot(rows, nf_v[3, 0]) + nb_v[3:4, :])).astype(BF16)
    centre(3)
    gp_copy = pltpu.make_async_copy(gp_v, gp_out, out_sem.at[1])
    es_copy = pltpu.make_async_copy(es_v.at[3], second_out.at[0], out_sem.at[2])
    ns_copy = pltpu.make_async_copy(ns_v.at[3], second_out.at[1], out_sem.at[3])
    outs = [gp_copy, es_copy, ns_copy]

    def dec_ids(step, carry):
        here = pl.ds(pl.multiple_of(step * 512, 512), 512)
        for k in range(3):
            senders = m2g_v[k, :, here]
            dec_near[k, here, :] = one_hot(columns(senders), 0, 256)
            rims = jnp.where(senders < M_DEV, NOWHERE, senders - M_DEV)
            dec_picks[k, here, :] = one_hot(columns(rims), 0, 128)
        return carry

    lax.fori_loop(0, G_DEV // 512, dec_ids, 0)
    outs.append(pltpu.make_async_copy(dec_picks, picks_out, out_sem.at[4]))
    for copy in outs:
        copy.start()
    arrived("nf2")
    def long_arrived(group):
        first = 1 if group == 0 else group * 32
        blocks = long_in.at[pl.ds(first, (group + 1) * 32 - first)]
        pltpu.make_async_copy(blocks, blocks, long_rsem.at[group]).wait()
        rows = long_in[group * 32 : (group + 1) * 32].astype(F32).reshape(32 * KL, D)
        long_rows[group * 256 : (group + 1) * 256, :] = rows.astype(BF16)

    for group in (2, 3, 1):
        long_arrived(group)
        some = pl.ds(group * 256, 256)
        for index in range(E_MESH // TILE_LOCAL):
            here = tile_of(index)
            partial[here, :] += dot(picks_v[here, some], long_rows[some, :]).astype(BF16)
    others = pl.ds(0, DEVICES - 1)
    pltpu.make_async_copy(long_out.at[others], long_out.at[others], long_ssem).wait()
    long_arrived(0)

    def long_picked(start):
        here = pl.ds(start, TILE_MESH)
        return partial[here, :] + dot(picks_v[here, 0:256], long_rows[0:256, :]).astype(BF16)

    rounds(2, TILE_MESH, long_v, E_MESH, long_picked)
    mesh_v[...] = updated(2, mesh_v[...], totals[...])

    copies = mesh_halo(3, 16, dec_rim, dec_halo, 0)
    outs.append(pltpu.make_async_copy(mesh_v, mesh_out, out_sem.at[5]))
    outs[-1].start()
    for half in range(2):
        for k in range(3):
            here = pl.ds(half * 512, 512)
            sums = dot(dec_near[k, here, :], proj_v[...]).astype(BF16)
            dec_sums[k, here, :] = sums + gq_v[here, :]
            outs.append(
                pltpu.make_async_copy(
                    dec_sums.at[k, here], gq_out.at[k, here], out_sem.at[7 + 3 * half + k]
                )
            )
            outs[-1].start()
    for copy in copies:
        copy.wait()
    outs.append(pltpu.make_async_copy(dec_halo, dec_out, out_sem.at[6]))
    outs[-1].start()
    for copy in outs:
        copy.wait()


def mesh_part(*operands):
    vmem = pltpu.VMEM
    anywhere = pl.BlockSpec(memory_space=pl.ANY)
    return pl.pallas_call(
        mesh_kernel,
        name="mesh_part",
        in_specs=[anywhere] * 17,
        out_specs=[anywhere] * 6,
        out_shape=[
            jax.ShapeDtypeStruct((8 * HB, D), BF16),
            jax.ShapeDtypeStruct((M_DEV, D), BF16),
            jax.ShapeDtypeStruct((3, G_DEV, D), BF16),
            jax.ShapeDtypeStruct((G_DEV, D), BF16),
            jax.ShapeDtypeStruct((3, G_DEV, 128), BF16),
            jax.ShapeDtypeStruct((2, D, D), BF16),
        ],
        scratch_shapes=[
            vmem((G_DEV, D), BF16),
            vmem((M_DEV, D), BF16),
            vmem((1, 8, GB), jnp.int32),
            vmem((1, 8, HB), jnp.int32),
            vmem((1, KL, DEVICES), jnp.int32),
            vmem((1, 2, E_G2M), jnp.int32),
            vmem((1, 2, E_MESH), jnp.int32),
            vmem((1, 2, E_MESH), jnp.int32),
            vmem((3, 1, G_DEV), jnp.int32),
            vmem((4, 2, D, D), BF16),
            vmem((4, D, D), BF16),
            vmem((4, D), F32),
            vmem((4, D), F32),
            vmem((4, 2, D, D), BF16),
            vmem((4, D, D), BF16),
            vmem((4, D), F32),
            vmem((4, D), F32),
            vmem((G_DEV + 256, D), BF16),
            vmem((8 * GB, D), BF16),
            vmem((8 * GB, D), BF16),
            vmem((E_G2M, D), BF16),
            vmem((E_G2M, 8 * GB), BF16),
            vmem((256, D), BF16),
            vmem((128, D), BF16),
            vmem((128, 128), BF16),
            vmem((DEVICES * KL, 128), BF16),
            vmem((512, D), BF16),
            vmem((8 * HB, D), BF16),
            vmem((2 * M_DEV, D), BF16),
            vmem((DEVICES, KL, D), BF16),
            vmem((DEVICES, KL, D), BF16),
            vmem((DEVICES * KL, D), BF16),
            vmem((8 * HB, D), BF16),
            vmem((8 * HB, D), BF16),
            vmem((3, G_DEV, 128), BF16),
            vmem((3, G_DEV, 256), BF16),
            vmem((3, G_DEV, D), BF16),
            vmem((M_DEV, D), F32),
            vmem((G_DEV, D), BF16),
            vmem((G_DEV, D), BF16),
            pltpu.SemaphoreType.DMA((30,)),
            pltpu.SemaphoreType.DMA((13,)),
            pltpu.SemaphoreType.DMA((24,)),
            pltpu.SemaphoreType.DMA((24,)),
            pltpu.SemaphoreType.DMA,
            pltpu.SemaphoreType.DMA((4,)),
            pltpu.SemaphoreType.REGULAR((3,)),
        ],
        compiler_params=pltpu.CompilerParams(
            collective_id=0, has_side_effects=True, vmem_limit_bytes=60 * 1024 * 1024
        ),
    )(*operands)


DEC_TILE = 512


def decode_kernel(
    owned,
    picks,
    halo,
    sums,
    gp,
    grid_rows,
    mesh_rows,
    seconds,
    node_sum,
    edge_gain,
    node_gain,
    grid_out,
    mesh_out,
    picks_v,
    halo_v,
    sums_v,
    added_v,
    total_v,
    gp_v,
    grid_v,
    mesh_v,
    second_v,
    sum_v,
    eg_v,
    ng_v,
    in_sem,
    out_sem,
):
    loads = {}

    def load(name, src, dst):
        copy = pltpu.make_async_copy(src, dst, in_sem.at[len(loads)])
        copy.start()
        loads[name] = copy

    order = [(half, k) for half in range(2) for k in range(3)]

    def rows_of(half):
        return pl.ds(half * DEC_TILE, DEC_TILE)

    load("halo", halo, halo_v)
    for half, k in order:
        here = rows_of(half)
        load(("picks", half, k), picks.at[k, here], picks_v.at[k, here])
        load(("sums", half, k), sums.at[k, here], sums_v.at[k, here])
        if half == 0 and k == 0:
            load("es", seconds.at[0], second_v.at[0])
            load("eg", edge_gain, eg_v)
    load("nf", node_sum.at[3, 1], sum_v)
    load("ns", seconds.at[1], second_v.at[1])
    load("ng", node_gain, ng_v)
    load("gp", gp, gp_v)
    load("grid", grid_rows, grid_v)
    load("mesh", mesh_rows, mesh_v)
    outs = []
    hidden, result, node, update = {}, {}, {}, {}
    starts = {5: [(0, 512)], 8: [(512, 256), (768, 256)]}

    def finish(first, count):
        here = pl.ds(first, count)
        change = normalised_bf16(update.pop((first, count))) * ng_v[3:4, :].astype(BF16)
        grid_v[here, :] = grid_v[here, :] + change
        outs.append(
            pltpu.make_async_copy(grid_v.at[here], grid_out.at[here], out_sem.at[len(outs)])
        )
        outs[-1].start()

    def half_sums(step):
        half, k = order[step]
        loads["picks", half, k].wait()
        loads["sums", half, k].wait()
        picked = dot(picks_v[k, rows_of(half), :], halo_v[...]).astype(BF16)
        return silu_of_half(picked + sums_v[k, rows_of(half), :])

    loads["halo"].wait()
    count = len(order)
    for step in range(count + 5):
        if step < count:
            hidden[step] = half_sums(step)
        if step == 1:
            loads["es"].wait()
            loads["eg"].wait()
        if 0 <= step - 1 < count:
            result[step - 1] = dot(hidden.pop(step - 1), second_v[0])
        if 0 <= step - 2 < count:
            before, part = order[step - 2]
            message = normalised_bf16(result.pop(step - 2))
            if part == 0:
                added_v[...] = message
            elif part == 1:
                added_v[...] += message
            else:
                total_v[rows_of(before), :] = (added_v[...] + message) * eg_v[3:4, :].astype(BF16)
        if step == 5:
            for name in ("nf", "ns", "ng", "gp", "grid"):
                loads[name].wait()
        pres = {}
        for block in starts.get(step, ()):
            pres[block] = (0.5 * dot(total_v[pl.ds(*block), :], sum_v[...])).astype(BF16)
        for block in list(update):
            finish(*block)
        for block in list(node):
            update[block] = dot(node.pop(block), second_v[1])
        for block, pre in pres.items():
            node[block] = silu_of_half(pre + gp_v[pl.ds(*block), :])
        if step == 6:
            loads["mesh"].wait()
            slot = lax.broadcasted_iota(jnp.int32, (M_DEV, D), 0)
            mesh_v[...] = jnp.where(slot < owned[0], mesh_v[...].astype(F32), 0.0).astype(BF16)
            outs.append(pltpu.make_async_copy(mesh_v, mesh_out, out_sem.at[len(outs)]))
            outs[-1].start()
    for copy in outs:
        copy.wait()


def decode_part(*operands):
    vmem = pltpu.VMEM
    anywhere = pl.BlockSpec(memory_space=pl.ANY)
    return pl.pallas_call(
        decode_kernel,
        name="decode_part",
        in_specs=[pl.BlockSpec(memory_space=pltpu.SMEM)] + [anywhere] * 10,
        out_specs=[anywhere] * 2,
        out_shape=[
            jax.ShapeDtypeStruct((G_DEV, D), BF16),
            jax.ShapeDtypeStruct((M_DEV, D), BF16),
        ],
        scratch_shapes=[
            vmem((3, G_DEV, 128), BF16),
            vmem((8 * HB, D), BF16),
            vmem((3, G_DEV, D), BF16),
            vmem((DEC_TILE, D), BF16),
            vmem((G_DEV, D), BF16),
            vmem((G_DEV, D), BF16),
            vmem((G_DEV, D), BF16),
            vmem((M_DEV, D), BF16),
            vmem((2, D, D), BF16),
            vmem((D, D), BF16),
            vmem((4, D), F32),
            vmem((4, D), F32),
            pltpu.SemaphoreType.DMA((21,)),
            pltpu.SemaphoreType.DMA((4,)),
        ],
        compiler_params=pltpu.CompilerParams(vmem_limit_bytes=60 * 1024 * 1024),
    )(*operands)


def per_device(
    grid_nodes,
    mesh_nodes,
    owned_nodes,
    grid_rim,
    mesh_rim,
    long_send,
    g2m_edges,
    short_edges,
    long_edges,
    m2g_edges,
    edge_first,
    edge_second,
    edge_bias,
    edge_gain,
    node_first,
    node_second,
    node_bias,
    node_gain,
):
    halo, mesh_three, sums, gp, picks, seconds = mesh_part(
        grid_nodes,
        mesh_nodes,
        grid_rim,
        mesh_rim,
        jnp.transpose(long_send, (0, 2, 1)),
        g2m_edges,
        short_edges,
        long_edges,
        jnp.transpose(m2g_edges, (1, 0, 2)),
        edge_first,
        edge_second,
        edge_bias,
        edge_gain,
        node_first,
        node_second,
        node_bias,
        node_gain,
    )
    grid_out, mesh_out = decode_part(
        owned_nodes,
        picks,
        halo,
        sums,
        gp,
        grid_nodes,
        mesh_three,
        seconds,
        node_first,
        edge_gain,
        node_gain,
    )
    return (grid_out, mesh_out)


def solution(mesh):
    rows = P(("aa", "ba"), None)
    lists = P(("aa", "ba"), None, None)
    in_specs = (rows, rows, P(("aa", "ba"))) + (lists,) * 7 + (P(),) * 8
    return jax.shard_map(
        per_device, mesh=mesh, in_specs=in_specs, out_specs=(rows, rows), check_vma=False
    )
```
